32 devices in a mesh: ctx: 16 (over z, y, x), wsh: 2 (over core).
Axes of the slice: x: 2, y: 2, z: 4, core: 2. Of those that a mesh axis runs over, the one named last changes fastest.
Arguments:
- tokens: bfloat16 [4, 4096, 768], P('wsh', 'ctx'), may hold values from -6 to 6
- cont_lengths: int32 [4, 8], P('wsh'), may hold values from 1 to 512, 2048 in all within a row
- grad_out: bfloat16 [4, 4096, 768], P('wsh', 'ctx'), may hold values from -6 to 6
- ln_gain_one: bfloat16 [768], P('wsh'), may hold values from 0.099609375 to 1.8984375
- ln_bias_one: bfloat16 [768], P('wsh'), may hold values from -1.25 to 1.25
- w_query: bfloat16 [768, 768], P('wsh'), may hold values from -0.21875 to 0.21875
- b_query: bfloat16 [768], P('wsh'), may hold values from -3 to 3
- w_key: bfloat16 [768, 768], P('wsh'), may hold values from -0.21875 to 0.21875
- w_value: bfloat16 [768, 768], P('wsh'), may hold values from -0.21875 to 0.21875
- b_value: bfloat16 [768], P('wsh'), may hold values from -0.625 to 0.625
- w_out: bfloat16 [768, 768], P('wsh'), may hold values from -1.25 to 1.25
- b_out: bfloat16 [768], P('wsh'), may hold values from -0.625 to 0.625
- ln_gain_two: bfloat16 [768], P('wsh'), may hold values from 0.099609375 to 1.8984375
- ln_bias_two: bfloat16 [768], P('wsh'), may hold values from -1.25 to 1.25
- w_in: bfloat16 [768, 3072], P('wsh'), may hold values from -0.21875 to 0.21875
- b_in: bfloat16 [3072], P('wsh'), may hold values from -3 to 3
- w_back: bfloat16 [3072, 768], P('wsh'), may hold values from -0.109375 to 0.109375
- b_back: bfloat16 [768], P('wsh'), may hold values from -0.625 to 0.625
Outputs:
- out_tokens: bfloat16 [4, 4096, 768], P('wsh', 'ctx')
- grad_tokens: float32 [4, 4096, 768], P('wsh', 'ctx')
- grad_ln_gain_one: float32 [768], P('wsh')
- grad_ln_bias_one: float32 [768], P('wsh')
- grad_w_query: float32 [768, 768], P('wsh')
- grad_b_query: float32 [768], P('wsh')
- grad_w_key: float32 [768, 768], P('wsh')
- grad_w_value: float32 [768, 768], P('wsh')
- grad_b_value: float32 [768], P('wsh')
- grad_w_out: float32 [768, 768], P('wsh')
- grad_b_out: float32 [768], P('wsh')
- grad_ln_gain_two: float32 [768], P('wsh')
- grad_ln_bias_two: float32 [768], P('wsh')
- grad_w_in: float32 [768, 3072], P('wsh')
- grad_b_in: float32 [3072], P('wsh')
- grad_w_back: float32 [3072, 768], P('wsh')
- grad_b_back: float32 [768], P('wsh')
The draws below stay inside these ranges and needn't reach their ends.
Inputs may be any that keep to these rules, and one draw needn't show every extreme that they name: `cont_lengths`: each row holds 8 continuation lengths that sum to 2048; the largest of each row is 512.
All inputs are finite; a program needn't handle non-finite values.
Results may differ from the reference program's by a relative error of at most 0.02.
Values may be sent and summed in bfloat16 or wider, within the bound.
No kernel may reach another device: no remote copies, remote signals or barrier semaphores. Data moves between devices by JAX's collectives and lax.ppermute only.
A program may use at most 256 MiB of HBM per device.

```python
import math
import jax
import jax.numpy as jnp
import numpy as np
from jax import lax

D = 768
HEADS = 12
HEAD = 64
FF = 3072
PROMPT = 2048
NCONT = 8
CONT = 2048
MOSTLEN = 512
SEQ = 4096
GROUPS = 4
N_CTX = 16


def block_levels(key, dims, pieces, low, top_value):
    def one(axis_at, shards_of):
        steps = jax.random.uniform(jax.random.fold_in(jax.random.fold_in(key, 6), axis_at), (shards_of,), jnp.float32, low / len(pieces), top_value / len(pieces))
        return jnp.repeat(jnp.exp(steps), dims[axis_at] // shards_of).reshape((-1,) + (1,) * (len(dims) - axis_at - 1))

    gain = one(*pieces[0])
    for cut in pieces[1:]:
        gain = gain * one(*cut)
    return gain


def split_up(count, total, bound, skew):
    portions = [(1 << 20) // math.isqrt(standing ** skew) + 1 for standing in range(2, count + 1)]
    rest, given = total - bound - (count - 1), [1] * (count - 1)
    while rest > 0:
        free = [i for i in range(count - 1) if given[i] < bound]
        mass, budget = sum([portions[i] for i in free]), rest
        for i in free:
            more = min(bound - given[i], max(1, budget * portions[i] // mass), rest)
            given[i] = given[i] + more
            rest = rest - more
    return np.array([bound] + given)


def ragged_sizes(rng, count, total, bound, lean):
    if count == 2:
        one = jax.random.randint(rng, (), max(1, total - bound), min(bound, total - 1) + 1)
        return jnp.stack([one, total - one])
    tallies = jnp.asarray(split_up(count, total, bound, lean), jnp.int32)
    pairs = (count - 1) // 2
    donor, taker = tallies[1:1 + 2 * pairs:2], tallies[2:2 + 2 * pairs:2]
    margin = jnp.minimum(donor - 1, bound - taker)
    passed = jax.random.randint(jax.random.fold_in(rng, 1), (pairs,), 0, 1 << 20) % (margin + 1)
    tallies = tallies.at[1:1 + 2 * pairs:2].set(donor - passed).at[2:2 + 2 * pairs:2].set(taker + passed)
    return tallies[jax.random.permutation(jax.random.fold_in(rng, 2), count)]


def bell_draw(stream_key, dims, deviation, bound, shards=(), kind=jnp.bfloat16):
    array = jax.random.normal(stream_key, dims, jnp.float32) * deviation
    if len(shards) > 0:
        array = block_levels(stream_key, dims, shards, -0.22, 0.18) * array
    return jnp.clip(array, min=-bound, max=bound).astype(kind)


def setup_inputs(seed: int = 0) -> dict:
    splits = jax.random.split(jax.random.key(seed), 19)
    tokens = bell_draw(splits[0], (GROUPS, SEQ, D), 1.0, 6.0, ((0, 2), (1, 16)))
    cont_lengths = jax.vmap(lambda own: ragged_sizes(own, NCONT, CONT, MOSTLEN, 2))(jax.random.split(splits[1], GROUPS)).reshape((GROUPS, NCONT)).astype(jnp.int32)
    grad_out = bell_draw(splits[2], (GROUPS, SEQ, D), 1.0, 6.0, ((0, 2), (1, 16)))
    ln_gain_one = jnp.clip(1.0 + 0.18 * jax.random.normal(splits[3], (D,), jnp.float32), 0.099609375, 1.8984375).astype(jnp.bfloat16)
    ln_bias_one = bell_draw(splits[4], (D,), 0.2, 1.25, ((0, 2),))
    w_query = bell_draw(splits[5], (D, D), D ** -0.5, 0.21875, ((0, 2),))
    b_query = bell_draw(splits[6], (D,), 0.5, 3.0, ((0, 2),))
    w_key = bell_draw(splits[7], (D, D), D ** -0.5, 0.21875, ((0, 2),))
    w_value = bell_draw(splits[8], (D, D), D ** -0.5, 0.21875, ((0, 2),))
    b_value = bell_draw(splits[9], (D,), 0.1, 0.625, ((0, 2),))
    w_out = bell_draw(splits[10], (D, D), (D // 32) ** -0.5, 1.25, ((0, 2),))
    b_out = bell_draw(splits[11], (D,), 0.1, 0.625, ((0, 2),))
    ln_gain_two = jnp.clip(1.0 + 0.18 * jax.random.normal(splits[12], (D,), jnp.float32), 0.099609375, 1.8984375).astype(jnp.bfloat16)
    ln_bias_two = bell_draw(splits[13], (D,), 0.2, 1.25, ((0, 2),))
    w_in = bell_draw(splits[14], (D, FF), D ** -0.5, 0.21875, ((0, 2),))
    b_in = bell_draw(splits[15], (FF,), 0.5, 3.0, ((0, 2),))
    w_back = bell_draw(splits[16], (FF, D), FF ** -0.5, 0.109375, ((0, 2),))
    b_back = bell_draw(splits[17], (D,), 0.1, 0.625, ((0, 2),))
    return {"tokens": tokens, "cont_lengths": cont_lengths, "grad_out": grad_out, "ln_gain_one": ln_gain_one, "ln_bias_one": ln_bias_one, "w_query": w_query, "b_query": b_query, "w_key": w_key, "w_value": w_value, "b_value": b_value, "w_out": w_out, "b_out": b_out, "ln_gain_two": ln_gain_two, "ln_bias_two": ln_bias_two, "w_in": w_in, "b_in": b_in, "w_back": w_back, "b_back": b_back}


EPSILON = 1e-12
NEGATIVE = -1e+30

@jax.custom_vjp
def low(v):
    return lax.optimization_barrier(v.astype(jnp.bfloat16)).astype(jnp.float32)

@jax.custom_vjp
def low_back(v):
    return v

def low_keep(v):
    return (low(v), None)

def low_pass(kept, grad):
    return (grad,)

def back_keep(v):
    return (v, None)

def back_low(kept, grad):
    return (low(grad),)
low.defvjp(low_keep, low_pass)
low_back.defvjp(back_keep, back_low)

def matmul_high(left_side, right_side):
    return jnp.dot(left_side, right_side, precision=lax.Precision.HIGHEST, preferred_element_type=jnp.float32)

def layer_norm(values, gain_vec, bias_vec):
    center = values - lax.optimization_barrier(jnp.mean(values, axis=-1, keepdims=True))
    variance = lax.optimization_barrier(jnp.mean(center * center, axis=-1, keepdims=True))
    return center * lax.rsqrt(variance + EPSILON) * gain_vec + bias_vec

def dealt_position(stored, stripe, n_ctx):
    block = stored // stripe
    within = stored % stripe
    device = block // 2
    return (jnp.where(block % 2 == 0, device, 2 * n_ctx - 1 - device) * stripe + within).astype(jnp.int32)

def group_forward(inputs, lengths, weights):
    gain_one, bias_one, query_w, query_b, key_w, value_w, value_b, out_w, out_b, gain_two, bias_two, in_w, in_b, back_w, back_b = weights
    normed = low(layer_norm(inputs, gain_one, bias_one))
    queries = low_back(low(matmul_high(normed, query_w) + query_b))
    key_vals = low_back(low(matmul_high(normed, key_w)))
    value_vals = low_back(low(matmul_high(normed, value_w) + value_b))
    positions = dealt_position(jnp.arange(SEQ, dtype=jnp.int32), SEQ // (2 * N_CTX), N_CTX)
    seg_ends = jnp.cumsum(lengths, dtype=jnp.int32)
    beyond = lax.optimization_barrier(jnp.sum(((positions - PROMPT)[:, None] >= seg_ends[None, :]).astype(jnp.int32), axis=1, dtype=jnp.int32))
    segment = jnp.where(positions >= PROMPT, beyond, -1)
    keys_heads = key_vals.reshape(SEQ, HEADS, HEAD)
    values_heads = value_vals.reshape(SEQ, HEADS, HEAD)
    query_block = math.gcd(SEQ, 512)

    def attend(block_index):
        block_start = block_index * query_block
        query_part = lax.dynamic_slice_in_dim(queries, block_start, query_block, 0).reshape(query_block, HEADS, HEAD)
        query_pos = lax.dynamic_slice_in_dim(positions, block_start, query_block, 0)
        query_seg = lax.dynamic_slice_in_dim(segment, block_start, query_block, 0)
        allowed = (positions[None, :] <= query_pos[:, None]) & ((positions < PROMPT)[None, :] | (segment[None, :] == query_seg[:, None]))
        raw_scores = jnp.einsum('rhe,nhe->hrn', query_part, keys_heads, precision=lax.Precision.HIGHEST)
        scores = low_back(raw_scores * HEAD ** (-0.5))
        scores = jnp.where(allowed[None], scores, NEGATIVE)
        shifted = scores - lax.optimization_barrier(jnp.max(scores, axis=-1, keepdims=True))
        exps = jnp.exp(shifted)
        soft = exps / lax.optimization_barrier(jnp.sum(exps, axis=-1, keepdims=True))
        mixed = jnp.einsum('hrn,nhe->rhe', low(soft), values_heads, precision=lax.Precision.HIGHEST)
        return mixed.reshape(query_block, HEADS * HEAD)
    attended = lax.map(jax.checkpoint(attend), jnp.arange(SEQ // query_block, dtype=jnp.int32))
    attended = low_back(low(attended.reshape(SEQ, HEADS * HEAD)))
    branch = low_back(matmul_high(attended, out_w) + out_b)
    middle = inputs + branch
    normed_two = low(layer_norm(middle, gain_two, bias_two))
    hidden_pre = low_back(matmul_high(normed_two, in_w) + in_b)
    hidden = low(jax.nn.gelu(hidden_pre, approximate=False))
    return middle + matmul_high(hidden, back_w) + back_b

def reference(tokens, cont_lengths, grad_out, ln_gain_one, ln_bias_one, w_query, b_query, w_key, w_value, b_value, w_out, b_out, ln_gain_two, ln_bias_two, w_in, b_in, w_back, b_back):
    params = tuple((member.astype(jnp.float32) for member in (ln_gain_one, ln_bias_one, w_query, b_query, w_key, w_value, b_value, w_out, b_out, ln_gain_two, ln_bias_two, w_in, b_in, w_back, b_back)))

    def forward(inputs, weights):

        def group_step(carried, group_item):
            return (carried, jax.checkpoint(group_forward)(group_item[0], group_item[1], weights))
        unused, results = lax.scan(group_step, jnp.zeros((), jnp.float32), (inputs, cont_lengths))
        return results
    results, pullback = jax.vjp(forward, tokens.astype(jnp.float32), params)
    grad_inputs, grad_params = pullback(grad_out.astype(jnp.float32))
    return (results.astype(jnp.bfloat16), grad_inputs, grad_params[0], grad_params[1], grad_params[2], grad_params[3], grad_params[4], grad_params[5], grad_params[6], grad_params[7], grad_params[8], grad_params[9], grad_params[10], grad_params[11], grad_params[12], grad_params[13], grad_params[14])
```

```python
import jax
import jax.numpy as jnp
from jax import lax
from jax.experimental import pallas as pl
from jax.experimental.pallas import tpu as pltpu
from jax.sharding import PartitionSpec as P

HEADS = 12
HEAD = 64
PROMPT = 2048
MOSTLEN = 512
HP = 8
TILE = 256

EPSILON = 1e-12
NEGATIVE = -1e30
F32 = jnp.float32
BF16 = jnp.bfloat16


def dot_plain(left_side, right_side):
    return jnp.dot(left_side, right_side, preferred_element_type=F32)


def dot_inner(left_side, right_side):
    return lax.dot_general(
        left_side, right_side, (((0,), (0,)), ((), ())), preferred_element_type=F32
    )


def dot_transposed(left_side, right_side):
    return lax.dot_general(
        left_side, right_side, (((1,), (1,)), ((), ())), preferred_element_type=F32
    )


def exact_gelu(values):
    return jax.nn.gelu(values, approximate=False)


def norm_forward(values, gain_vec, bias_vec):
    center = values - jnp.mean(values, axis=-1, keepdims=True)
    scaled = lax.rsqrt(jnp.mean(center * center, axis=-1, keepdims=True) + EPSILON)
    normed = center * scaled
    return (normed * gain_vec + bias_vec, normed, scaled)


def norm_backward(upstream, normed, scaled, gain_vec):
    inner_grad = upstream * gain_vec
    result = scaled * (
        inner_grad
        - jnp.mean(inner_grad, axis=-1, keepdims=True)
        - normed * jnp.mean(inner_grad * normed, axis=-1, keepdims=True)
    )
    return (
        result,
        jnp.sum(upstream * normed, axis=0, keepdims=True),
        jnp.sum(upstream, axis=0, keepdims=True),
    )


def vmem_specs(count):
    return [pl.BlockSpec(memory_space=pltpu.VMEM) for unused in range(count)]


SMEM_SPEC = pl.BlockSpec(memory_space=pltpu.SMEM)
PARAMS = pltpu.CompilerParams(vmem_limit_bytes=56 << 20)


def project_kernel(
    wsh_ref, x_ref, gain_ref, bias_ref, mine_ref, other_ref, add_ref, out_ref, low_ref
):
    half = mine_ref.shape[1]
    mine_at = wsh_ref[0]

    @pl.when(pl.program_id(0) == 0)
    def _():
        normed, unused, unused_two = norm_forward(
            x_ref[...].astype(F32), gain_ref[...], bias_ref[...]
        )
        low_ref[0] = normed[:, :half].astype(BF16)
        low_ref[1] = normed[:, half:].astype(BF16)

    total = dot_plain(low_ref[mine_at], mine_ref[0]) + dot_plain(low_ref[1 - mine_at], other_ref[0])
    out_ref[0] = (total + add_ref[0]).astype(BF16)


def project(mine_at, rows_in, gain, bias, mine, other, add):
    parts, half, width = mine.shape
    count, model = rows_in.shape
    whole = lambda i, *unused: (0, 0)
    return pl.pallas_call(
        project_kernel,
        grid_spec=pltpu.PrefetchScalarGridSpec(
            num_scalar_prefetch=1,
            grid=(parts,),
            in_specs=[
                pl.BlockSpec((count, model), whole),
                pl.BlockSpec((1, model), whole),
                pl.BlockSpec((1, model), whole),
                pl.BlockSpec((1, half, width), lambda i, *unused: (i, 0, 0)),
                pl.BlockSpec((1, half, width), lambda i, *unused: (i, 0, 0)),
                pl.BlockSpec((1, 1, width), lambda i, *unused: (i, 0, 0)),
            ],
            out_specs=[
                pl.BlockSpec((1, count, width), lambda i, *unused: (i, 0, 0)),
                pl.BlockSpec((2, count, half), lambda i, *unused: (0, 0, 0)),
            ],
        ),
        out_shape=[
            jax.ShapeDtypeStruct((parts, count, width), BF16),
            jax.ShapeDtypeStruct((2, count, half), BF16),
        ],
        compiler_params=PARAMS,
        name="project",
    )(mine_at, rows_in, gain, bias, mine, other, add)


def finish_kernel(
    wsh_ref,
    x_ref,
    gain_ref,
    dmid_ref,
    low_ref,
    grads_ref,
    mine_ref,
    other_ref,
    keep_ref,
    send_ref,
    cols_ref,
    out_ref,
    dgain_ref,
    dbias_ref,
    acc_ref,
):
    step = pl.program_id(0)
    mine_at = wsh_ref[0]
    grads = grads_ref[0]
    keep_ref[0] = dot_inner(low_ref[mine_at], grads).astype(BF16)
    send_ref[0] = dot_inner(low_ref[1 - mine_at], grads).astype(BF16)
    cols_ref[0] = jnp.sum(grads.astype(F32), axis=0, keepdims=True)

    @pl.when(step == 0)
    def _():
        acc_ref[...] = jnp.zeros_like(acc_ref)

    acc_ref[mine_at] += dot_transposed(grads, mine_ref[0])
    acc_ref[1 - mine_at] += dot_transposed(grads, other_ref[0])

    @pl.when(step == pl.num_programs(0) - 1)
    def _():
        unused, normed, scaled = norm_forward(x_ref[...].astype(F32), 1.0, 0.0)
        upstream = jnp.concatenate([acc_ref[0], acc_ref[1]], axis=1)
        result, dgain, dbias = norm_backward(upstream, normed, scaled, gain_ref[...])
        out_ref[...] = dmid_ref[...] + result
        dgain_ref[...] = dgain
        dbias_ref[...] = dbias


def finish(mine_at, rows_in, gain, dmid, low, grads, mine, other):
    parts, half, width = mine.shape
    count, model = rows_in.shape
    whole = lambda i, *unused: (0, 0)
    each = lambda i, *unused: (i, 0, 0)
    return pl.pallas_call(
        finish_kernel,
        grid_spec=pltpu.PrefetchScalarGridSpec(
            num_scalar_prefetch=1,
            grid=(parts,),
            in_specs=[
                pl.BlockSpec((count, model), whole),
                pl.BlockSpec((1, model), whole),
                pl.BlockSpec((count, model), whole),
                pl.BlockSpec((2, count, half), lambda i, *unused: (0, 0, 0)),
                pl.BlockSpec((1, count, width), each),
                pl.BlockSpec((1, half, width), each),
                pl.BlockSpec((1, half, width), each),
            ],
            out_specs=[
                pl.BlockSpec((1, half, width), each),
                pl.BlockSpec((1, half, width), each),
                pl.BlockSpec((1, 1, width), each),
                pl.BlockSpec((count, model), whole),
                pl.BlockSpec((1, model), whole),
                pl.BlockSpec((1, model), whole),
            ],
            scratch_shapes=[pltpu.VMEM((2, count, half), F32)],
        ),
        out_shape=[
            jax.ShapeDtypeStruct((parts, half, width), BF16),
            jax.ShapeDtypeStruct((parts, half, width), BF16),
            jax.ShapeDtypeStruct((parts, 1, width), F32),
            jax.ShapeDtypeStruct((count, model), F32),
            jax.ShapeDtypeStruct((1, model), F32),
            jax.ShapeDtypeStruct((1, model), F32),
        ],
        compiler_params=PARAMS,
        name="finish",
    )(mine_at, rows_in, gain, dmid, low, grads, mine, other)


def head_columns(block, kind, head, heads):
    at = (kind * heads + head) * HEAD
    return block[:, at : at + HEAD]


def sorted_rows(stripe, source, half, span):
    return source * stripe if half == 0 else span + (HP - 1 - source) * stripe


def load_queries(packed_ref, target_ref, heads, kind, scaled):
    stripe = packed_ref.shape[2]
    span = HP * stripe
    for source in range(HP):
        for half in range(2):
            at = sorted_rows(stripe, source, half, span)
            block = packed_ref[source, half]
            for head in range(heads):
                part = head_columns(block, kind, head, heads)
                if scaled:
                    part = part * jnp.asarray(HEAD**-0.5, BF16)
                target_ref[head, at : at + stripe, :] = part


def load_keys(rows_of, total, stripe, heads, keys_ref, values_ref, turned_ref, turned_kind):
    for block_at in range(total // stripe):
        block = rows_of(block_at)
        at = block_at * stripe
        for head in range(heads):
            keys_ref[head, at : at + stripe, :] = head_columns(block, 0, head, heads)
            values_ref[head, at : at + stripe, :] = head_columns(block, 1, head, heads)
    source_ref = keys_ref if turned_kind == 0 else values_ref
    for chunk in range(total // TILE):
        for head in range(heads):
            turned_ref[head, chunk] = source_ref[
                head, chunk * TILE : (chunk + 1) * TILE, :
            ].T


def local_rows(packed_ref):
    stripe = packed_ref.shape[2]

    def rows_of(block_at):
        if block_at < HP:
            return packed_ref[block_at, 0]
        return packed_ref[2 * HP - 1 - block_at, 1]

    return rows_of


def remote_rows(prompts_ref, halo_ref):
    parts = prompts_ref.shape[0]
    halo_blocks = halo_ref.shape[0]

    def rows_of(block_at):
        if block_at < parts * HP:
            return prompts_ref[block_at // HP, block_at % HP]
        return halo_ref[halo_blocks - 1 - (block_at - parts * HP)]

    return rows_of


def row_slice(index, size=TILE):
    return pl.ds(pl.multiple_of(index * size, size), size)


def tile_iotas():
    return (
        lax.broadcasted_iota(jnp.int32, (TILE, TILE), 0),
        lax.broadcasted_iota(jnp.int32, (TILE, TILE), 1),
    )


def forward_step(query_tile, chunk, subs, mask, refs, heads):
    queries_ref, keys_ref, turned_ref, top_ref, sum_ref, acc_ref = refs
    for head in range(heads):
        query = queries_ref[head, row_slice(query_tile), :]
        scores = []
        for sub in range(subs):
            part = dot_transposed(keys_ref[head, row_slice(chunk + sub), :], query)
            if mask is not None:
                part = jnp.where(mask, part, NEGATIVE)
            scores.append(part)
        old = top_ref[query_tile, head]
        new = old
        for part in scores:
            new = jnp.maximum(new, jnp.max(part, axis=0, keepdims=True))
        alpha = jnp.exp(old - new)
        total = sum_ref[query_tile, head] * alpha
        acc = acc_ref[query_tile, head] * alpha
        for sub, part in enumerate(scores):
            soft = jnp.exp(part - new)
            total = total + jnp.sum(soft, axis=0, keepdims=True)
            acc = acc + dot_plain(turned_ref[head, chunk + sub], soft.astype(BF16))
        top_ref[query_tile, head] = new
        sum_ref[query_tile, head] = total
        acc_ref[query_tile, head] = acc


def loop(first, last, step):
    def run(index, unused):
        step(index)
        return unused

    lax.fori_loop(first, last, run, 0)


def walk_local(tiles, scalars_ref, starts_ref, step):
    wide = 2 if tiles % 2 == 0 else 1

    def prompt_tile(tile):
        loop(0, tile, lambda chunk: step(tile, chunk, 1, None))
        down, across = tile_iotas()
        step(tile, tile, 1, down <= across)

    def cont_tile(tile):
        query_tile = tiles + tile
        loop(0, tiles // wide, lambda chunk: step(query_tile, chunk * wide, wide, None))

        def band(chunk):
            down, across = tile_iotas()
            shifted = down + (chunk - tile) * TILE
            begin = starts_ref[tile] - tile * TILE
            mask = (shifted <= across) & (shifted >= begin)
            step(query_tile, tiles + chunk, 1, mask)

        loop(scalars_ref[tile], tile + 1, band)

    loop(0, tiles, prompt_tile)
    loop(0, tiles, cont_tile)


def walk_remote(tiles, parts, halo_tiles, scalars_ref, starts_ref, step, done):
    wide = 2 if tiles % 2 == 0 else 1

    def whole(query_tile, part):
        loop(
            0,
            tiles // wide,
            lambda chunk: step(query_tile, part * tiles + chunk * wide, wide, None),
        )

    def prompt_tile(tile):
        for part in range(parts):

            @pl.when(scalars_ref[2 * tiles + part] > 0)
            def _():
                whole(tile, part)

        done(tile, False)

    def cont_tile(tile):
        query_tile = tiles + tile
        for part in range(parts):
            whole(query_tile, part)

        def band(chunk):
            down, unused = tile_iotas()
            shifted = down + (chunk - halo_tiles) * TILE
            step(query_tile, parts * tiles + chunk, 1, shifted >= starts_ref[tile])

        loop(scalars_ref[tiles + tile], halo_tiles, band)
        done(query_tile, True)

    loop(0, tiles, prompt_tile)
    loop(0, tiles, cont_tile)


def forward_local_kernel(
    scalars_ref,
    starts_ref,
    packed_ref,
    top_ref,
    sum_ref,
    acc_ref,
    queries_ref,
    keys_ref,
    values_ref,
    turned_ref,
):
    heads = queries_ref.shape[0]
    stripe = packed_ref.shape[2]
    span = HP * stripe
    load_queries(packed_ref, queries_ref, heads, 2, True)
    load_keys(
        local_rows(packed_ref), 2 * span, stripe, heads, keys_ref, values_ref, turned_ref, 1
    )
    top_ref[...] = jnp.full(top_ref.shape, NEGATIVE, F32)
    sum_ref[...] = jnp.zeros(sum_ref.shape, F32)
    acc_ref[...] = jnp.zeros(acc_ref.shape, F32)
    refs = (queries_ref, keys_ref, turned_ref, top_ref, sum_ref, acc_ref)
    walk_local(
        span // TILE,
        scalars_ref,
        starts_ref,
        lambda tile, chunk, subs, mask: forward_step(tile, chunk, subs, mask, refs, heads),
    )


def store_rows(out_ref, block, query_tile, continued, columns):
    stripe = out_ref.shape[2]
    per = TILE // stripe
    tiles = HP // per
    for piece in range(per):
        rows = block[piece * stripe : (piece + 1) * stripe, :]
        if continued:
            source = HP - 1 - ((query_tile - tiles) * per + piece)
            out_ref[source, 1, :, columns] = rows
        else:
            out_ref[query_tile * per + piece, 0, :, columns] = rows


def forward_remote_kernel(
    scalars_ref,
    starts_ref,
    packed_ref,
    prompts_ref,
    halo_ref,
    top_in_ref,
    sum_in_ref,
    acc_in_ref,
    out_ref,
    log_ref,
    mixed_ref,
    queries_ref,
    keys_ref,
    values_ref,
    turned_ref,
    top_ref,
    sum_ref,
    acc_ref,
):
    heads = queries_ref.shape[0]
    stripe = packed_ref.shape[2]
    span = HP * stripe
    parts = prompts_ref.shape[0]
    halo = halo_ref.shape[0] * stripe
    load_queries(packed_ref, queries_ref, heads, 2, True)
    load_keys(
        remote_rows(prompts_ref, halo_ref),
        parts * span + halo,
        stripe,
        heads,
        keys_ref,
        values_ref,
        turned_ref,
        1,
    )
    top_ref[...] = top_in_ref[...]
    sum_ref[...] = sum_in_ref[...]
    acc_ref[...] = acc_in_ref[...]
    refs = (queries_ref, keys_ref, turned_ref, top_ref, sum_ref, acc_ref)

    def done(query_tile, continued):
        mixed = []
        for head in range(heads):
            total = sum_ref[query_tile, head]
            part = acc_ref[query_tile, head] / total
            log_ref[query_tile, head] = top_ref[query_tile, head] + jnp.log(total)
            mixed_ref[query_tile, head] = part
            mixed.append(part)
        block = jnp.concatenate(mixed, axis=0).T.astype(BF16)
        store_rows(out_ref, block, query_tile, continued, slice(None))

    walk_remote(
        span // TILE,
        parts,
        halo // TILE,
        scalars_ref,
        starts_ref,
        lambda tile, chunk, subs, mask: forward_step(tile, chunk, subs, mask, refs, heads),
        done,
    )


def forward_local(scalars, starts, packed, heads):
    stripe = packed.shape[2]
    span = HP * stripe
    tiles = 2 * span // TILE
    return pl.pallas_call(
        forward_local_kernel,
        in_specs=[SMEM_SPEC] + vmem_specs(2),
        out_specs=vmem_specs(3),
        out_shape=[
            jax.ShapeDtypeStruct((tiles, heads, 1, TILE), F32),
            jax.ShapeDtypeStruct((tiles, heads, 1, TILE), F32),
            jax.ShapeDtypeStruct((tiles, heads, HEAD, TILE), F32),
        ],
        scratch_shapes=[
            pltpu.VMEM((heads, 2 * span, HEAD), BF16),
            pltpu.VMEM((heads, 2 * span, HEAD), BF16),
            pltpu.VMEM((heads, 2 * span, HEAD), BF16),
            pltpu.VMEM((heads, tiles, HEAD, TILE), BF16),
        ],
        compiler_params=PARAMS,
        name="forward_local",
    )(scalars, starts, packed)


def forward_remote(scalars, starts, packed, prompts, halo, state, heads):
    stripe = packed.shape[2]
    span = HP * stripe
    tiles = 2 * span // TILE
    rows = prompts.shape[0] * span + halo.shape[0] * stripe
    return pl.pallas_call(
        forward_remote_kernel,
        in_specs=[SMEM_SPEC] + vmem_specs(7),
        out_specs=vmem_specs(3),
        out_shape=[
            jax.ShapeDtypeStruct((HP, 2, stripe, heads * HEAD), BF16),
            jax.ShapeDtypeStruct((tiles, heads, 1, TILE), F32),
            jax.ShapeDtypeStruct((tiles, heads, HEAD, TILE), F32),
        ],
        scratch_shapes=[
            pltpu.VMEM((heads, 2 * span, HEAD), BF16),
            pltpu.VMEM((heads, rows, HEAD), BF16),
            pltpu.VMEM((heads, rows, HEAD), BF16),
            pltpu.VMEM((heads, rows // TILE, HEAD, TILE), BF16),
            pltpu.VMEM((tiles, heads, 1, TILE), F32),
            pltpu.VMEM((tiles, heads, 1, TILE), F32),
            pltpu.VMEM((tiles, heads, HEAD, TILE), F32),
        ],
        compiler_params=PARAMS,
        name="forward_remote",
    )(scalars, starts, packed, prompts, halo, *state)


def backward_step(query_tile, chunk, subs, mask, refs, heads):
    (
        queries_ref,
        ups_ref,
        keys_ref,
        values_ref,
        turned_ref,
        log_ref,
        delta_ref,
        dquery_ref,
        dkeys_ref,
        dvalues_ref,
    ) = refs
    for head in range(heads):
        query = queries_ref[head, row_slice(query_tile), :]
        ups = ups_ref[head, row_slice(query_tile), :]
        logsum = log_ref[query_tile, head]
        delta = delta_ref[query_tile, head]
        dquery = dquery_ref[query_tile, head]
        for sub in range(subs):
            rows = row_slice(chunk + sub)
            scores = dot_transposed(keys_ref[head, rows, :], query)
            grad_soft = dot_transposed(values_ref[head, rows, :], ups)
            soft = jnp.exp(scores - logsum)
            if mask is not None:
                soft = jnp.where(mask, soft, 0.0)
            grad_scores = (soft * (grad_soft - delta)).astype(BF16)
            dvalues_ref[head, rows, :] += dot_plain(soft.astype(BF16), ups)
            dkeys_ref[head, rows, :] += dot_plain(grad_scores, query)
            dquery = dquery + dot_plain(turned_ref[head, chunk + sub], grad_scores)
        dquery_ref[query_tile, head] = dquery


def key_grad_rows(dkeys_ref, dvalues_ref, at, stripe, heads):
    pieces = [dkeys_ref[head, at : at + stripe, :] for head in range(heads)]
    pieces = pieces + [dvalues_ref[head, at : at + stripe, :] for head in range(heads)]
    return jnp.concatenate(pieces, axis=1).astype(BF16)


def backward_remote_kernel(
    scalars_ref,
    starts_ref,
    packed_ref,
    ups_in_ref,
    prompts_ref,
    halo_ref,
    log_ref,
    mixed_ref,
    dprompts_ref,
    dhalo_ref,
    dquery_ref,
    delta_ref,
    queries_ref,
    ups_ref,
    keys_ref,
    values_ref,
    turned_ref,
    dkeys_ref,
    dvalues_ref,
):
    heads = queries_ref.shape[0]
    stripe = packed_ref.shape[2]
    span = HP * stripe
    parts = prompts_ref.shape[0]
    halo_blocks = halo_ref.shape[0]
    halo = halo_blocks * stripe
    load_queries(packed_ref, queries_ref, heads, 2, True)
    load_queries(ups_in_ref, ups_ref, heads, 0, False)
    load_keys(
        remote_rows(prompts_ref, halo_ref),
        parts * span + halo,
        stripe,
        heads,
        keys_ref,
        values_ref,
        turned_ref,
        0,
    )
    for query_tile in range(2 * span // TILE):
        for head in range(heads):
            ups = ups_ref[head, query_tile * TILE : (query_tile + 1) * TILE, :]
            delta_ref[query_tile, head] = jnp.sum(
                ups.T.astype(F32) * mixed_ref[query_tile, head], axis=0, keepdims=True
            )
    dquery_ref[...] = jnp.zeros(dquery_ref.shape, F32)
    dkeys_ref[...] = jnp.zeros(dkeys_ref.shape, F32)
    dvalues_ref[...] = jnp.zeros(dvalues_ref.shape, F32)
    refs = (
        queries_ref,
        ups_ref,
        keys_ref,
        values_ref,
        turned_ref,
        log_ref,
        delta_ref,
        dquery_ref,
        dkeys_ref,
        dvalues_ref,
    )
    walk_remote(
        span // TILE,
        parts,
        halo // TILE,
        scalars_ref,
        starts_ref,
        lambda tile, chunk, subs, mask: backward_step(tile, chunk, subs, mask, refs, heads),
        lambda tile, continued: None,
    )
    for block_at in range(parts * HP):
        dprompts_ref[block_at // HP, block_at % HP] = key_grad_rows(
            dkeys_ref, dvalues_ref, block_at * stripe, stripe, heads
        )
    for block_at in range(halo_blocks):
        dhalo_ref[halo_blocks - 1 - block_at] = key_grad_rows(
            dkeys_ref, dvalues_ref, parts * span + block_at * stripe, stripe, heads
        )


def backward_local_kernel(
    scalars_ref,
    starts_ref,
    packed_ref,
    ups_in_ref,
    log_ref,
    delta_ref,
    dquery_in_ref,
    out_ref,
    queries_ref,
    ups_ref,
    keys_ref,
    values_ref,
    turned_ref,
    dquery_ref,
    dkeys_ref,
    dvalues_ref,
):
    heads = queries_ref.shape[0]
    stripe = packed_ref.shape[2]
    span = HP * stripe
    width = heads * HEAD
    load_queries(packed_ref, queries_ref, heads, 2, True)
    load_queries(ups_in_ref, ups_ref, heads, 0, False)
    load_keys(
        local_rows(packed_ref), 2 * span, stripe, heads, keys_ref, values_ref, turned_ref, 0
    )
    dquery_ref[...] = dquery_in_ref[...]
    dkeys_ref[...] = jnp.zeros(dkeys_ref.shape, F32)
    dvalues_ref[...] = jnp.zeros(dvalues_ref.shape, F32)
    refs = (
        queries_ref,
        ups_ref,
        keys_ref,
        values_ref,
        turned_ref,
        log_ref,
        delta_ref,
        dquery_ref,
        dkeys_ref,
        dvalues_ref,
    )
    walk_local(
        span // TILE,
        scalars_ref,
        starts_ref,
        lambda tile, chunk, subs, mask: backward_step(tile, chunk, subs, mask, refs, heads),
    )
    for source in range(HP):
        for half in range(2):
            at = sorted_rows(stripe, source, half, span)
            out_ref[source, half, :, : 2 * width] = key_grad_rows(
                dkeys_ref, dvalues_ref, at, stripe, heads
            )
    pad = out_ref.shape[3] - 3 * width
    for query_tile in range(2 * span // TILE):
        turned = jnp.concatenate([dquery_ref[query_tile, head] for head in range(heads)], axis=0)
        block = (turned * HEAD**-0.5).T
        if pad:
            block = jnp.concatenate([block, jnp.zeros((TILE, pad), F32)], axis=1)
        store_rows(
            out_ref,
            block.astype(BF16),
            query_tile,
            query_tile >= span // TILE,
            slice(2 * width, None),
        )


def backward_remote(scalars, starts, packed, ups, prompts, halo, logsum, mixed, heads):
    stripe = packed.shape[2]
    span = HP * stripe
    tiles = 2 * span // TILE
    rows = prompts.shape[0] * span + halo.shape[0] * stripe
    return pl.pallas_call(
        backward_remote_kernel,
        in_specs=[SMEM_SPEC] + vmem_specs(7),
        out_specs=vmem_specs(4),
        out_shape=[
            jax.ShapeDtypeStruct(prompts.shape, BF16),
            jax.ShapeDtypeStruct(halo.shape, BF16),
            jax.ShapeDtypeStruct((tiles, heads, HEAD, TILE), F32),
            jax.ShapeDtypeStruct((tiles, heads, 1, TILE), F32),
        ],
        scratch_shapes=[
            pltpu.VMEM((heads, 2 * span, HEAD), BF16),
            pltpu.VMEM((heads, 2 * span, HEAD), BF16),
            pltpu.VMEM((heads, rows, HEAD), BF16),
            pltpu.VMEM((heads, rows, HEAD), BF16),
            pltpu.VMEM((heads, rows // TILE, HEAD, TILE), BF16),
            pltpu.VMEM((heads, rows, HEAD), F32),
            pltpu.VMEM((heads, rows, HEAD), F32),
        ],
        compiler_params=PARAMS,
        name="backward_remote",
    )(scalars, starts, packed, ups, prompts, halo, logsum, mixed)


def backward_local(scalars, starts, packed, ups, logsum, delta, dquery, heads):
    stripe = packed.shape[2]
    span = HP * stripe
    tiles = 2 * span // TILE
    rows = 2 * span
    return pl.pallas_call(
        backward_local_kernel,
        in_specs=[SMEM_SPEC] + vmem_specs(6),
        out_specs=vmem_specs(1)[0],
        out_shape=jax.ShapeDtypeStruct(packed.shape, BF16),
        scratch_shapes=[
            pltpu.VMEM((heads, rows, HEAD), BF16),
            pltpu.VMEM((heads, rows, HEAD), BF16),
            pltpu.VMEM((heads, rows, HEAD), BF16),
            pltpu.VMEM((heads, rows, HEAD), BF16),
            pltpu.VMEM((heads, tiles, HEAD, TILE), BF16),
            pltpu.VMEM((tiles, heads, HEAD, TILE), F32),
            pltpu.VMEM((heads, rows, HEAD), F32),
            pltpu.VMEM((heads, rows, HEAD), F32),
        ],
        compiler_params=PARAMS,
        name="backward_local",
    )(scalars, starts, packed, ups, logsum, delta, dquery)


def gather_pair(shard, axis):
    ways = lax.axis_size("wsh")
    if ways == 2:
        other = lax.ppermute(shard, "wsh", [(0, 1), (1, 0)])
        return (shard, other, lax.axis_index("wsh"))
    whole = lax.all_gather(shard, "wsh", axis=axis, tiled=True)
    first, second = jnp.split(whole, 2, axis=axis)
    return (first, second, jnp.zeros((), jnp.int32))


def scatter_rows(keep, send):
    ways = lax.axis_size("wsh")
    if ways == 2:
        got = lax.ppermute(send, "wsh", [(0, 1), (1, 0)])
        return (keep.astype(F32) + got.astype(F32)).astype(BF16)
    whole = jnp.concatenate([keep, send], axis=-2)
    return lax.psum_scatter(whole, "wsh", scatter_dimension=whole.ndim - 2, tiled=True)


def reduce_parts(parts, axis="ctx"):
    ways = lax.axis_size(axis)
    bits = ways.bit_length() - 1
    index = lax.axis_index(axis)
    rest = tuple(range(3, bits))
    orders = [(0, 1, 2) + rest, (1, 2, 0) + rest, (2, 0, 1) + rest]
    parts = list(parts)

    def traded(value, bit):
        return lax.ppermute(value, axis, [(i, i ^ (1 << bit)) for i in range(ways)])

    for step in range(bits):
        for at in range(len(parts)):
            bit = orders[at % 3][step]
            flag = (index >> bit) & 1
            count = parts[at].shape[0] // 2
            keep = lax.dynamic_slice_in_dim(parts[at], flag * count, count, 0)
            send = lax.dynamic_slice_in_dim(parts[at], (1 - flag) * count, count, 0)
            got = traded(send, bit)
            parts[at] = (keep.astype(F32) + got.astype(F32)).astype(BF16)
    for step in reversed(range(bits)):
        for at in range(len(parts)):
            bit = orders[at % 3][step]
            flag = (index >> bit) & 1
            mine = parts[at]
            got = traded(mine, bit)
            parts[at] = jnp.where(
                flag == 0,
                jnp.concatenate([mine, got], axis=0),
                jnp.concatenate([got, mine], axis=0),
            )
    return parts


def own_half(value, at, axis=0):
    count = value.shape[axis] // 2
    keep = lax.dynamic_slice_in_dim(value, at * count, count, axis)
    send = lax.dynamic_slice_in_dim(value, (1 - at) * count, count, axis)
    return keep, send


def body(
    tokens,
    cont_lengths,
    grad_out,
    ln_gain_one,
    ln_bias_one,
    w_query,
    b_query,
    w_key,
    w_value,
    b_value,
    w_out,
    b_out,
    ln_gain_two,
    ln_bias_two,
    w_in,
    b_in,
    w_back,
    b_back,
):
    groups, rows, model = tokens.shape
    ways = lax.axis_size("ctx")
    shards = lax.axis_size("wsh")
    wsh_at = lax.axis_index("wsh")
    parts = ways // HP
    stripe = rows // 2
    span = HP * stripe
    tiles = span // TILE
    heads = HEADS * groups // HP
    triples = HEADS // heads
    width = heads * HEAD
    packed_width = -(-3 * width // 128) * 128
    pad = packed_width - 3 * width
    count = groups * rows
    hidden_size = w_in.shape[1]
    my_ctx = lax.axis_index("ctx")
    part_at = my_ctx // HP
    group_at = (my_ctx % HP) % groups

    small_rows = [ln_gain_one, ln_bias_one, b_query, b_value, b_out, ln_gain_two, ln_bias_two]
    small_rows = small_rows + [b_back, b_in]
    shard_width = model // shards
    small = jnp.concatenate([row.reshape(-1, shard_width) for row in small_rows], axis=0)
    small = lax.all_gather(small, "wsh", axis=0, tiled=False) if shards != 2 else None or (
        lambda mine: (
            lambda got: jnp.where(wsh_at == 0, jnp.stack([mine, got]), jnp.stack([got, mine]))
        )(lax.ppermute(mine, "wsh", [(0, 1), (1, 0)]))
    )(small)
    vectors = [small[:, at].reshape(1, model).astype(F32) for at in range(8)]
    gain_one, bias_one, query_b, value_b, out_b, gain_two, bias_two, back_b = vectors
    in_b = small[:, 8:].reshape(1, hidden_size).astype(F32)

    def by_triple(value):
        return value.reshape(value.shape[0], triples, width).transpose(1, 0, 2)

    stacked = [by_triple(w_key), by_triple(w_value), by_triple(w_query)]
    stacked_b = [jnp.zeros((triples, 1, width), F32), by_triple(value_b), by_triple(query_b)]
    if pad:
        stacked.append(jnp.zeros((triples, w_key.shape[0], pad), BF16))
        stacked_b.append(jnp.zeros((triples, 1, pad), F32))
    stacked = jnp.concatenate(stacked, axis=2)
    stacked_b = jnp.concatenate(stacked_b, axis=2)
    first_w, second_w, first_at = gather_pair(stacked, 1)
    at_vector = first_at.reshape(1)
    out_w = lax.all_gather(w_out, "wsh", axis=0, tiled=True)
    in_w = lax.all_gather(w_in, "wsh", axis=0, tiled=True)
    back_w = lax.all_gather(w_back, "wsh", axis=0, tiled=True)

    token_rows = tokens.reshape(count, model)
    packed, low_one = project(
        at_vector, token_rows, gain_one, bias_one, first_w, second_w, stacked_b
    )
    cube = [[part * HP + at for at in range(HP)] for part in range(parts)]

    def exchange(value):
        return lax.all_to_all(value, "ctx", 0, 0, axis_index_groups=cube)

    packed = exchange(packed.reshape(HP, rows, packed_width)).reshape(HP, 2, stripe, packed_width)

    lengths = lax.dynamic_index_in_dim(cont_lengths, group_at, 0, keepdims=False)
    seg_ends = jnp.cumsum(lengths, dtype=jnp.int32)
    chunk_start = (parts - 1 - part_at) * span
    places = chunk_start + jnp.arange(span, dtype=jnp.int32)
    begins = jnp.max(
        jnp.where(seg_ends[None, :] <= places[:, None], seg_ends[None, :], 0), axis=1
    )
    starts = (begins - chunk_start).reshape(tiles, 1, TILE)
    halo_rows = min(MOSTLEN, span)
    halo_tiles = halo_rows // TILE
    halo_blocks = halo_rows // stripe
    first_start = starts[:, 0, 0]
    local_first = jnp.maximum(first_start, 0) // TILE
    has_halo = part_at < parts - 1
    halo_first = jnp.where(
        has_halo, jnp.clip(first_start + halo_rows, 0, halo_rows) // TILE, halo_tiles
    )
    seen = [(part_at >= shift).astype(jnp.int32).reshape(1) for shift in range(1, parts)]
    scalars = jnp.concatenate([local_first, halo_first] + seen).astype(jnp.int32)

    def shifted(value, shift):
        pairs = [
            (part * HP + at, ((part + shift) % parts) * HP + at)
            for part in range(parts)
            for at in range(HP)
        ]
        return lax.ppermute(value, "ctx", pairs)

    def to_former(value):
        pairs = [(i, i - HP) for i in range(HP, ways)]
        return lax.ppermute(value, "ctx", pairs)

    def to_latter(value):
        pairs = [(i, i + HP) for i in range(ways - HP)]
        return lax.ppermute(value, "ctx", pairs)

    own_prompts = packed[:, 0, :, : 2 * width]
    prompts = jnp.stack([shifted(own_prompts, shift) for shift in range(1, parts)])
    halo = to_former(packed[:halo_blocks, 1, :, : 2 * width])
    state = forward_local(scalars, starts, packed, heads)
    mixed_rows, logsum, mixed = forward_remote(
        scalars, starts, packed, prompts, halo, state, heads
    )

    def to_tokens(value):
        back = exchange(value.reshape(HP, rows, width)).reshape(triples, count, width)
        return back.transpose(1, 0, 2).reshape(count, model)

    def to_heads(value):
        split = value.reshape(count, triples, width).transpose(1, 0, 2)
        return exchange(split.reshape(HP, rows, width)).reshape(HP, 2, stripe, width)

    low_attended = to_tokens(mixed_rows)

    inputs = token_rows.astype(F32)
    middle = inputs + dot_plain(low_attended, out_w) + out_b
    normed_two, hat_two, scale_two = norm_forward(middle, gain_two, bias_two)
    low_two = normed_two.astype(BF16)
    hidden_pre = dot_plain(low_two, in_w) + in_b
    hidden, gelu_back = jax.vjp(exact_gelu, hidden_pre)
    low_hidden = hidden.astype(BF16)
    result = middle + dot_plain(low_hidden, back_w) + back_b
    out_tokens = result.astype(BF16).reshape(groups, rows, model)
    upstream_low = grad_out.reshape(count, model)
    upstream = upstream_low.astype(F32)
    grad_back_w = dot_inner(low_hidden, upstream_low).astype(BF16)
    grad_back_b = jnp.sum(upstream, axis=0, keepdims=True)
    grad_hidden = dot_transposed(upstream_low, back_w)
    grad_pre = gelu_back(grad_hidden)[0].astype(BF16)
    grad_in_w = dot_inner(low_two, grad_pre).astype(BF16)
    grad_in_b = jnp.sum(grad_pre.astype(F32), axis=0, keepdims=True)
    grad_normed_two = dot_transposed(grad_pre, in_w)
    grad_mid_norm, grad_gain_two, grad_bias_two = norm_backward(
        grad_normed_two, hat_two, scale_two, gain_two
    )
    grad_middle = upstream + grad_mid_norm
    grad_branch = grad_middle.astype(BF16)
    grad_out_w = dot_inner(low_attended, grad_branch).astype(BF16)
    grad_out_b = jnp.sum(grad_branch.astype(F32), axis=0, keepdims=True)
    grad_attended = dot_transposed(grad_branch, out_w).astype(BF16)

    ups = to_heads(grad_attended)
    dprompts, dhalo, dquery, delta = backward_remote(
        scalars, starts, packed, ups, prompts, halo, logsum, mixed, heads
    )
    returned = sum(
        shifted(dprompts[shift - 1], parts - shift).astype(F32) for shift in range(1, parts)
    )
    returned_halo = to_latter(dhalo).astype(F32)
    dpacked = backward_local(scalars, starts, packed, ups, logsum, delta, dquery, heads)
    extra = jnp.zeros((HP, 2, stripe, packed_width), F32)
    extra = extra.at[:, 0, :, : 2 * width].set(returned)
    extra = extra.at[:halo_blocks, 1, :, : 2 * width].set(returned_halo)
    dpacked = (dpacked.astype(F32) + extra).astype(BF16)

    blocks = hidden_size // model

    def to_blocks(value):
        split = value.reshape(value.shape[0], blocks, model)
        return split.transpose(1, 0, 2).reshape(-1, model)

    small_mid = jnp.concatenate(
        [grad_out_b, grad_gain_two, grad_bias_two, grad_back_b, grad_in_b.reshape(-1, model)],
        axis=0,
    )
    shard_rows = model // shards
    mid_rows = (2 * blocks + 1) * shard_rows
    mid_total = -(-(mid_rows + 8) // 512) * 512
    if shards == 2:
        keep_in, send_in = own_half(grad_in_w, wsh_at)
        keep_back, send_back = own_half(grad_back_w, wsh_at)
        keep_out, send_out = own_half(grad_out_w, wsh_at)
        filler = jnp.zeros((mid_total - mid_rows - small_mid.shape[0], model), BF16)
        tail = [small_mid.astype(BF16), filler]
        mid_keep = jnp.concatenate([to_blocks(keep_in), keep_back, keep_out] + tail, axis=0)
        mid_send = jnp.concatenate([to_blocks(send_in), send_back, send_out] + tail, axis=0)
        mid_sum = scatter_rows(mid_keep, mid_send)
    else:
        scattered = [
            lax.psum_scatter(part, "wsh", scatter_dimension=0, tiled=True)
            for part in (grad_in_w, grad_back_w, grad_out_w)
        ]
        small_sum = lax.psum(small_mid.astype(BF16), "wsh")
        filler = jnp.zeros((mid_total - mid_rows - small_mid.shape[0], model), BF16)
        mid_sum = jnp.concatenate(
            [to_blocks(scattered[0]), scattered[1], scattered[2], small_sum, filler], axis=0
        )
    third = mid_total // 3 // 256 * 256
    cuts = [third + 256 * (mid_total // 256 - 3 * (third // 256) > at) for at in range(3)]
    edges = [0, cuts[0], cuts[0] + cuts[1], mid_total]
    mid_parts = reduce_parts([mid_sum[edges[at] : edges[at + 1]] for at in range(3)])
    mid_done = jnp.concatenate(mid_parts, axis=0)

    grads = exchange(dpacked.reshape(HP, rows, packed_width)).reshape(triples, count, packed_width)
    keep, send, columns, grad_rows, grad_gain_one, grad_bias_one = finish(
        at_vector, token_rows, gain_one, grad_middle, low_one, grads, first_w, second_w
    )
    small_last = jnp.concatenate(
        [
            columns.reshape(triples, packed_width),
            jnp.pad(
                jnp.concatenate([grad_gain_one, grad_bias_one], axis=0),
                ((0, 0), (0, 2 * packed_width - model)),
            ).reshape(4, packed_width),
        ],
        axis=0,
    ).astype(BF16)
    last_rows = triples * shard_rows
    last_total = -(-(last_rows + 8) // 128) * 128
    filler = jnp.zeros((last_total - last_rows - small_last.shape[0], packed_width), BF16)
    if shards == 2:
        tail = [small_last, filler]
        last_sum = scatter_rows(
            jnp.concatenate([keep.reshape(last_rows, packed_width)] + tail, axis=0),
            jnp.concatenate([send.reshape(last_rows, packed_width)] + tail, axis=0),
        )
    else:
        scattered = scatter_rows(keep, send).reshape(last_rows, packed_width)
        last_sum = jnp.concatenate([scattered, lax.psum(small_last, "wsh"), filler], axis=0)
    third = last_total // 3 // 128 * 128
    cuts = [third + 128 * (last_total // 128 - 3 * (third // 128) > at) for at in range(3)]
    edges = [0, cuts[0], cuts[0] + cuts[1], last_total]
    last_parts = reduce_parts([last_sum[edges[at] : edges[at + 1]] for at in range(3)])
    last_done = jnp.concatenate(last_parts, axis=0)

    def own(vector):
        size = vector.shape[0] // shards
        return lax.dynamic_slice_in_dim(vector, wsh_at * size, size, 0).astype(F32)

    at = blocks * shard_rows
    new_in_w = mid_done[:at].reshape(blocks, shard_rows, model).transpose(1, 0, 2)
    new_in_w = new_in_w.reshape(shard_rows, hidden_size).astype(F32)
    new_back_w = mid_done[at : 2 * at].astype(F32)
    new_out_w = mid_done[2 * at : mid_rows].astype(F32)
    tail = mid_done[mid_rows : mid_rows + 4 + blocks]
    new_out_b, new_gain_two, new_bias_two, new_back_b = [own(tail[i]) for i in range(4)]
    new_in_b = own(tail[4:].reshape(hidden_size))

    last_w = last_done[:last_rows].reshape(triples, shard_rows, packed_width)
    tail = last_done[last_rows : last_rows + triples + 4]

    def untriple(kind):
        piece = last_w[:, :, kind * width : (kind + 1) * width]
        return piece.transpose(1, 0, 2).reshape(shard_rows, model).astype(F32)

    def unvector(kind):
        return own(tail[:triples, kind * width : (kind + 1) * width].reshape(model))

    new_key_w, new_value_w, new_query_w = [untriple(kind) for kind in range(3)]
    new_value_b, new_query_b = unvector(1), unvector(2)
    new_gain_one = own(tail[triples : triples + 2].reshape(-1)[:model])
    new_bias_one = own(tail[triples + 2 :].reshape(-1)[:model])
    return (
        out_tokens,
        grad_rows.reshape(groups, rows, model),
        new_gain_one,
        new_bias_one,
        new_query_w,
        new_query_b,
        new_key_w,
        new_value_w,
        new_value_b,
        new_out_w,
        new_out_b,
        new_gain_two,
        new_bias_two,
        new_in_w,
        new_in_b,
        new_back_w,
        new_back_b,
    )


def solution(mesh):
    placed = (
        P("wsh", "ctx", None),
        P("wsh", None),
        P("wsh", "ctx", None),
        P("wsh"),
        P("wsh"),
        P("wsh", None),
        P("wsh"),
        P("wsh", None),
        P("wsh", None),
        P("wsh"),
        P("wsh", None),
        P("wsh"),
        P("wsh"),
        P("wsh"),
        P("wsh", None),
        P("wsh"),
        P("wsh", None),
        P("wsh"),
    )
    return jax.shard_map(
        body,
        mesh=mesh,
        in_specs=placed,
        out_specs=(
            P("wsh", "ctx", None),
            P("wsh", "ctx", None),
            P("wsh"),
            P("wsh"),
            P("wsh", None),
            P("wsh"),
            P("wsh", None),
            P("wsh", None),
            P("wsh"),
            P("wsh", None),
            P("wsh"),
            P("wsh"),
            P("wsh"),
            P("wsh", None),
            P("wsh"),
            P("wsh", None),
            P("wsh"),
        ),
        check_vma=False,
    )
```

```python
import jax
import jax.numpy as jnp
from jax import lax
from jax.experimental import pallas as pl
from jax.experimental.pallas import tpu as pltpu
from jax.sharding import PartitionSpec as P

HEADS = 12
HEAD = 64
PROMPT = 2048
MOSTLEN = 512
HP = 8
TILE = 256

EPSILON = 1e-12
NEGATIVE = -1e30
F32 = jnp.float32
BF16 = jnp.bfloat16


def dot_plain(left_side, right_side):
    return jnp.dot(left_side, right_side, preferred_element_type=F32)


def dot_inner(left_side, right_side):
    return lax.dot_general(
        left_side, right_side, (((0,), (0,)), ((), ())), preferred_element_type=F32
    )


def dot_transposed(left_side, right_side):
    return lax.dot_general(
        left_side, right_side, (((1,), (1,)), ((), ())), preferred_element_type=F32
    )


def norm_forward(values, gain_vec, bias_vec):
    center = values - jnp.mean(values, axis=-1, keepdims=True)
    scaled = lax.rsqrt(jnp.mean(center * center, axis=-1, keepdims=True) + EPSILON)
    normed = center * scaled
    return (normed * gain_vec + bias_vec, normed, scaled)


def norm_backward(upstream, normed, scaled, gain_vec):
    inner_grad = upstream * gain_vec
    result = scaled * (
        inner_grad
        - jnp.mean(inner_grad, axis=-1, keepdims=True)
        - normed * jnp.mean(inner_grad * normed, axis=-1, keepdims=True)
    )
    return (
        result,
        jnp.sum(upstream * normed, axis=0, keepdims=True),
        jnp.sum(upstream, axis=0, keepdims=True),
    )


def vmem_specs(count):
    return [pl.BlockSpec(memory_space=pltpu.VMEM) for unused in range(count)]


SMEM_SPEC = pl.BlockSpec(memory_space=pltpu.SMEM)
PARAMS = pltpu.CompilerParams(vmem_limit_bytes=56 << 20)


def whole_weight(at_ref, mine_ref, other_ref, weight_ref):
    half = mine_ref.shape[0]

    @pl.when(pl.program_id(0) == 0)
    def _():
        weight_ref[pl.ds(pl.multiple_of(at_ref[0] * half, half), half), :] = mine_ref[...]
        weight_ref[pl.ds(pl.multiple_of((1 - at_ref[0]) * half, half), half), :] = other_ref[...]


def project_kernel(at_ref, low_ref, mine_ref, other_ref, add_ref, out_ref, weight_ref):
    whole_weight(at_ref, mine_ref, other_ref, weight_ref)
    step, rows, model = low_ref.shape
    low = low_ref[...].reshape(step * rows, model)
    total = dot_plain(low, weight_ref[...]) + add_ref[...]
    out_ref[...] = total.astype(BF16).reshape(step, rows, total.shape[1])


def project(at, low, mine, other, add):
    sources, rows, model = low.shape
    half, width = mine.shape
    whole = lambda i, *unused: (0, 0)
    each = lambda i, *unused: (i, 0, 0)
    return pl.pallas_call(
        project_kernel,
        grid_spec=pltpu.PrefetchScalarGridSpec(
            num_scalar_prefetch=1,
            grid=(sources // 2,),
            in_specs=[
                pl.BlockSpec((2, rows, model), each),
                pl.BlockSpec((half, width), whole),
                pl.BlockSpec((half, width), whole),
                pl.BlockSpec((1, width), whole),
            ],
            out_specs=pl.BlockSpec((2, rows, width), each),
            scratch_shapes=[pltpu.VMEM((2 * half, width), BF16)],
        ),
        out_shape=jax.ShapeDtypeStruct((sources, rows, width), BF16),
        compiler_params=PARAMS,
        name="project",
    )(at, low, mine, other, add)


def unproject_kernel(
    at_ref,
    halo_ref,
    low_ref,
    packed_ref,
    extra_ref,
    extra_halo_ref,
    mine_ref,
    other_ref,
    back_ref,
    keep_ref,
    send_ref,
    cols_ref,
    weight_ref,
    acc_ref,
):
    whole_weight(at_ref, mine_ref, other_ref, weight_ref)
    step = pl.program_id(0)
    sources, halves, stripe, width = packed_ref.shape
    part = extra_ref.shape[2]
    half, unused = mine_ref.shape
    pieces = []
    for source in range(sources):
        first = packed_ref[source, 0].astype(F32)
        second = packed_ref[source, 1].astype(F32)
        added = extra_halo_ref[source].astype(F32)
        added = jnp.where(step * sources + source < halo_ref[0], added, 0.0)
        first = jnp.concatenate([first[:, :part] + extra_ref[source].astype(F32), first[:, part:]], 1)
        second = jnp.concatenate([second[:, :part] + added, second[:, part:]], 1)
        pieces = pieces + [first, second]
    grads = jnp.concatenate(pieces, axis=0).astype(BF16)
    low = low_ref[...].reshape(grads.shape[0], low_ref.shape[2])
    back = dot_transposed(grads, weight_ref[...]).astype(BF16)
    back_ref[...] = back.reshape(back_ref.shape)
    share = dot_inner(low, grads)
    columns = jnp.sum(grads.astype(F32), axis=0, keepdims=True)

    @pl.when(step == 0)
    def _():
        acc_ref[...] = share
        cols_ref[...] = columns

    @pl.when(step > 0)
    def _():
        acc_ref[...] += share
        cols_ref[...] += columns

    @pl.when(step == pl.num_programs(0) - 1)
    def _():
        own = pl.ds(pl.multiple_of(at_ref[0] * half, half), half)
        rest = pl.ds(pl.multiple_of((1 - at_ref[0]) * half, half), half)
        keep_ref[...] = acc_ref[own, :].astype(BF16)
        send_ref[...] = acc_ref[rest, :].astype(BF16)


def unproject(at, halo_count, low, packed, extra, extra_halo, mine, other):
    sources, rows, model = low.shape
    stripe = packed.shape[2]
    half, width = mine.shape
    part = extra.shape[2]
    halo_steps = extra_halo.shape[0] // 2
    whole = lambda i, *unused: (0, 0)
    each = lambda i, *unused: (i, 0, 0)
    return pl.pallas_call(
        unproject_kernel,
        grid_spec=pltpu.PrefetchScalarGridSpec(
            num_scalar_prefetch=2,
            grid=(sources // 2,),
            in_specs=[
                pl.BlockSpec((2, rows, model), each),
                pl.BlockSpec((2, 2, stripe, width), lambda i, *unused: (i, 0, 0, 0)),
                pl.BlockSpec((2, stripe, part), each),
                pl.BlockSpec(
                    (2, stripe, part),
                    lambda i, *unused: (jnp.minimum(i, halo_steps - 1), 0, 0),
                ),
                pl.BlockSpec((half, width), whole),
                pl.BlockSpec((half, width), whole),
            ],
            out_specs=[
                pl.BlockSpec((2, rows, model), each),
                pl.BlockSpec((half, width), whole),
                pl.BlockSpec((half, width), whole),
                pl.BlockSpec((1, width), whole),
            ],
            scratch_shapes=[
                pltpu.VMEM((2 * half, width), BF16),
                pltpu.VMEM((2 * half, width), F32),
            ],
        ),
        out_shape=[
            jax.ShapeDtypeStruct((sources, rows, model), BF16),
            jax.ShapeDtypeStruct((half, width), BF16),
            jax.ShapeDtypeStruct((half, width), BF16),
            jax.ShapeDtypeStruct((1, width), F32),
        ],
        compiler_params=PARAMS,
        name="unproject",
    )(at, halo_count, low, packed, extra, extra_halo, mine, other)


def feed_kernel(
    at_ref,
    x_ref,
    ups_ref,
    mixed_ref,
    out_w_ref,
    out_b_ref,
    gain_ref,
    bias_ref,
    back_b_ref,
    in_w_ref,
    in_b_ref,
    back_w_ref,
    out_ref,
    dmid_ref,
    dmixed_ref,
    din_keep_ref,
    din_send_ref,
    dback_ref,
    dout_keep_ref,
    dout_send_ref,
    din_b_ref,
    vectors_ref,
    attended_ref,
    middle_ref,
    low_ref,
    acc_ref,
    grad_acc_ref,
    square_ref,
):
    step = pl.program_id(0)
    sources, rows, width = mixed_ref.shape
    count, model = x_ref.shape
    half = model // 2
    groups = count // rows
    triples = sources // groups
    own = pl.ds(pl.multiple_of(at_ref[0] * half, half), half)
    rest = pl.ds(pl.multiple_of((1 - at_ref[0]) * half, half), half)

    @pl.when(step == 0)
    def _():
        for group in range(groups):
            attended_ref[group * rows : (group + 1) * rows, :] = jnp.concatenate(
                [mixed_ref[triple * groups + group] for triple in range(triples)], axis=1
            )
        middle = x_ref[...].astype(F32) + dot_plain(attended_ref[...], out_w_ref[...])
        middle = middle + out_b_ref[...]
        middle_ref[...] = middle
        low_ref[...] = norm_forward(middle, gain_ref[...], bias_ref[...])[0].astype(BF16)

    hidden_pre = dot_plain(low_ref[...], in_w_ref[...]) + in_b_ref[...]
    grad_hidden = dot_transposed(ups_ref[...], back_w_ref[...])
    below = 0.5 * (1.0 + lax.erf(hidden_pre * 0.5**0.5))
    hidden = (hidden_pre * below).astype(BF16)
    density = jnp.exp(-0.5 * hidden_pre * hidden_pre) * 0.3989422804014327
    grad_pre_wide = grad_hidden * (below + hidden_pre * density)
    grad_pre = grad_pre_wide.astype(BF16)
    din_b_ref[0] = jnp.sum(grad_pre.astype(F32), axis=0, keepdims=True)
    share = dot_plain(hidden, back_w_ref[...])
    grad_share = dot_transposed(grad_pre, in_w_ref[...])
    dback_ref[0] = dot_inner(hidden, ups_ref[...]).astype(BF16)
    square_ref[...] = dot_inner(low_ref[...], grad_pre).astype(BF16)
    din_keep_ref[0] = square_ref[own, :]
    din_send_ref[0] = square_ref[rest, :]

    @pl.when(step == 0)
    def _():
        acc_ref[...] = share
        grad_acc_ref[...] = grad_share

    @pl.when(step > 0)
    def _():
        acc_ref[...] += share
        grad_acc_ref[...] += grad_share

    @pl.when(step == pl.num_programs(0) - 1)
    def _():
        middle = middle_ref[...]
        out_ref[...] = (middle + acc_ref[...] + back_b_ref[...]).astype(BF16)
        upstream = ups_ref[...].astype(F32)
        unused, normed, scaled = norm_forward(middle, 1.0, 0.0)
        change, dgain, dbias = norm_backward(grad_acc_ref[...], normed, scaled, gain_ref[...])
        dmid = upstream + change
        dmid_ref[...] = dmid
        branch = dmid.astype(BF16)
        square_ref[...] = dot_inner(attended_ref[...], branch).astype(BF16)
        dout_keep_ref[...] = square_ref[own, :]
        dout_send_ref[...] = square_ref[rest, :]
        vectors_ref[0:1, :] = jnp.sum(branch.astype(F32), axis=0, keepdims=True)
        vectors_ref[1:2, :] = dgain
        vectors_ref[2:3, :] = dbias
        vectors_ref[3:4, :] = jnp.sum(upstream, axis=0, keepdims=True)
        dattended = dot_transposed(branch, out_w_ref[...]).astype(BF16)
        for group in range(groups):
            for triple in range(triples):
                dmixed_ref[triple * groups + group] = dattended[
                    group * rows : (group + 1) * rows, triple * width : (triple + 1) * width
                ]


def feed(at, rows_in, ups, mixed, out_w, out_b, gain, bias, back_b, in_w, in_b, back_w):
    count, model = rows_in.shape
    hidden = in_w.shape[1]
    blocks = hidden // model
    half = model // 2
    whole = lambda i, *unused: (0, 0)
    whole_three = lambda i, *unused: (0, 0, 0)

    def block_at(i, at_ref):
        return (i + at_ref[0] * (blocks // 2)) % blocks

    full = pl.BlockSpec((count, model), whole)
    vector = pl.BlockSpec((1, model), whole)
    return pl.pallas_call(
        feed_kernel,
        grid_spec=pltpu.PrefetchScalarGridSpec(
            num_scalar_prefetch=1,
            grid=(blocks,),
            in_specs=[
                full,
                full,
                pl.BlockSpec(mixed.shape, whole_three),
                pl.BlockSpec((model, model), whole),
                vector,
                vector,
                vector,
                vector,
                pl.BlockSpec((model, model), lambda i, at_ref: (0, block_at(i, at_ref))),
                pl.BlockSpec((1, model), lambda i, at_ref: (0, block_at(i, at_ref))),
                pl.BlockSpec((model, model), lambda i, at_ref: (block_at(i, at_ref), 0)),
            ],
            out_specs=[
                full,
                full,
                pl.BlockSpec(mixed.shape, whole_three),
                pl.BlockSpec((1, half, model), lambda i, at_ref: (block_at(i, at_ref), 0, 0)),
                pl.BlockSpec((1, half, model), lambda i, at_ref: (block_at(i, at_ref), 0, 0)),
                pl.BlockSpec((1, model, model), lambda i, *unused: (i, 0, 0)),
                pl.BlockSpec((half, model), whole),
                pl.BlockSpec((half, model), whole),
                pl.BlockSpec((1, 1, model), lambda i, at_ref: (block_at(i, at_ref), 0, 0)),
                pl.BlockSpec((4, model), whole),
            ],
            scratch_shapes=[
                pltpu.VMEM((count, model), BF16),
                pltpu.VMEM((count, model), F32),
                pltpu.VMEM((count, model), BF16),
                pltpu.VMEM((count, model), F32),
                pltpu.VMEM((count, model), F32),
                pltpu.VMEM((model, model), BF16),
            ],
        ),
        out_shape=[
            jax.ShapeDtypeStruct((count, model), BF16),
            jax.ShapeDtypeStruct((count, model), F32),
            jax.ShapeDtypeStruct(mixed.shape, BF16),
            jax.ShapeDtypeStruct((blocks, half, model), BF16),
            jax.ShapeDtypeStruct((blocks, half, model), BF16),
            jax.ShapeDtypeStruct((blocks, model, model), BF16),
            jax.ShapeDtypeStruct((half, model), BF16),
            jax.ShapeDtypeStruct((half, model), BF16),
            jax.ShapeDtypeStruct((blocks, 1, model), F32),
            jax.ShapeDtypeStruct((4, model), F32),
        ],
        compiler_params=PARAMS,
        name="feed",
    )(at, rows_in, ups, mixed, out_w, out_b, gain, bias, back_b, in_w, in_b, back_w)


def head_columns(block, kind, head, heads):
    at = (kind * heads + head) * HEAD
    return block[:, at : at + HEAD]


def sorted_rows(stripe, source, half, span):
    return source * stripe if half == 0 else span + (HP - 1 - source) * stripe


def load_queries(packed_ref, target_ref, heads, kind, scaled):
    stripe = packed_ref.shape[2]
    span = HP * stripe
    for source in range(HP):
        for half in range(2):
            at = sorted_rows(stripe, source, half, span)
            block = packed_ref[source, half]
            for head in range(heads):
                part = head_columns(block, kind, head, heads)
                if scaled:
                    part = part * jnp.asarray(HEAD**-0.5, BF16)
                target_ref[head, at : at + stripe, :] = part


def load_keys(rows_of, total, stripe, heads, keys_ref, values_ref, turned_ref, turned_kind):
    for block_at in range(total // stripe):
        block = rows_of(block_at)
        at = block_at * stripe
        for head in range(heads):
            keys_ref[head, at : at + stripe, :] = head_columns(block, 0, head, heads)
            values_ref[head, at : at + stripe, :] = head_columns(block, 1, head, heads)
    source_ref = keys_ref if turned_kind == 0 else values_ref
    for chunk in range(total // TILE):
        for head in range(heads):
            turned_ref[head, chunk] = source_ref[
                head, chunk * TILE : (chunk + 1) * TILE, :
            ].T


def local_rows(packed_ref):
    stripe = packed_ref.shape[2]

    def rows_of(block_at):
        if block_at < HP:
            return packed_ref[block_at, 0]
        return packed_ref[2 * HP - 1 - block_at, 1]

    return rows_of


def remote_rows(prompts_ref, halo_ref):
    parts = prompts_ref.shape[0]
    halo_blocks = halo_ref.shape[0]

    def rows_of(block_at):
        if block_at < parts * HP:
            return prompts_ref[block_at // HP, block_at % HP]
        return halo_ref[halo_blocks - 1 - (block_at - parts * HP)]

    return rows_of


def row_slice(index, size=TILE):
    return pl.ds(pl.multiple_of(index * size, size), size)


def tile_iotas():
    return (
        lax.broadcasted_iota(jnp.int32, (TILE, TILE), 0),
        lax.broadcasted_iota(jnp.int32, (TILE, TILE), 1),
    )


def forward_step(query_tile, chunk, subs, mask, refs, heads):
    queries_ref, keys_ref, turned_ref, top_ref, sum_ref, acc_ref = refs
    for head in range(heads):
        query = queries_ref[head, row_slice(query_tile), :]
        scores = []
        for sub in range(subs):
            part = dot_transposed(keys_ref[head, row_slice(chunk + sub), :], query)
            if mask is not None:
                part = jnp.where(mask, part, NEGATIVE)
            scores.append(part)
        old = top_ref[query_tile, head]
        new = old
        for part in scores:
            new = jnp.maximum(new, jnp.max(part, axis=0, keepdims=True))
        alpha = jnp.exp(old - new)
        total = sum_ref[query_tile, head] * alpha
        acc = acc_ref[query_tile, head] * alpha
        for sub, part in enumerate(scores):
            soft = jnp.exp(part - new)
            total = total + jnp.sum(soft, axis=0, keepdims=True)
            acc = acc + dot_plain(turned_ref[head, chunk + sub], soft.astype(BF16))
        top_ref[query_tile, head] = new
        sum_ref[query_tile, head] = total
        acc_ref[query_tile, head] = acc


def loop(first, last, step):
    def run(index, unused):
        step(index)
        return unused

    lax.fori_loop(first, last, run, 0)


def walk_local(tiles, scalars_ref, starts_ref, step):
    wide = 2 if tiles % 2 == 0 else 1

    def prompt_tile(tile):
        loop(0, tile, lambda chunk: step(tile, chunk, 1, None))
        down, across = tile_iotas()
        step(tile, tile, 1, down <= across)

    def cont_tile(tile):
        query_tile = tiles + tile
        loop(0, tiles // wide, lambda chunk: step(query_tile, chunk * wide, wide, None))

        def band(chunk):
            down, across = tile_iotas()
            shifted = down + (chunk - tile) * TILE
            begin = starts_ref[tile] - tile * TILE
            mask = (shifted <= across) & (shifted >= begin)
            step(query_tile, tiles + chunk, 1, mask)

        loop(scalars_ref[tile], tile + 1, band)

    loop(0, tiles, prompt_tile)
    loop(0, tiles, cont_tile)


def walk_remote(tiles, parts, halo_tiles, scalars_ref, starts_ref, step, done):
    wide = 2 if tiles % 2 == 0 else 1

    def whole(query_tile, part):
        loop(
            0,
            tiles // wide,
            lambda chunk: step(query_tile, part * tiles + chunk * wide, wide, None),
        )

    def prompt_tile(tile):
        for part in range(parts):

            @pl.when(scalars_ref[2 * tiles + part] > 0)
            def _():
                whole(tile, part)

        done(tile, False)

    def cont_tile(tile):
        query_tile = tiles + tile
        for part in range(parts):
            whole(query_tile, part)

        def band(chunk):
            down, unused = tile_iotas()
            shifted = down + (chunk - halo_tiles) * TILE
            step(query_tile, parts * tiles + chunk, 1, shifted >= starts_ref[tile])

        loop(scalars_ref[tiles + tile], halo_tiles, band)
        done(query_tile, True)

    loop(0, tiles, prompt_tile)
    loop(0, tiles, cont_tile)


def forward_local_kernel(
    scalars_ref,
    starts_ref,
    packed_ref,
    top_ref,
    sum_ref,
    acc_ref,
    queries_ref,
    keys_ref,
    values_ref,
    turned_ref,
):
    heads = queries_ref.shape[0]
    stripe = packed_ref.shape[2]
    span = HP * stripe
    load_queries(packed_ref, queries_ref, heads, 2, True)
    load_keys(
        local_rows(packed_ref), 2 * span, stripe, heads, keys_ref, values_ref, turned_ref, 1
    )
    top_ref[...] = jnp.full(top_ref.shape, NEGATIVE, F32)
    sum_ref[...] = jnp.zeros(sum_ref.shape, F32)
    acc_ref[...] = jnp.zeros(acc_ref.shape, F32)
    refs = (queries_ref, keys_ref, turned_ref, top_ref, sum_ref, acc_ref)
    walk_local(
        span // TILE,
        scalars_ref,
        starts_ref,
        lambda tile, chunk, subs, mask: forward_step(tile, chunk, subs, mask, refs, heads),
    )


def store_rows(out_ref, block, query_tile, continued, columns):
    stripe = out_ref.shape[2]
    per = TILE // stripe
    tiles = HP // per
    for piece in range(per):
        rows = block[piece * stripe : (piece + 1) * stripe, :]
        if continued:
            source = HP - 1 - ((query_tile - tiles) * per + piece)
            out_ref[source, 1, :, columns] = rows
        else:
            out_ref[query_tile * per + piece, 0, :, columns] = rows


def forward_remote_kernel(
    scalars_ref,
    starts_ref,
    packed_ref,
    prompts_ref,
    halo_ref,
    top_in_ref,
    sum_in_ref,
    acc_in_ref,
    out_ref,
    log_ref,
    mixed_ref,
    queries_ref,
    keys_ref,
    values_ref,
    turned_ref,
    top_ref,
    sum_ref,
    acc_ref,
):
    heads = queries_ref.shape[0]
    stripe = packed_ref.shape[2]
    span = HP * stripe
    parts = prompts_ref.shape[0]
    halo = halo_ref.shape[0] * stripe
    load_queries(packed_ref, queries_ref, heads, 2, True)
    load_keys(
        remote_rows(prompts_ref, halo_ref),
        parts * span + halo,
        stripe,
        heads,
        keys_ref,
        values_ref,
        turned_ref,
        1,
    )
    top_ref[...] = top_in_ref[...]
    sum_ref[...] = sum_in_ref[...]
    acc_ref[...] = acc_in_ref[...]
    refs = (queries_ref, keys_ref, turned_ref, top_ref, sum_ref, acc_ref)

    def done(query_tile, continued):
        mixed = []
        for head in range(heads):
            total = sum_ref[query_tile, head]
            part = acc_ref[query_tile, head] / total
            log_ref[query_tile, head] = top_ref[query_tile, head] + jnp.log(total)
            mixed_ref[query_tile, head] = part
            mixed.append(part)
        block = jnp.concatenate(mixed, axis=0).T.astype(BF16)
        store_rows(out_ref, block, query_tile, continued, slice(None))

    walk_remote(
        span // TILE,
        parts,
        halo // TILE,
        scalars_ref,
        starts_ref,
        lambda tile, chunk, subs, mask: forward_step(tile, chunk, subs, mask, refs, heads),
        done,
    )


def forward_local(scalars, starts, packed, heads):
    stripe = packed.shape[2]
    span = HP * stripe
    tiles = 2 * span // TILE
    return pl.pallas_call(
        forward_local_kernel,
        in_specs=[SMEM_SPEC] + vmem_specs(2),
        out_specs=vmem_specs(3),
        out_shape=[
            jax.ShapeDtypeStruct((tiles, heads, 1, TILE), F32),
            jax.ShapeDtypeStruct((tiles, heads, 1, TILE), F32),
            jax.ShapeDtypeStruct((tiles, heads, HEAD, TILE), F32),
        ],
        scratch_shapes=[
            pltpu.VMEM((heads, 2 * span, HEAD), BF16),
            pltpu.VMEM((heads, 2 * span, HEAD), BF16),
            pltpu.VMEM((heads, 2 * span, HEAD), BF16),
            pltpu.VMEM((heads, tiles, HEAD, TILE), BF16),
        ],
        compiler_params=PARAMS,
        name="forward_local",
    )(scalars, starts, packed)


def forward_remote(scalars, starts, packed, prompts, halo, state, heads):
    stripe = packed.shape[2]
    span = HP * stripe
    tiles = 2 * span // TILE
    rows = prompts.shape[0] * span + halo.shape[0] * stripe
    return pl.pallas_call(
        forward_remote_kernel,
        in_specs=[SMEM_SPEC] + vmem_specs(7),
        out_specs=vmem_specs(3),
        out_shape=[
            jax.ShapeDtypeStruct((HP, 2, stripe, heads * HEAD), BF16),
            jax.ShapeDtypeStruct((tiles, heads, 1, TILE), F32),
            jax.ShapeDtypeStruct((tiles, heads, HEAD, TILE), F32),
        ],
        scratch_shapes=[
            pltpu.VMEM((heads, 2 * span, HEAD), BF16),
            pltpu.VMEM((heads, rows, HEAD), BF16),
            pltpu.VMEM((heads, rows, HEAD), BF16),
            pltpu.VMEM((heads, rows // TILE, HEAD, TILE), BF16),
            pltpu.VMEM((tiles, heads, 1, TILE), F32),
            pltpu.VMEM((tiles, heads, 1, TILE), F32),
            pltpu.VMEM((tiles, heads, HEAD, TILE), F32),
        ],
        compiler_params=PARAMS,
        name="forward_remote",
    )(scalars, starts, packed, prompts, halo, *state)


def backward_step(query_tile, chunk, subs, mask, refs, heads):
    (
        queries_ref,
        ups_ref,
        keys_ref,
        values_ref,
        turned_ref,
        log_ref,
        delta_ref,
        dquery_ref,
        dkeys_ref,
        dvalues_ref,
    ) = refs
    for head in range(heads):
        query = queries_ref[head, row_slice(query_tile), :]
        ups = ups_ref[head, row_slice(query_tile), :]
        logsum = log_ref[query_tile, head]
        delta = delta_ref[query_tile, head]
        dquery = dquery_ref[query_tile, head]
        for sub in range(subs):
            rows = row_slice(chunk + sub)
            scores = dot_transposed(keys_ref[head, rows, :], query)
            grad_soft = dot_transposed(values_ref[head, rows, :], ups)
            soft = jnp.exp(scores - logsum)
            if mask is not None:
                soft = jnp.where(mask, soft, 0.0)
            grad_scores = (soft * (grad_soft - delta)).astype(BF16)
            dvalues_ref[head, rows, :] += dot_plain(soft.astype(BF16), ups)
            dkeys_ref[head, rows, :] += dot_plain(grad_scores, query)
            dquery = dquery + dot_plain(turned_ref[head, chunk + sub], grad_scores)
        dquery_ref[query_tile, head] = dquery


def key_grad_rows(dkeys_ref, dvalues_ref, at, stripe, heads):
    pieces = [dkeys_ref[head, at : at + stripe, :] for head in range(heads)]
    pieces = pieces + [dvalues_ref[head, at : at + stripe, :] for head in range(heads)]
    return jnp.concatenate(pieces, axis=1).astype(BF16)


def backward_remote_kernel(
    scalars_ref,
    starts_ref,
    packed_ref,
    ups_in_ref,
    prompts_ref,
    halo_ref,
    log_ref,
    mixed_ref,
    dprompts_ref,
    dhalo_ref,
    dquery_ref,
    delta_ref,
    queries_ref,
    ups_ref,
    keys_ref,
    values_ref,
    turned_ref,
    dkeys_ref,
    dvalues_ref,
):
    heads = queries_ref.shape[0]
    stripe = packed_ref.shape[2]
    span = HP * stripe
    parts = prompts_ref.shape[0]
    halo_blocks = halo_ref.shape[0]
    halo = halo_blocks * stripe
    load_queries(packed_ref, queries_ref, heads, 2, True)
    load_queries(ups_in_ref, ups_ref, heads, 0, False)
    load_keys(
        remote_rows(prompts_ref, halo_ref),
        parts * span + halo,
        stripe,
        heads,
        keys_ref,
        values_ref,
        turned_ref,
        0,
    )
    for query_tile in range(2 * span // TILE):
        for head in range(heads):
            ups = ups_ref[head, query_tile * TILE : (query_tile + 1) * TILE, :]
            delta_ref[query_tile, head] = jnp.sum(
                ups.T.astype(F32) * mixed_ref[query_tile, head], axis=0, keepdims=True
            )
    dquery_ref[...] = jnp.zeros(dquery_ref.shape, F32)
    dkeys_ref[...] = jnp.zeros(dkeys_ref.shape, F32)
    dvalues_ref[...] = jnp.zeros(dvalues_ref.shape, F32)
    refs = (
        queries_ref,
        ups_ref,
        keys_ref,
        values_ref,
        turned_ref,
        log_ref,
        delta_ref,
        dquery_ref,
        dkeys_ref,
        dvalues_ref,
    )
    walk_remote(
        span // TILE,
        parts,
        halo // TILE,
        scalars_ref,
        starts_ref,
        lambda tile, chunk, subs, mask: backward_step(tile, chunk, subs, mask, refs, heads),
        lambda tile, continued: None,
    )
    for block_at in range(parts * HP):
        dprompts_ref[block_at // HP, block_at % HP] = key_grad_rows(
            dkeys_ref, dvalues_ref, block_at * stripe, stripe, heads
        )
    for block_at in range(halo_blocks):
        dhalo_ref[halo_blocks - 1 - block_at] = key_grad_rows(
            dkeys_ref, dvalues_ref, parts * span + block_at * stripe, stripe, heads
        )


def backward_local_kernel(
    scalars_ref,
    starts_ref,
    packed_ref,
    ups_in_ref,
    log_ref,
    delta_ref,
    dquery_in_ref,
    out_ref,
    queries_ref,
    ups_ref,
    keys_ref,
    values_ref,
    turned_ref,
    dquery_ref,
    dkeys_ref,
    dvalues_ref,
):
    heads = queries_ref.shape[0]
    stripe = packed_ref.shape[2]
    span = HP * stripe
    width = heads * HEAD
    load_queries(packed_ref, queries_ref, heads, 2, True)
    load_queries(ups_in_ref, ups_ref, heads, 0, False)
    load_keys(
        local_rows(packed_ref), 2 * span, stripe, heads, keys_ref, values_ref, turned_ref, 0
    )
    dquery_ref[...] = dquery_in_ref[...]
    dkeys_ref[...] = jnp.zeros(dkeys_ref.shape, F32)
    dvalues_ref[...] = jnp.zeros(dvalues_ref.shape, F32)
    refs = (
        queries_ref,
        ups_ref,
        keys_ref,
        values_ref,
        turned_ref,
        log_ref,
        delta_ref,
        dquery_ref,
        dkeys_ref,
        dvalues_ref,
    )
    walk_local(
        span // TILE,
        scalars_ref,
        starts_ref,
        lambda tile, chunk, subs, mask: backward_step(tile, chunk, subs, mask, refs, heads),
    )
    for source in range(HP):
        for half in range(2):
            at = sorted_rows(stripe, source, half, span)
            out_ref[source, half, :, : 2 * width] = key_grad_rows(
                dkeys_ref, dvalues_ref, at, stripe, heads
            )
    pad = out_ref.shape[3] - 3 * width
    for query_tile in range(2 * span // TILE):
        turned = jnp.concatenate([dquery_ref[query_tile, head] for head in range(heads)], axis=0)
        block = (turned * HEAD**-0.5).T
        if pad:
            block = jnp.concatenate([block, jnp.zeros((TILE, pad), F32)], axis=1)
        store_rows(
            out_ref,
            block.astype(BF16),
            query_tile,
            query_tile >= span // TILE,
            slice(2 * width, None),
        )


def backward_remote(scalars, starts, packed, ups, prompts, halo, logsum, mixed, heads):
    stripe = packed.shape[2]
    span = HP * stripe
    tiles = 2 * span // TILE
    rows = prompts.shape[0] * span + halo.shape[0] * stripe
    return pl.pallas_call(
        backward_remote_kernel,
        in_specs=[SMEM_SPEC] + vmem_specs(7),
        out_specs=vmem_specs(4),
        out_shape=[
            jax.ShapeDtypeStruct(prompts.shape, BF16),
            jax.ShapeDtypeStruct(halo.shape, BF16),
            jax.ShapeDtypeStruct((tiles, heads, HEAD, TILE), F32),
            jax.ShapeDtypeStruct((tiles, heads, 1, TILE), F32),
        ],
        scratch_shapes=[
            pltpu.VMEM((heads, 2 * span, HEAD), BF16),
            pltpu.VMEM((heads, 2 * span, HEAD), BF16),
            pltpu.VMEM((heads, rows, HEAD), BF16),
            pltpu.VMEM((heads, rows, HEAD), BF16),
            pltpu.VMEM((heads, rows // TILE, HEAD, TILE), BF16),
            pltpu.VMEM((heads, rows, HEAD), F32),
            pltpu.VMEM((heads, rows, HEAD), F32),
        ],
        compiler_params=PARAMS,
        name="backward_remote",
    )(scalars, starts, packed, ups, prompts, halo, logsum, mixed)


def backward_local(scalars, starts, packed, ups, logsum, delta, dquery, heads):
    stripe = packed.shape[2]
    span = HP * stripe
    tiles = 2 * span // TILE
    rows = 2 * span
    return pl.pallas_call(
        backward_local_kernel,
        in_specs=[SMEM_SPEC] + vmem_specs(6),
        out_specs=vmem_specs(1)[0],
        out_shape=jax.ShapeDtypeStruct(packed.shape, BF16),
        scratch_shapes=[
            pltpu.VMEM((heads, rows, HEAD), BF16),
            pltpu.VMEM((heads, rows, HEAD), BF16),
            pltpu.VMEM((heads, rows, HEAD), BF16),
            pltpu.VMEM((heads, rows, HEAD), BF16),
            pltpu.VMEM((heads, tiles, HEAD, TILE), BF16),
            pltpu.VMEM((tiles, heads, HEAD, TILE), F32),
            pltpu.VMEM((heads, rows, HEAD), F32),
            pltpu.VMEM((heads, rows, HEAD), F32),
        ],
        compiler_params=PARAMS,
        name="backward_local",
    )(scalars, starts, packed, ups, logsum, delta, dquery)


def gather_pair(shard):
    if lax.axis_size("wsh") == 2:
        other = lax.ppermute(shard, "wsh", [(0, 1), (1, 0)])
        return (shard, other)
    whole = lax.all_gather(shard, "wsh", axis=0, tiled=True)
    return tuple(jnp.split(whole, 2, axis=0))


def scatter_rows(keep, send, axis):
    if lax.axis_size("wsh") == 2:
        got = lax.ppermute(send, "wsh", [(0, 1), (1, 0)])
        return (keep.astype(F32) + got.astype(F32)).astype(BF16)
    whole = jnp.concatenate([keep, send], axis=axis)
    return lax.psum_scatter(whole, "wsh", scatter_dimension=axis, tiled=True)


def traded(value, bit):
    ways = lax.axis_size("ctx")
    return lax.ppermute(value, "ctx", [(i, i ^ (1 << bit)) for i in range(ways)])


def reduce_gather(value, sum_bits, gather_bits, pieces):
    index = lax.axis_index("ctx")
    rows, width = value.shape
    size = rows // pieces
    parts = [value[at * size : (at + 1) * size] for at in range(pieces)]
    for bit in sum_bits:
        flag = (index >> bit) & 1
        for at in range(pieces):
            count = parts[at].shape[0] // 2
            keep = lax.dynamic_slice_in_dim(parts[at], flag * count, count, 0)
            send = lax.dynamic_slice_in_dim(parts[at], (1 - flag) * count, count, 0)
            got = traded(send, bit)
            parts[at] = (keep.astype(F32) + got.astype(F32)).astype(BF16)
    near = [bit for bit in sum_bits if bit < 3] + list(gather_bits)
    far = [bit for bit in sum_bits if bit >= 3]
    orders = [far + near[at % len(near) :] + near[: at % len(near)] for at in range(pieces)]
    parts = [part[None] for part in parts]
    for step in range(len(orders[0])):
        for at in range(pieces):
            flag = (index >> orders[at][step]) & 1
            mine = parts[at]
            got = traded(mine, orders[at][step])
            parts[at] = jnp.where(
                flag == 0,
                jnp.concatenate([mine, got], axis=0),
                jnp.concatenate([got, mine], axis=0),
            )
    wanted = sorted(gather_bits, reverse=True) + list(sum_bits)
    done = []
    for at in range(pieces):
        held = list(reversed(orders[at]))
        count = parts[at].shape[1]
        split = parts[at].reshape((2,) * len(held) + (count, width))
        split = split.transpose([held.index(bit) for bit in wanted] + [len(held), len(held) + 1])
        done.append(split.reshape(1 << len(gather_bits), size, width))
    return jnp.concatenate(done, axis=1)


def scatter_step(parts, orders, step):
    index = lax.axis_index("ctx")
    done = []
    for part, order in zip(parts, orders):
        flag = (index >> order[step]) & 1
        count = part.shape[0] // 2
        keep = lax.dynamic_slice_in_dim(part, flag * count, count, 0)
        send = lax.dynamic_slice_in_dim(part, (1 - flag) * count, count, 0)
        got = traded(send, order[step])
        done.append((keep.astype(F32) + got.astype(F32)).astype(BF16))
    return done


def gather_step(parts, orders, step):
    index = lax.axis_index("ctx")
    done = []
    for part, order in zip(parts, orders):
        flag = (index >> order[step]) & 1
        got = traded(part, order[step])
        first = jnp.where(flag == 0, part, got)
        second = jnp.where(flag == 0, got, part)
        done.append(jnp.concatenate([first, second], axis=0))
    return done


def small_sum(value):
    ways = lax.axis_size("ctx")
    if lax.axis_size("wsh") == 2:
        value = value + lax.ppermute(value, "wsh", [(0, 1), (1, 0)])
    else:
        value = lax.psum(value, "wsh")
    for bit in range(ways.bit_length() - 1):
        value = value + traded(value, bit)
    return value


def body(
    tokens,
    cont_lengths,
    grad_out,
    ln_gain_one,
    ln_bias_one,
    w_query,
    b_query,
    w_key,
    w_value,
    b_value,
    w_out,
    b_out,
    ln_gain_two,
    ln_bias_two,
    w_in,
    b_in,
    w_back,
    b_back,
):
    groups, rows, model = tokens.shape
    ways = lax.axis_size("ctx")
    shards = lax.axis_size("wsh")
    wsh_at = lax.axis_index("wsh")
    parts = ways // HP
    stripe = rows // 2
    span = HP * stripe
    tiles = span // TILE
    heads = HEADS * groups // HP
    triples = HEADS // heads
    width = heads * HEAD
    packed_width = -(-3 * width // 128) * 128
    pad = packed_width - 3 * width
    count = groups * rows
    hidden_size = w_in.shape[1]
    blocks = hidden_size // model
    shard_rows = model // shards
    my_ctx = lax.axis_index("ctx")
    part_at = my_ctx // HP
    group_at = (my_ctx % HP) % groups
    triple_at = (my_ctx % HP) // groups
    half_at = wsh_at if shards == 2 else jnp.zeros((), jnp.int32)
    at_vector = half_at.astype(jnp.int32).reshape(1)

    small_rows = [ln_gain_one, ln_bias_one, b_query, b_value, b_out, ln_gain_two, ln_bias_two]
    small_rows = small_rows + [b_back, b_in]
    small = jnp.concatenate([row.reshape(-1, shard_rows) for row in small_rows], axis=0)
    if shards == 2:
        got = lax.ppermute(small, "wsh", [(0, 1), (1, 0)])
        small = jnp.where(wsh_at == 0, jnp.stack([small, got]), jnp.stack([got, small]))
    else:
        small = lax.all_gather(small, "wsh", axis=0, tiled=False)
    vectors = [small[:, at].reshape(1, model).astype(F32) for at in range(8)]
    gain_one, bias_one, query_b, value_b, out_b, gain_two, bias_two, back_b = vectors
    in_b = small[:, 8:].reshape(1, hidden_size).astype(F32)
    out_w = lax.all_gather(w_out, "wsh", axis=0, tiled=True)
    in_w = lax.all_gather(w_in, "wsh", axis=0, tiled=True)
    back_w = lax.all_gather(w_back, "wsh", axis=0, tiled=True)

    token_rows = tokens.reshape(count, model)
    inputs = token_rows.astype(F32)
    cube = [[part * HP + at for at in range(HP)] for part in range(parts)]

    def exchange(value):
        return lax.all_to_all(value, "ctx", 0, 0, axis_index_groups=cube)

    low_one = norm_forward(inputs, gain_one, bias_one)[0].astype(BF16)
    low_one = low_one.reshape(1, groups, rows, model)
    low_one = jnp.broadcast_to(low_one, (HP // groups, groups, rows, model))
    low_all = exchange(low_one.reshape(HP, rows, model))

    def own_columns(value):
        return lax.dynamic_slice_in_dim(value, triple_at * width, width, 1)

    stacked = [own_columns(w_key), own_columns(w_value), own_columns(w_query)]
    stacked_b = [jnp.zeros((1, width), F32), own_columns(value_b), own_columns(query_b)]
    if pad:
        stacked.append(jnp.zeros((shard_rows, pad), BF16))
        stacked_b.append(jnp.zeros((1, pad), F32))
    first_w, second_w = gather_pair(jnp.concatenate(stacked, axis=1))
    packed = project(at_vector, low_all, first_w, second_w, jnp.concatenate(stacked_b, axis=1))
    packed = packed.reshape(HP, 2, stripe, packed_width)

    lengths = lax.dynamic_index_in_dim(cont_lengths, group_at, 0, keepdims=False)
    seg_ends = jnp.cumsum(lengths, dtype=jnp.int32)
    chunk_start = (parts - 1 - part_at) * span
    places = chunk_start + jnp.arange(span, dtype=jnp.int32)
    begins = jnp.max(
        jnp.where(seg_ends[None, :] <= places[:, None], seg_ends[None, :], 0), axis=1
    )
    starts = (begins - chunk_start).reshape(tiles, 1, TILE)
    halo_rows = min(MOSTLEN, span)
    halo_tiles = halo_rows // TILE
    halo_blocks = halo_rows // stripe
    first_start = starts[:, 0, 0]
    local_first = jnp.maximum(first_start, 0) // TILE
    has_halo = part_at < parts - 1
    halo_first = jnp.where(
        has_halo, jnp.clip(first_start + halo_rows, 0, halo_rows) // TILE, halo_tiles
    )
    seen = [(part_at >= shift).astype(jnp.int32).reshape(1) for shift in range(1, parts)]
    scalars = jnp.concatenate([local_first, halo_first] + seen).astype(jnp.int32)

    def shifted(value, shift):
        pairs = [
            (part * HP + at, ((part + shift) % parts) * HP + at)
            for part in range(parts)
            for at in range(HP)
        ]
        return lax.ppermute(value, "ctx", pairs)

    def to_former(value):
        pairs = [(i, i - HP) for i in range(HP, ways)]
        return lax.ppermute(value, "ctx", pairs)

    def to_latter(value):
        pairs = [(i, i + HP) for i in range(ways - HP)]
        return lax.ppermute(value, "ctx", pairs)

    own_prompts = packed[:, 0, :, : 2 * width]
    prompts = jnp.stack([shifted(own_prompts, shift) for shift in range(1, parts)])
    halo = to_former(packed[:halo_blocks, 1, :, : 2 * width])
    state = forward_local(scalars, starts, packed, heads)
    mixed_rows, logsum, mixed = forward_remote(
        scalars, starts, packed, prompts, halo, state, heads
    )
    attended = exchange(mixed_rows.reshape(HP, rows, width))

    (
        out_rows,
        grad_middle,
        dattended,
        din_keep,
        din_send,
        dback,
        dout_keep,
        dout_send,
        din_b,
        mid_vectors,
    ) = feed(
        at_vector,
        token_rows,
        grad_out.reshape(count, model),
        attended,
        out_w,
        out_b,
        gain_two,
        bias_two,
        back_b,
        in_w,
        in_b,
        back_w,
    )
    ups = exchange(dattended).reshape(HP, 2, stripe, width)
    in_sum = scatter_rows(din_keep, din_send, 1)
    back_sum = scatter_rows(
        dback[: blocks // 2].reshape(-1, model), dback[blocks // 2 :].reshape(-1, model), 0
    )
    out_sum = scatter_rows(dout_keep, dout_send, 0)
    sums = [in_sum.reshape(-1, model), back_sum, out_sum]
    bits = ways.bit_length() - 1
    rest = tuple(range(3, bits))
    orders = [(0, 1, 2) + rest, (1, 0, 2) + rest, (2, 0, 1) + rest]
    *sums, ups = lax.optimization_barrier((*sums, ups))
    sums = scatter_step(sums, orders, 0)

    dprompts, dhalo, dquery, delta = backward_remote(
        scalars, starts, packed, ups, prompts, halo, logsum, mixed, heads
    )
    *sums, dprompts, dhalo, dquery = lax.optimization_barrier((*sums, dprompts, dhalo, dquery))
    sums = scatter_step(sums, orders, 1)
    returned = [shifted(dprompts[shift - 1], parts - shift) for shift in range(1, parts)]
    if parts > 2:
        returned = [sum(piece.astype(F32) for piece in returned).astype(BF16)]
    returned_halo = to_latter(dhalo)
    dpacked = backward_local(scalars, starts, packed, ups, logsum, delta, dquery, heads)
    *sums, dpacked = lax.optimization_barrier((*sums, dpacked))
    sums = scatter_step(sums, orders, 2)
    halo_count = jnp.full((1,), halo_blocks, jnp.int32)
    dlow, keep, send, columns = unproject(
        at_vector, halo_count, low_all, dpacked, returned[0], returned_halo, first_w, second_w
    )

    *sums, dlow = lax.optimization_barrier((*sums, dlow))
    for step in range(3, bits):
        sums = scatter_step(sums, orders, step)
    for step in reversed(range(bits)):
        sums = gather_step(sums, orders, step)
    in_done, back_done, out_done = sums

    group_bits = groups.bit_length() - 1
    sum_bits = list(range(group_bits)) + list(range(3, ways.bit_length() - 1))
    last = reduce_gather(scatter_rows(keep, send, 0), sum_bits, range(group_bits, 3), 3)

    upstream = exchange(dlow).reshape(triples, count, model)
    upstream = jnp.sum(upstream.astype(F32), axis=0)
    unused, hat_one, scale_one = norm_forward(inputs, gain_one, bias_one)
    change, grad_gain_one, grad_bias_one = norm_backward(upstream, hat_one, scale_one, gain_one)
    grad_rows = grad_middle + change
    place = (jnp.arange(triples) == triple_at)[:, None]
    spread = jnp.where(place, columns, 0.0)
    pieces = [mid_vectors, din_b, grad_gain_one, grad_bias_one, spread]
    flat = jnp.concatenate([piece.reshape(-1) for piece in pieces])
    length = flat.shape[0]
    flat = small_sum(flat.reshape(-1, 128)).reshape(-1)

    def own(vector):
        size = vector.shape[0] // shards
        return lax.dynamic_slice_in_dim(vector, wsh_at * size, size, 0)

    new_out_b, new_gain_two, new_bias_two, new_back_b = [
        own(flat[at * model : (at + 1) * model]) for at in range(4)
    ]
    at = 4 * model + hidden_size
    new_in_b = own(flat[4 * model : at])
    new_gain_one = own(flat[at : at + model])
    new_bias_one = own(flat[at + model : at + 2 * model])
    columns = flat[at + 2 * model : length].reshape(triples, packed_width)

    def unvector(kind):
        return own(columns[:, kind * width : (kind + 1) * width].reshape(model))

    def untriple(kind):
        piece = last[:, :, kind * width : (kind + 1) * width]
        return piece.transpose(1, 0, 2).reshape(shard_rows, model).astype(F32)

    new_key_w, new_value_w, new_query_w = [untriple(kind) for kind in range(3)]
    return (
        out_rows.reshape(groups, rows, model),
        grad_rows.reshape(groups, rows, model),
        new_gain_one,
        new_bias_one,
        new_query_w,
        unvector(2),
        new_key_w,
        new_value_w,
        unvector(1),
        out_done.astype(F32),
        new_out_b,
        new_gain_two,
        new_bias_two,
        in_done.reshape(blocks, shard_rows, model).transpose(1, 0, 2).reshape(shard_rows, hidden_size).astype(F32),
        new_in_b,
        back_done.astype(F32),
        new_back_b,
    )


def solution(mesh):
    placed = (
        P("wsh", "ctx", None),
        P("wsh", None),
        P("wsh", "ctx", None),
        P("wsh"),
        P("wsh"),
        P("wsh", None),
        P("wsh"),
        P("wsh", None),
        P("wsh", None),
        P("wsh"),
        P("wsh", None),
        P("wsh"),
        P("wsh"),
        P("wsh"),
        P("wsh", None),
        P("wsh"),
        P("wsh", None),
        P("wsh"),
    )
    return jax.shard_map(
        body,
        mesh=mesh,
        in_specs=placed,
        out_specs=(
            P("wsh", "ctx", None),
            P("wsh", "ctx", None),
            P("wsh"),
            P("wsh"),
            P("wsh", None),
            P("wsh"),
            P("wsh", None),
            P("wsh", None),
            P("wsh"),
            P("wsh", None),
            P("wsh"),
            P("wsh"),
            P("wsh"),
            P("wsh", None),
            P("wsh"),
            P("wsh", None),
            P("wsh"),
        ),
        check_vma=False,
    )
```

```python
import jax
import jax.numpy as jnp
from jax import lax
from jax.experimental import pallas as pl
from jax.experimental.pallas import tpu as pltpu
from jax.sharding import PartitionSpec as P

HEADS = 12
HEAD = 64
PROMPT = 2048
MOSTLEN = 512
HP = 8
TILE = 256

EPSILON = 1e-12
NEGATIVE = -1e30
F32 = jnp.float32
BF16 = jnp.bfloat16


def dot_plain(left_side, right_side):
    return jnp.dot(left_side, right_side, preferred_element_type=F32)


def dot_inner(left_side, right_side):
    return lax.dot_general(
        left_side, right_side, (((0,), (0,)), ((), ())), preferred_element_type=F32
    )


def dot_transposed(left_side, right_side):
    return lax.dot_general(
        left_side, right_side, (((1,), (1,)), ((), ())), preferred_element_type=F32
    )


def norm_forward(values, gain_vec, bias_vec):
    center = values - jnp.mean(values, axis=-1, keepdims=True)
    scaled = lax.rsqrt(jnp.mean(center * center, axis=-1, keepdims=True) + EPSILON)
    normed = center * scaled
    return (normed * gain_vec + bias_vec, normed, scaled)


def norm_backward(upstream, normed, scaled, gain_vec):
    inner_grad = upstream * gain_vec
    result = scaled * (
        inner_grad
        - jnp.mean(inner_grad, axis=-1, keepdims=True)
        - normed * jnp.mean(inner_grad * normed, axis=-1, keepdims=True)
    )
    return (
        result,
        jnp.sum(upstream * normed, axis=0, keepdims=True),
        jnp.sum(upstream, axis=0, keepdims=True),
    )


def vmem_specs(count):
    return [pl.BlockSpec(memory_space=pltpu.VMEM) for unused in range(count)]


SMEM_SPEC = pl.BlockSpec(memory_space=pltpu.SMEM)
PARAMS = pltpu.CompilerParams(vmem_limit_bytes=56 << 20)


def whole_weight(at_ref, mine_ref, other_ref, weight_ref):
    half = mine_ref.shape[0]

    @pl.when(pl.program_id(0) == 0)
    def _():
        weight_ref[pl.ds(pl.multiple_of(at_ref[0] * half, half), half), :] = mine_ref[...]
        weight_ref[pl.ds(pl.multiple_of((1 - at_ref[0]) * half, half), half), :] = other_ref[...]


def project_kernel(at_ref, low_ref, mine_ref, other_ref, add_ref, out_ref, weight_ref):
    whole_weight(at_ref, mine_ref, other_ref, weight_ref)
    step, rows, model = low_ref.shape
    low = low_ref[...].reshape(step * rows, model)
    total = dot_plain(low, weight_ref[...]) + add_ref[...]
    out_ref[...] = total.astype(BF16).reshape(step, rows, total.shape[1])


def project(at, low, mine, other, add):
    sources, rows, model = low.shape
    half, width = mine.shape
    whole = lambda i, *unused: (0, 0)
    each = lambda i, *unused: (i, 0, 0)
    return pl.pallas_call(
        project_kernel,
        grid_spec=pltpu.PrefetchScalarGridSpec(
            num_scalar_prefetch=1,
            grid=(sources // 2,),
            in_specs=[
                pl.BlockSpec((2, rows, model), each),
                pl.BlockSpec((half, width), whole),
                pl.BlockSpec((half, width), whole),
                pl.BlockSpec((1, width), whole),
            ],
            out_specs=pl.BlockSpec((2, rows, width), each),
            scratch_shapes=[pltpu.VMEM((2 * half, width), BF16)],
        ),
        out_shape=jax.ShapeDtypeStruct((sources, rows, width), BF16),
        compiler_params=PARAMS,
        name="project",
    )(at, low, mine, other, add)


def unproject_kernel(
    at_ref,
    halo_ref,
    low_ref,
    packed_ref,
    extra_ref,
    extra_halo_ref,
    mine_ref,
    other_ref,
    back_ref,
    keep_ref,
    send_ref,
    cols_ref,
    gain_ref,
    shift_ref,
    weight_ref,
    acc_ref,
):
    whole_weight(at_ref, mine_ref, other_ref, weight_ref)
    step = pl.program_id(0)
    sources, halves, stripe, width = packed_ref.shape
    part = extra_ref.shape[2]
    half, unused = mine_ref.shape
    pieces = []
    for source in range(sources):
        first = packed_ref[source, 0].astype(F32)
        second = packed_ref[source, 1].astype(F32)
        added = extra_halo_ref[source].astype(F32)
        added = jnp.where(step * sources + source < halo_ref[0], added, 0.0)
        first = jnp.concatenate([first[:, :part] + extra_ref[source].astype(F32), first[:, part:]], 1)
        second = jnp.concatenate([second[:, :part] + added, second[:, part:]], 1)
        pieces = pieces + [first, second]
    grads = jnp.concatenate(pieces, axis=0).astype(BF16)
    low = low_ref[...].reshape(grads.shape[0], low_ref.shape[2])
    back = dot_transposed(grads, weight_ref[...]).astype(BF16)
    back_ref[...] = back.reshape(back_ref.shape)
    share = dot_inner(low, grads)
    columns = jnp.sum(grads.astype(F32), axis=0, keepdims=True)

    @pl.when(step == 0)
    def _():
        acc_ref[...] = share
        cols_ref[...] = columns

    @pl.when(step > 0)
    def _():
        acc_ref[...] += share
        cols_ref[...] += columns

    @pl.when(step == pl.num_programs(0) - 1)
    def _():
        own = pl.ds(pl.multiple_of(at_ref[0] * half, half), half)
        rest = pl.ds(pl.multiple_of((1 - at_ref[0]) * half, half), half)
        weight = weight_ref[...].astype(F32)
        gain_ref[...] = jnp.sum(acc_ref[...] * weight, axis=1, keepdims=True)
        shift_ref[...] = jnp.sum(cols_ref[...] * weight, axis=1, keepdims=True)
        for ref, at in ((keep_ref, own), (send_ref, rest)):
            ref[:, :width] = acc_ref[at, :].astype(BF16)
            ref[:, width:] = jnp.zeros((half, ref.shape[1] - width), BF16)


def unproject(at, halo_count, low, packed, extra, extra_halo, mine, other):
    sources, rows, model = low.shape
    stripe = packed.shape[2]
    half, width = mine.shape
    part = extra.shape[2]
    halo_steps = extra_halo.shape[0] // 2
    whole = lambda i, *unused: (0, 0)
    each = lambda i, *unused: (i, 0, 0)
    return pl.pallas_call(
        unproject_kernel,
        grid_spec=pltpu.PrefetchScalarGridSpec(
            num_scalar_prefetch=2,
            grid=(sources // 2,),
            in_specs=[
                pl.BlockSpec((2, rows, model), each),
                pl.BlockSpec((2, 2, stripe, width), lambda i, *unused: (i, 0, 0, 0)),
                pl.BlockSpec((2, stripe, part), each),
                pl.BlockSpec(
                    (2, stripe, part),
                    lambda i, *unused: (jnp.minimum(i, halo_steps - 1), 0, 0),
                ),
                pl.BlockSpec((half, width), whole),
                pl.BlockSpec((half, width), whole),
            ],
            out_specs=[
                pl.BlockSpec((2, rows, model), each),
                pl.BlockSpec((half, model), whole),
                pl.BlockSpec((half, model), whole),
                pl.BlockSpec((1, width), whole),
                pl.BlockSpec((model, 1), whole),
                pl.BlockSpec((model, 1), whole),
            ],
            scratch_shapes=[
                pltpu.VMEM((2 * half, width), BF16),
                pltpu.VMEM((2 * half, width), F32),
            ],
        ),
        out_shape=[
            jax.ShapeDtypeStruct((sources, rows, model), BF16),
            jax.ShapeDtypeStruct((half, model), BF16),
            jax.ShapeDtypeStruct((half, model), BF16),
            jax.ShapeDtypeStruct((1, width), F32),
            jax.ShapeDtypeStruct((model, 1), F32),
            jax.ShapeDtypeStruct((model, 1), F32),
        ],
        compiler_params=PARAMS,
        name="unproject",
    )(at, halo_count, low, packed, extra, extra_halo, mine, other)


def feed_kernel(
    at_ref,
    x_ref,
    ups_ref,
    mixed_ref,
    out_w_ref,
    out_b_ref,
    gain_ref,
    bias_ref,
    back_b_ref,
    in_w_ref,
    in_b_ref,
    back_w_ref,
    out_ref,
    dmid_ref,
    dmixed_ref,
    din_keep_ref,
    din_send_ref,
    dback_keep_ref,
    dback_send_ref,
    din_b_ref,
    vectors_ref,
    attended_ref,
    middle_ref,
    low_ref,
    acc_ref,
    grad_acc_ref,
    square_ref,
):
    step = pl.program_id(0)
    sources, rows, width = mixed_ref.shape
    count, model = x_ref.shape
    half = model // 2
    groups = count // rows
    triples = sources // groups
    own = pl.ds(pl.multiple_of(at_ref[0] * half, half), half)
    rest = pl.ds(pl.multiple_of((1 - at_ref[0]) * half, half), half)

    @pl.when(step == 0)
    def _():
        for group in range(groups):
            attended_ref[group * rows : (group + 1) * rows, :] = jnp.concatenate(
                [mixed_ref[triple * groups + group] for triple in range(triples)], axis=1
            )
        middle = x_ref[...].astype(F32) + dot_plain(attended_ref[...], out_w_ref[...])
        middle = middle + out_b_ref[...]
        middle_ref[...] = middle
        low_ref[...] = norm_forward(middle, gain_ref[...], bias_ref[...])[0].astype(BF16)
        acc_ref[...] = jnp.zeros_like(acc_ref)
        grad_acc_ref[...] = jnp.zeros_like(grad_acc_ref)

    @pl.when(step < pl.num_programs(0) - 1)
    def _():
        hidden_pre = dot_plain(low_ref[...], in_w_ref[...]) + in_b_ref[...]
        grad_hidden = dot_transposed(ups_ref[...], back_w_ref[...])
        below = 0.5 * (1.0 + lax.erf(hidden_pre * 0.5**0.5))
        hidden = (hidden_pre * below).astype(BF16)
        density = jnp.exp(-0.5 * hidden_pre * hidden_pre) * 0.3989422804014327
        grad_pre_wide = grad_hidden * (below + hidden_pre * density)
        grad_pre = grad_pre_wide.astype(BF16)
        din_b_ref[0] = jnp.sum(grad_pre.astype(F32), axis=0, keepdims=True)
        share = dot_plain(hidden, back_w_ref[...])
        grad_share = dot_transposed(grad_pre, in_w_ref[...])
        dback = dot_inner(hidden, ups_ref[...]).astype(BF16)

        @pl.when(step < (pl.num_programs(0) - 1) // 2)
        def _():
            dback_keep_ref[0] = dback

        @pl.when(step >= (pl.num_programs(0) - 1) // 2)
        def _():
            dback_send_ref[0] = dback

        square_ref[...] = dot_inner(low_ref[...], grad_pre).astype(BF16)
        din_keep_ref[0] = square_ref[own, :]
        din_send_ref[0] = square_ref[rest, :]

        acc_ref[...] += share
        grad_acc_ref[...] += grad_share

    @pl.when(step == pl.num_programs(0) - 1)
    def _():
        middle = middle_ref[...]
        out_ref[...] = (middle + acc_ref[...] + back_b_ref[...]).astype(BF16)
        upstream = ups_ref[...].astype(F32)
        unused, normed, scaled = norm_forward(middle, 1.0, 0.0)
        change, dgain, dbias = norm_backward(grad_acc_ref[...], normed, scaled, gain_ref[...])
        dmid = upstream + change
        dmid_ref[...] = dmid
        branch = dmid.astype(BF16)
        square_ref[...] = dot_inner(attended_ref[...], branch).astype(BF16)
        din_keep_ref[0] = square_ref[own, :]
        din_send_ref[0] = square_ref[rest, :]
        vectors_ref[0:1, :] = jnp.sum(branch.astype(F32), axis=0, keepdims=True)
        vectors_ref[1:2, :] = dgain
        vectors_ref[2:3, :] = dbias
        vectors_ref[3:4, :] = jnp.sum(upstream, axis=0, keepdims=True)
        dattended = dot_transposed(branch, out_w_ref[...]).astype(BF16)
        for group in range(groups):
            for triple in range(triples):
                dmixed_ref[triple * groups + group] = dattended[
                    group * rows : (group + 1) * rows, triple * width : (triple + 1) * width
                ]


def feed(at, rows_in, ups, mixed, out_w, out_b, gain, bias, back_b, in_w, in_b, back_w):
    count, model = rows_in.shape
    hidden = in_w.shape[1]
    blocks = hidden // model
    half = model // 2
    whole = lambda i, *unused: (0, 0)
    whole_three = lambda i, *unused: (0, 0, 0)

    def step_at(i):
        return jnp.minimum(i, blocks - 1)

    def block_at(i, at_ref):
        return (step_at(i) + at_ref[0] * (blocks // 2)) % blocks

    def grad_at(i, at_ref):
        return jnp.where(i < blocks, block_at(i, at_ref), blocks)

    full = pl.BlockSpec((count, model), whole)
    vector = pl.BlockSpec((1, model), whole)
    return pl.pallas_call(
        feed_kernel,
        grid_spec=pltpu.PrefetchScalarGridSpec(
            num_scalar_prefetch=1,
            grid=(blocks + 1,),
            in_specs=[
                full,
                full,
                pl.BlockSpec(mixed.shape, whole_three),
                pl.BlockSpec((model, model), whole),
                vector,
                vector,
                vector,
                vector,
                pl.BlockSpec((model, model), lambda i, at_ref: (0, block_at(i, at_ref))),
                pl.BlockSpec((1, model), lambda i, at_ref: (0, block_at(i, at_ref))),
                pl.BlockSpec((model, model), lambda i, at_ref: (block_at(i, at_ref), 0)),
            ],
            out_specs=[
                full,
                full,
                pl.BlockSpec(mixed.shape, whole_three),
                pl.BlockSpec((1, half, model), lambda i, at_ref: (grad_at(i, at_ref), 0, 0)),
                pl.BlockSpec((1, half, model), lambda i, at_ref: (grad_at(i, at_ref), 0, 0)),
                pl.BlockSpec(
                    (1, model, model),
                    lambda i, *unused: (jnp.minimum(i, blocks // 2 - 1), 0, 0),
                ),
                pl.BlockSpec(
                    (1, model, model),
                    lambda i, *unused: (jnp.maximum(step_at(i) - blocks // 2, 0), 0, 0),
                ),
                pl.BlockSpec((1, 1, model), lambda i, at_ref: (block_at(i, at_ref), 0, 0)),
                pl.BlockSpec((4, model), whole),
            ],
            scratch_shapes=[
                pltpu.VMEM((count, model), BF16),
                pltpu.VMEM((count, model), F32),
                pltpu.VMEM((count, model), BF16),
                pltpu.VMEM((count, model), F32),
                pltpu.VMEM((count, model), F32),
                pltpu.VMEM((model, model), BF16),
            ],
        ),
        out_shape=[
            jax.ShapeDtypeStruct((count, model), BF16),
            jax.ShapeDtypeStruct((count, model), F32),
            jax.ShapeDtypeStruct(mixed.shape, BF16),
            jax.ShapeDtypeStruct((blocks + 1, half, model), BF16),
            jax.ShapeDtypeStruct((blocks + 1, half, model), BF16),
            jax.ShapeDtypeStruct((blocks // 2, model, model), BF16),
            jax.ShapeDtypeStruct((blocks // 2, model, model), BF16),
            jax.ShapeDtypeStruct((blocks, 1, model), F32),
            jax.ShapeDtypeStruct((4, model), F32),
        ],
        compiler_params=PARAMS,
        name="feed",
    )(at, rows_in, ups, mixed, out_w, out_b, gain, bias, back_b, in_w, in_b, back_w)


def head_columns(block, kind, head, heads):
    at = (kind * heads + head) * HEAD
    return block[:, at : at + HEAD]


def sorted_rows(stripe, source, half, span):
    return source * stripe if half == 0 else span + (HP - 1 - source) * stripe


def load_queries(packed_ref, target_ref, heads, kind, scaled):
    stripe = packed_ref.shape[2]
    span = HP * stripe
    for source in range(HP):
        for half in range(2):
            at = sorted_rows(stripe, source, half, span)
            block = packed_ref[source, half]
            for head in range(heads):
                part = head_columns(block, kind, head, heads)
                if scaled:
                    part = part * jnp.asarray(HEAD**-0.5, BF16)
                target_ref[head, at : at + stripe, :] = part


def load_keys(rows_of, total, stripe, heads, keys_ref, values_ref, turned_ref, turned_kind):
    for block_at in range(total // stripe):
        block = rows_of(block_at)
        at = block_at * stripe
        for head in range(heads):
            keys_ref[head, at : at + stripe, :] = head_columns(block, 0, head, heads)
            values_ref[head, at : at + stripe, :] = head_columns(block, 1, head, heads)
    source_ref = keys_ref if turned_kind == 0 else values_ref
    for chunk in range(total // TILE):
        for head in range(heads):
            turned_ref[head, chunk] = source_ref[
                head, chunk * TILE : (chunk + 1) * TILE, :
            ].T


def local_rows(packed_ref):
    stripe = packed_ref.shape[2]

    def rows_of(block_at):
        if block_at < HP:
            return packed_ref[block_at, 0]
        return packed_ref[2 * HP - 1 - block_at, 1]

    return rows_of


def remote_rows(prompts_ref, halo_ref):
    parts = prompts_ref.shape[0]
    halo_blocks = halo_ref.shape[0]

    def rows_of(block_at):
        if block_at < parts * HP:
            return prompts_ref[block_at // HP, block_at % HP]
        return halo_ref[halo_blocks - 1 - (block_at - parts * HP)]

    return rows_of


def row_slice(index, size=TILE):
    if isinstance(index, int):
        return pl.ds(index * size, size)
    return pl.ds(pl.multiple_of(index * size, size), size)


def tile_iotas():
    return (
        lax.broadcasted_iota(jnp.int32, (TILE, TILE), 0),
        lax.broadcasted_iota(jnp.int32, (TILE, TILE), 1),
    )


def forward_step(query_tile, chunk, subs, mask, refs, heads):
    queries_ref, keys_ref, turned_ref, top_ref, sum_ref, acc_ref = refs
    for head in range(heads):
        query = queries_ref[head, row_slice(query_tile), :]
        scores = []
        for sub in range(subs):
            part = dot_transposed(keys_ref[head, row_slice(chunk + sub), :], query)
            if mask is not None and sub == subs - 1:
                part = jnp.where(mask, part, NEGATIVE)
            scores.append(part)
        old = top_ref[query_tile, head]
        new = old
        for part in scores:
            new = jnp.maximum(new, jnp.max(part, axis=0, keepdims=True))
        alpha = jnp.exp(old - new)
        total = sum_ref[query_tile, head] * alpha
        acc = acc_ref[query_tile, head] * alpha
        for sub, part in enumerate(scores):
            soft = jnp.exp(part - new)
            total = total + jnp.sum(soft, axis=0, keepdims=True)
            acc = acc + dot_plain(turned_ref[head, chunk + sub], soft.astype(BF16))
        top_ref[query_tile, head] = new
        sum_ref[query_tile, head] = total
        acc_ref[query_tile, head] = acc


def loop(first, last, step):
    def run(index, unused):
        step(index)
        return unused

    lax.fori_loop(first, last, run, 0)


def walk_local(tiles, scalars_ref, starts_ref, step):
    wide = 4 if tiles % 4 == 0 else 1

    def prompt_tile(tile):
        down, across = tile_iotas()
        step(tile, 0, tile + 1, down <= across)

    def cont_tile(tile):
        query_tile = tiles + tile
        loop(0, tiles // wide, lambda chunk: step(query_tile, chunk * wide, wide, None))

        def band(chunk):
            down, across = tile_iotas()
            shifted = down + (chunk - tile) * TILE
            begin = starts_ref[tile] - tile * TILE
            mask = (shifted <= across) & (shifted >= begin)
            step(query_tile, tiles + chunk, 1, mask)

        loop(scalars_ref[tile], tile + 1, band)

    for tile in range(tiles):
        prompt_tile(tile)
    loop(0, tiles, cont_tile)


def walk_remote(tiles, parts, halo_tiles, scalars_ref, starts_ref, step, done):
    wide = 4 if tiles % 4 == 0 else 1

    def whole(query_tile, part):
        loop(
            0,
            tiles // wide,
            lambda chunk: step(query_tile, part * tiles + chunk * wide, wide, None),
        )

    def prompt_tile(tile):
        for part in range(parts):

            @pl.when(scalars_ref[2 * tiles + part] > 0)
            def _():
                whole(tile, part)

        done(tile, False)

    def cont_tile(tile):
        query_tile = tiles + tile
        for part in range(parts):
            whole(query_tile, part)

        def band(chunk):
            down, unused = tile_iotas()
            shifted = down + (chunk - halo_tiles) * TILE
            step(query_tile, parts * tiles + chunk, 1, shifted >= starts_ref[tile])

        loop(scalars_ref[tiles + tile], halo_tiles, band)
        done(query_tile, True)

    loop(0, tiles, prompt_tile)
    loop(0, tiles, cont_tile)


def forward_local_kernel(
    scalars_ref,
    starts_ref,
    packed_ref,
    top_ref,
    sum_ref,
    acc_ref,
    queries_ref,
    keys_ref,
    values_ref,
    turned_ref,
):
    heads = queries_ref.shape[0]
    stripe = packed_ref.shape[2]
    span = HP * stripe
    load_queries(packed_ref, queries_ref, heads, 2, True)
    load_keys(
        local_rows(packed_ref), 2 * span, stripe, heads, keys_ref, values_ref, turned_ref, 1
    )
    top_ref[...] = jnp.full(top_ref.shape, NEGATIVE, F32)
    sum_ref[...] = jnp.zeros(sum_ref.shape, F32)
    acc_ref[...] = jnp.zeros(acc_ref.shape, F32)
    refs = (queries_ref, keys_ref, turned_ref, top_ref, sum_ref, acc_ref)
    walk_local(
        span // TILE,
        scalars_ref,
        starts_ref,
        lambda tile, chunk, subs, mask: forward_step(tile, chunk, subs, mask, refs, heads),
    )


def store_rows(out_ref, block, query_tile, continued, columns):
    stripe = out_ref.shape[2]
    per = TILE // stripe
    tiles = HP // per
    for piece in range(per):
        rows = block[piece * stripe : (piece + 1) * stripe, :]
        if continued:
            source = HP - 1 - ((query_tile - tiles) * per + piece)
            out_ref[source, 1, :, columns] = rows
        else:
            out_ref[query_tile * per + piece, 0, :, columns] = rows


def forward_remote_kernel(
    scalars_ref,
    starts_ref,
    packed_ref,
    prompts_ref,
    halo_ref,
    top_in_ref,
    sum_in_ref,
    acc_in_ref,
    out_ref,
    log_ref,
    mixed_ref,
    queries_ref,
    keys_ref,
    values_ref,
    turned_ref,
    top_ref,
    sum_ref,
    acc_ref,
):
    heads = queries_ref.shape[0]
    stripe = packed_ref.shape[2]
    span = HP * stripe
    parts = prompts_ref.shape[0]
    halo = halo_ref.shape[0] * stripe
    load_queries(packed_ref, queries_ref, heads, 2, True)
    load_keys(
        remote_rows(prompts_ref, halo_ref),
        parts * span + halo,
        stripe,
        heads,
        keys_ref,
        values_ref,
        turned_ref,
        1,
    )
    top_ref[...] = top_in_ref[...]
    sum_ref[...] = sum_in_ref[...]
    acc_ref[...] = acc_in_ref[...]
    refs = (queries_ref, keys_ref, turned_ref, top_ref, sum_ref, acc_ref)

    def done(query_tile, continued):
        mixed = []
        for head in range(heads):
            total = sum_ref[query_tile, head]
            part = acc_ref[query_tile, head] / total
            log_ref[query_tile, head] = top_ref[query_tile, head] + jnp.log(total)
            mixed_ref[query_tile, head] = part
            mixed.append(part)
        block = jnp.concatenate(mixed, axis=0).T.astype(BF16)
        store_rows(out_ref, block, query_tile, continued, slice(None))

    walk_remote(
        span // TILE,
        parts,
        halo // TILE,
        scalars_ref,
        starts_ref,
        lambda tile, chunk, subs, mask: forward_step(tile, chunk, subs, mask, refs, heads),
        done,
    )


def forward_local(scalars, starts, packed, heads):
    stripe = packed.shape[2]
    span = HP * stripe
    tiles = 2 * span // TILE
    return pl.pallas_call(
        forward_local_kernel,
        in_specs=[SMEM_SPEC] + vmem_specs(2),
        out_specs=vmem_specs(3),
        out_shape=[
            jax.ShapeDtypeStruct((tiles, heads, 1, TILE), F32),
            jax.ShapeDtypeStruct((tiles, heads, 1, TILE), F32),
            jax.ShapeDtypeStruct((tiles, heads, HEAD, TILE), F32),
        ],
        scratch_shapes=[
            pltpu.VMEM((heads, 2 * span, HEAD), BF16),
            pltpu.VMEM((heads, 2 * span, HEAD), BF16),
            pltpu.VMEM((heads, 2 * span, HEAD), BF16),
            pltpu.VMEM((heads, tiles, HEAD, TILE), BF16),
        ],
        compiler_params=PARAMS,
        name="forward_local",
    )(scalars, starts, packed)


def forward_remote(scalars, starts, packed, prompts, halo, state, heads):
    stripe = packed.shape[2]
    span = HP * stripe
    tiles = 2 * span // TILE
    rows = prompts.shape[0] * span + halo.shape[0] * stripe
    return pl.pallas_call(
        forward_remote_kernel,
        in_specs=[SMEM_SPEC] + vmem_specs(7),
        out_specs=vmem_specs(3),
        out_shape=[
            jax.ShapeDtypeStruct((HP, 2, stripe, heads * HEAD), BF16),
            jax.ShapeDtypeStruct((tiles, heads, 1, TILE), F32),
            jax.ShapeDtypeStruct((tiles, heads, HEAD, TILE), F32),
        ],
        scratch_shapes=[
            pltpu.VMEM((heads, 2 * span, HEAD), BF16),
            pltpu.VMEM((heads, rows, HEAD), BF16),
            pltpu.VMEM((heads, rows, HEAD), BF16),
            pltpu.VMEM((heads, rows // TILE, HEAD, TILE), BF16),
            pltpu.VMEM((tiles, heads, 1, TILE), F32),
            pltpu.VMEM((tiles, heads, 1, TILE), F32),
            pltpu.VMEM((tiles, heads, HEAD, TILE), F32),
        ],
        compiler_params=PARAMS,
        name="forward_remote",
    )(scalars, starts, packed, prompts, halo, *state)


def backward_step(query_tile, chunk, subs, mask, refs, heads):
    (
        queries_ref,
        ups_ref,
        keys_ref,
        values_ref,
        turned_ref,
        log_ref,
        delta_ref,
        dquery_ref,
        dkeys_ref,
        dvalues_ref,
    ) = refs
    for head in range(heads):
        query = queries_ref[head, row_slice(query_tile), :]
        ups = ups_ref[head, row_slice(query_tile), :]
        logsum = log_ref[query_tile, head]
        delta = delta_ref[query_tile, head]
        dquery = dquery_ref[query_tile, head]
        for sub in range(subs):
            rows = row_slice(chunk + sub)
            scores = dot_transposed(keys_ref[head, rows, :], query)
            grad_soft = dot_transposed(values_ref[head, rows, :], ups)
            soft = jnp.exp(scores - logsum)
            if mask is not None and sub == subs - 1:
                soft = jnp.where(mask, soft, 0.0)
            grad_scores = (soft * (grad_soft - delta)).astype(BF16)
            dvalues_ref[head, rows, :] += dot_plain(soft.astype(BF16), ups)
            dkeys_ref[head, rows, :] += dot_plain(grad_scores, query)
            dquery = dquery + dot_plain(turned_ref[head, chunk + sub], grad_scores)
        dquery_ref[query_tile, head] = dquery


def key_grad_rows(dkeys_ref, dvalues_ref, at, stripe, heads):
    pieces = [dkeys_ref[head, at : at + stripe, :] for head in range(heads)]
    pieces = pieces + [dvalues_ref[head, at : at + stripe, :] for head in range(heads)]
    return jnp.concatenate(pieces, axis=1).astype(BF16)


def backward_remote_kernel(
    scalars_ref,
    starts_ref,
    packed_ref,
    ups_in_ref,
    prompts_ref,
    halo_ref,
    log_ref,
    mixed_ref,
    dprompts_ref,
    dhalo_ref,
    dquery_ref,
    delta_ref,
    queries_ref,
    ups_ref,
    keys_ref,
    values_ref,
    turned_ref,
    dkeys_ref,
    dvalues_ref,
):
    heads = queries_ref.shape[0]
    stripe = packed_ref.shape[2]
    span = HP * stripe
    parts = prompts_ref.shape[0]
    halo_blocks = halo_ref.shape[0]
    halo = halo_blocks * stripe
    load_queries(packed_ref, queries_ref, heads, 2, True)
    load_queries(ups_in_ref, ups_ref, heads, 0, False)
    load_keys(
        remote_rows(prompts_ref, halo_ref),
        parts * span + halo,
        stripe,
        heads,
        keys_ref,
        values_ref,
        turned_ref,
        0,
    )
    for query_tile in range(2 * span // TILE):
        for head in range(heads):
            ups = ups_ref[head, query_tile * TILE : (query_tile + 1) * TILE, :]
            delta_ref[query_tile, head] = jnp.sum(
                ups.T.astype(F32) * mixed_ref[query_tile, head], axis=0, keepdims=True
            )
    dquery_ref[...] = jnp.zeros(dquery_ref.shape, F32)
    dkeys_ref[...] = jnp.zeros(dkeys_ref.shape, F32)
    dvalues_ref[...] = jnp.zeros(dvalues_ref.shape, F32)
    refs = (
        queries_ref,
        ups_ref,
        keys_ref,
        values_ref,
        turned_ref,
        log_ref,
        delta_ref,
        dquery_ref,
        dkeys_ref,
        dvalues_ref,
    )
    walk_remote(
        span // TILE,
        parts,
        halo // TILE,
        scalars_ref,
        starts_ref,
        lambda tile, chunk, subs, mask: backward_step(tile, chunk, subs, mask, refs, heads),
        lambda tile, continued: None,
    )
    for block_at in range(parts * HP):
        dprompts_ref[block_at // HP, block_at % HP] = key_grad_rows(
            dkeys_ref, dvalues_ref, block_at * stripe, stripe, heads
        )
    for block_at in range(halo_blocks):
        dhalo_ref[halo_blocks - 1 - block_at] = key_grad_rows(
            dkeys_ref, dvalues_ref, parts * span + block_at * stripe, stripe, heads
        )


def backward_local_kernel(
    scalars_ref,
    starts_ref,
    packed_ref,
    ups_in_ref,
    log_ref,
    delta_ref,
    dquery_in_ref,
    out_ref,
    queries_ref,
    ups_ref,
    keys_ref,
    values_ref,
    turned_ref,
    dquery_ref,
    dkeys_ref,
    dvalues_ref,
):
    heads = queries_ref.shape[0]
    stripe = packed_ref.shape[2]
    span = HP * stripe
    width = heads * HEAD
    load_queries(packed_ref, queries_ref, heads, 2, True)
    load_queries(ups_in_ref, ups_ref, heads, 0, False)
    load_keys(
        local_rows(packed_ref), 2 * span, stripe, heads, keys_ref, values_ref, turned_ref, 0
    )
    dquery_ref[...] = dquery_in_ref[...]
    dkeys_ref[...] = jnp.zeros(dkeys_ref.shape, F32)
    dvalues_ref[...] = jnp.zeros(dvalues_ref.shape, F32)
    refs = (
        queries_ref,
        ups_ref,
        keys_ref,
        values_ref,
        turned_ref,
        log_ref,
        delta_ref,
        dquery_ref,
        dkeys_ref,
        dvalues_ref,
    )
    walk_local(
        span // TILE,
        scalars_ref,
        starts_ref,
        lambda tile, chunk, subs, mask: backward_step(tile, chunk, subs, mask, refs, heads),
    )
    for source in range(HP):
        for half in range(2):
            at = sorted_rows(stripe, source, half, span)
            out_ref[source, half, :, : 2 * width] = key_grad_rows(
                dkeys_ref, dvalues_ref, at, stripe, heads
            )
    pad = out_ref.shape[3] - 3 * width
    for query_tile in range(2 * span // TILE):
        turned = jnp.concatenate([dquery_ref[query_tile, head] for head in range(heads)], axis=0)
        block = (turned * HEAD**-0.5).T
        if pad:
            block = jnp.concatenate([block, jnp.zeros((TILE, pad), F32)], axis=1)
        store_rows(
            out_ref,
            block.astype(BF16),
            query_tile,
            query_tile >= span // TILE,
            slice(2 * width, None),
        )


def backward_remote(scalars, starts, packed, ups, prompts, halo, logsum, mixed, heads):
    stripe = packed.shape[2]
    span = HP * stripe
    tiles = 2 * span // TILE
    rows = prompts.shape[0] * span + halo.shape[0] * stripe
    return pl.pallas_call(
        backward_remote_kernel,
        in_specs=[SMEM_SPEC] + vmem_specs(7),
        out_specs=vmem_specs(4),
        out_shape=[
            jax.ShapeDtypeStruct(prompts.shape, BF16),
            jax.ShapeDtypeStruct(halo.shape, BF16),
            jax.ShapeDtypeStruct((tiles, heads, HEAD, TILE), F32),
            jax.ShapeDtypeStruct((tiles, heads, 1, TILE), F32),
        ],
        scratch_shapes=[
            pltpu.VMEM((heads, 2 * span, HEAD), BF16),
            pltpu.VMEM((heads, 2 * span, HEAD), BF16),
            pltpu.VMEM((heads, rows, HEAD), BF16),
            pltpu.VMEM((heads, rows, HEAD), BF16),
            pltpu.VMEM((heads, rows // TILE, HEAD, TILE), BF16),
            pltpu.VMEM((heads, rows, HEAD), F32),
            pltpu.VMEM((heads, rows, HEAD), F32),
        ],
        compiler_params=PARAMS,
        name="backward_remote",
    )(scalars, starts, packed, ups, prompts, halo, logsum, mixed)


def backward_local(scalars, starts, packed, ups, logsum, delta, dquery, heads):
    stripe = packed.shape[2]
    span = HP * stripe
    tiles = 2 * span // TILE
    rows = 2 * span
    return pl.pallas_call(
        backward_local_kernel,
        in_specs=[SMEM_SPEC] + vmem_specs(6),
        out_specs=vmem_specs(1)[0],
        out_shape=jax.ShapeDtypeStruct(packed.shape, BF16),
        scratch_shapes=[
            pltpu.VMEM((heads, rows, HEAD), BF16),
            pltpu.VMEM((heads, rows, HEAD), BF16),
            pltpu.VMEM((heads, rows, HEAD), BF16),
            pltpu.VMEM((heads, rows, HEAD), BF16),
            pltpu.VMEM((heads, tiles, HEAD, TILE), BF16),
            pltpu.VMEM((tiles, heads, HEAD, TILE), F32),
            pltpu.VMEM((heads, rows, HEAD), F32),
            pltpu.VMEM((heads, rows, HEAD), F32),
        ],
        compiler_params=PARAMS,
        name="backward_local",
    )(scalars, starts, packed, ups, logsum, delta, dquery)


def gather_pair(shard):
    if lax.axis_size("wsh") == 2:
        other = lax.ppermute(shard, "wsh", [(0, 1), (1, 0)])
        return (shard, other)
    whole = lax.all_gather(shard, "wsh", axis=0, tiled=True)
    return tuple(jnp.split(whole, 2, axis=0))


def scatter_rows(keep, send, axis):
    if lax.axis_size("wsh") == 2:
        got = lax.ppermute(send, "wsh", [(0, 1), (1, 0)])
        return (keep.astype(F32) + got.astype(F32)).astype(BF16)
    whole = jnp.concatenate([keep, send], axis=axis)
    return lax.psum_scatter(whole, "wsh", scatter_dimension=axis, tiled=True)


def traded(value, bit):
    ways = lax.axis_size("ctx")
    return lax.ppermute(value, "ctx", [(i, i ^ (1 << bit)) for i in range(ways)])


def scatter_step(parts, orders, step):
    index = lax.axis_index("ctx")
    done = []
    for part, order in zip(parts, orders):
        flag = (index >> order[step]) & 1
        count = part.shape[0] // 2
        keep = lax.dynamic_slice_in_dim(part, flag * count, count, 0)
        send = lax.dynamic_slice_in_dim(part, (1 - flag) * count, count, 0)
        got = traded(send, order[step])
        done.append((keep.astype(F32) + got.astype(F32)).astype(BF16))
    return done


def gather_step(parts, orders, step):
    index = lax.axis_index("ctx")
    done = []
    for part, order in zip(parts, orders):
        flag = (index >> order[step]) & 1
        got = traded(part, order[step])
        first = jnp.where(flag == 0, part, got)
        second = jnp.where(flag == 0, got, part)
        done.append(jnp.concatenate([first, second], axis=0))
    return done


def body(
    tokens,
    cont_lengths,
    grad_out,
    ln_gain_one,
    ln_bias_one,
    w_query,
    b_query,
    w_key,
    w_value,
    b_value,
    w_out,
    b_out,
    ln_gain_two,
    ln_bias_two,
    w_in,
    b_in,
    w_back,
    b_back,
):
    groups, rows, model = tokens.shape
    ways = lax.axis_size("ctx")
    shards = lax.axis_size("wsh")
    wsh_at = lax.axis_index("wsh")
    parts = ways // HP
    stripe = rows // 2
    span = HP * stripe
    tiles = span // TILE
    heads = HEADS * groups // HP
    triples = HEADS // heads
    width = heads * HEAD
    packed_width = -(-3 * width // 128) * 128
    pad = packed_width - 3 * width
    count = groups * rows
    hidden_size = w_in.shape[1]
    blocks = hidden_size // model
    shard_rows = model // shards
    my_ctx = lax.axis_index("ctx")
    part_at = my_ctx // HP
    group_at = (my_ctx % HP) % groups
    triple_at = (my_ctx % HP) // groups
    half_at = wsh_at if shards == 2 else jnp.zeros((), jnp.int32)
    at_vector = half_at.astype(jnp.int32).reshape(1)

    small_rows = [ln_gain_one, ln_bias_one, b_query, b_value, b_out, ln_gain_two, ln_bias_two]
    small_rows = small_rows + [b_back, b_in]
    small = jnp.concatenate([row.reshape(-1, shard_rows) for row in small_rows], axis=0)
    if shards == 2:
        got = lax.ppermute(small, "wsh", [(0, 1), (1, 0)])
        small = jnp.where(wsh_at == 0, jnp.stack([small, got]), jnp.stack([got, small]))
    else:
        small = lax.all_gather(small, "wsh", axis=0, tiled=False)
    vectors = [small[:, at].reshape(1, model).astype(F32) for at in range(8)]
    gain_one, bias_one, query_b, value_b, out_b, gain_two, bias_two, back_b = vectors
    in_b = small[:, 8:].reshape(1, hidden_size).astype(F32)
    out_w = lax.all_gather(w_out, "wsh", axis=0, tiled=True)
    in_w = lax.all_gather(w_in, "wsh", axis=0, tiled=True)
    back_w = lax.all_gather(w_back, "wsh", axis=0, tiled=True)

    token_rows = tokens.reshape(count, model)
    inputs = token_rows.astype(F32)
    cube = [[part * HP + at for at in range(HP)] for part in range(parts)]

    def exchange(value):
        return lax.all_to_all(value, "ctx", 0, 0, axis_index_groups=cube)

    low_one = norm_forward(inputs, gain_one, bias_one)[0].astype(BF16)
    low_one = low_one.reshape(1, groups, rows, model)
    low_one = jnp.broadcast_to(low_one, (HP // groups, groups, rows, model))
    low_all = exchange(low_one.reshape(HP, rows, model))

    def own_columns(value):
        return lax.dynamic_slice_in_dim(value, triple_at * width, width, 1)

    stacked = [own_columns(w_key), own_columns(w_value), own_columns(w_query)]
    stacked_b = [jnp.zeros((1, width), F32), own_columns(value_b), own_columns(query_b)]
    if pad:
        stacked.append(jnp.zeros((shard_rows, pad), BF16))
        stacked_b.append(jnp.zeros((1, pad), F32))
    first_w, second_w = gather_pair(jnp.concatenate(stacked, axis=1))
    packed = project(at_vector, low_all, first_w, second_w, jnp.concatenate(stacked_b, axis=1))
    packed = packed.reshape(HP, 2, stripe, packed_width)

    lengths = lax.dynamic_index_in_dim(cont_lengths, group_at, 0, keepdims=False)
    seg_ends = jnp.cumsum(lengths, dtype=jnp.int32)
    chunk_start = (parts - 1 - part_at) * span
    places = chunk_start + jnp.arange(span, dtype=jnp.int32)
    begins = jnp.max(
        jnp.where(seg_ends[None, :] <= places[:, None], seg_ends[None, :], 0), axis=1
    )
    starts = (begins - chunk_start).reshape(tiles, 1, TILE)
    halo_rows = min(MOSTLEN, span)
    halo_tiles = halo_rows // TILE
    halo_blocks = halo_rows // stripe
    first_start = starts[:, 0, 0]
    local_first = jnp.maximum(first_start, 0) // TILE
    has_halo = part_at < parts - 1
    halo_first = jnp.where(
        has_halo, jnp.clip(first_start + halo_rows, 0, halo_rows) // TILE, halo_tiles
    )
    seen = [(part_at >= shift).astype(jnp.int32).reshape(1) for shift in range(1, parts)]
    scalars = jnp.concatenate([local_first, halo_first] + seen).astype(jnp.int32)

    def shifted(value, shift):
        pairs = [
            (part * HP + at, ((part + shift) % parts) * HP + at)
            for part in range(parts)
            for at in range(HP)
        ]
        return lax.ppermute(value, "ctx", pairs)

    def to_former(value):
        pairs = [(i, i - HP) for i in range(HP, ways)]
        return lax.ppermute(value, "ctx", pairs)

    def to_latter(value):
        pairs = [(i, i + HP) for i in range(ways - HP)]
        return lax.ppermute(value, "ctx", pairs)

    own_prompts = packed[:, 0, :, : 2 * width]
    prompts = jnp.stack([shifted(own_prompts, shift) for shift in range(1, parts)])
    halo = to_former(packed[:halo_blocks, 1, :, : 2 * width])
    state = forward_local(scalars, starts, packed, heads)
    mixed_rows, logsum, mixed = forward_remote(
        scalars, starts, packed, prompts, halo, state, heads
    )
    attended = exchange(mixed_rows.reshape(HP, rows, width))

    (
        out_rows,
        grad_middle,
        dattended,
        din_keep,
        din_send,
        dback_keep,
        dback_send,
        din_b,
        mid_vectors,
    ) = feed(
        at_vector,
        token_rows,
        grad_out.reshape(count, model),
        attended,
        out_w,
        out_b,
        gain_two,
        bias_two,
        back_b,
        in_w,
        in_b,
        back_w,
    )
    ups = exchange(dattended).reshape(HP, 2, stripe, width)
    back_keep = dback_keep.reshape(-1, model)
    back_send = dback_send.reshape(-1, model)
    sums = [
        scatter_rows(din_keep, din_send, 1).reshape(-1, model),
        scatter_rows(back_keep, back_send, 0),
    ]
    bits = ways.bit_length() - 1
    rest = tuple(range(2, bits))
    orders = [(0, 1) + rest, (1, 0) + rest]
    own_order = (2, 0, 1) + tuple(range(3, bits))
    *sums, ups = lax.optimization_barrier((*sums, ups))
    sums = scatter_step(sums, orders, 0)

    dprompts, dhalo, dquery, delta = backward_remote(
        scalars, starts, packed, ups, prompts, halo, logsum, mixed, heads
    )
    *sums, dprompts, dhalo, dquery = lax.optimization_barrier((*sums, dprompts, dhalo, dquery))
    sums = scatter_step(sums, orders, 1)
    returned = [shifted(dprompts[shift - 1], parts - shift) for shift in range(1, parts)]
    if parts > 2:
        returned = [sum(piece.astype(F32) for piece in returned).astype(BF16)]
    returned_halo = to_latter(dhalo)
    dpacked = backward_local(scalars, starts, packed, ups, logsum, delta, dquery, heads)
    *sums, dpacked = lax.optimization_barrier((*sums, dpacked))
    sums = scatter_step(sums, orders, 2)
    halo_count = jnp.full((1,), halo_blocks, jnp.int32)
    dlow, keep, send, columns, gain_rows, shift_rows = unproject(
        at_vector, halo_count, low_all, dpacked, returned[0], returned_halo, first_w, second_w
    )

    upstream = exchange(dlow).reshape(triples, count, model)
    for step in range(3, bits):
        sums = scatter_step(sums, orders, step)
    group_bits = groups.bit_length() - 1
    sum_bits = list(range(group_bits)) + list(range(3, bits))
    own_sum = scatter_rows(keep, send, 0)
    for bit in sum_bits:
        (own_sum,) = scatter_step([own_sum], [(bit,)], 0)
    upstream = jnp.sum(upstream.astype(F32), axis=0)
    unused, hat_one, scale_one = norm_forward(inputs, gain_one, bias_one)
    change = norm_backward(upstream, hat_one, scale_one, gain_one)[0]
    grad_rows = grad_middle + change

    grad_bias_one = shift_rows.reshape(1, model)
    grad_gain_one = (gain_rows.reshape(1, model) - bias_one * grad_bias_one) / gain_one
    place = (jnp.arange(triples) == triple_at)[:, None]
    spread = jnp.where(place, columns, 0.0)
    pieces = [mid_vectors, din_b, grad_gain_one, grad_bias_one, spread]
    flat = jnp.concatenate([piece.reshape(-1) for piece in pieces])
    length = flat.shape[0]
    flat = flat.reshape(-1, 128)
    if shards == 2:
        flat = flat + lax.ppermute(flat, "wsh", [(0, 1), (1, 0)])
    else:
        flat = lax.psum(flat, "wsh")
    for bit in range(bits):
        flat = flat + traded(flat, bit)
    own_piece = own_sum[None]
    for step in reversed(range(bits)):
        (own_piece,) = gather_step([own_piece], [own_order], step)
        sums = gather_step(sums, orders, step)
    flat = flat.reshape(-1)
    in_rows = blocks * shard_rows
    first_sum = sums[0].reshape(-1, model)
    in_done, out_done = first_sum[:in_rows], first_sum[in_rows:]
    back_done = sums[1]
    piece_rows = own_piece.shape[1]
    own_piece = own_piece.reshape((2,) * bits + (piece_rows, model))
    wanted = list(range(2, group_bits - 1, -1)) + sum_bits
    own_piece = own_piece.transpose([own_order.index(bit) for bit in wanted] + [bits, bits + 1])
    last = own_piece.reshape(triples, shard_rows, model)

    def own(vector):
        size = vector.shape[0] // shards
        return lax.dynamic_slice_in_dim(vector, wsh_at * size, size, 0)

    new_out_b, new_gain_two, new_bias_two, new_back_b = [
        own(flat[at * model : (at + 1) * model]) for at in range(4)
    ]
    at = 4 * model + hidden_size
    new_in_b = own(flat[4 * model : at])
    new_gain_one = own(flat[at : at + model])
    new_bias_one = own(flat[at + model : at + 2 * model])
    columns = flat[at + 2 * model : length].reshape(triples, packed_width)

    def unvector(kind):
        return own(columns[:, kind * width : (kind + 1) * width].reshape(model))

    def untriple(kind):
        piece = last[:, :, kind * width : (kind + 1) * width]
        return piece.transpose(1, 0, 2).reshape(shard_rows, model).astype(F32)

    new_key_w, new_value_w, new_query_w = [untriple(kind) for kind in range(3)]
    return (
        out_rows.reshape(groups, rows, model),
        grad_rows.reshape(groups, rows, model),
        new_gain_one,
        new_bias_one,
        new_query_w,
        unvector(2),
        new_key_w,
        new_value_w,
        unvector(1),
        out_done.astype(F32),
        new_out_b,
        new_gain_two,
        new_bias_two,
        in_done.reshape(blocks, shard_rows, model).transpose(1, 0, 2).reshape(shard_rows, hidden_size).astype(F32),
        new_in_b,
        back_done.astype(F32),
        new_back_b,
    )


def solution(mesh):
    placed = (
        P("wsh", "ctx", None),
        P("wsh", None),
        P("wsh", "ctx", None),
        P("wsh"),
        P("wsh"),
        P("wsh", None),
        P("wsh"),
        P("wsh", None),
        P("wsh", None),
        P("wsh"),
        P("wsh", None),
        P("wsh"),
        P("wsh"),
        P("wsh"),
        P("wsh", None),
        P("wsh"),
        P("wsh", None),
        P("wsh"),
    )
    return jax.shard_map(
        body,
        mesh=mesh,
        in_specs=placed,
        out_specs=(
            P("wsh", "ctx", None),
            P("wsh", "ctx", None),
            P("wsh"),
            P("wsh"),
            P("wsh", None),
            P("wsh"),
            P("wsh", None),
            P("wsh", None),
            P("wsh"),
            P("wsh", None),
            P("wsh"),
            P("wsh"),
            P("wsh"),
            P("wsh", None),
            P("wsh"),
            P("wsh", None),
            P("wsh"),
        ),
        check_vma=False,
    )
```

```python
import jax
import jax.numpy as jnp
from jax import lax
from jax.experimental import pallas as pl
from jax.experimental.pallas import tpu as pltpu
from jax.sharding import PartitionSpec as P

HEADS = 12
HEAD = 64
PROMPT = 2048
MOSTLEN = 512
HP = 8
TILE = 256

EPSILON = 1e-12
NEGATIVE = -1e30
F32 = jnp.float32
BF16 = jnp.bfloat16


def dot_plain(left_side, right_side):
    return jnp.dot(left_side, right_side, preferred_element_type=F32)


def dot_inner(left_side, right_side):
    return lax.dot_general(
        left_side, right_side, (((0,), (0,)), ((), ())), preferred_element_type=F32
    )


def dot_transposed(left_side, right_side):
    return lax.dot_general(
        left_side, right_side, (((1,), (1,)), ((), ())), preferred_element_type=F32
    )


def norm_forward(values, gain_vec, bias_vec):
    center = values - jnp.mean(values, axis=-1, keepdims=True)
    scaled = lax.rsqrt(jnp.mean(center * center, axis=-1, keepdims=True) + EPSILON)
    normed = center * scaled
    return (normed * gain_vec + bias_vec, normed, scaled)


def norm_backward(upstream, normed, scaled, gain_vec):
    inner_grad = upstream * gain_vec
    result = scaled * (
        inner_grad
        - jnp.mean(inner_grad, axis=-1, keepdims=True)
        - normed * jnp.mean(inner_grad * normed, axis=-1, keepdims=True)
    )
    return (
        result,
        jnp.sum(upstream * normed, axis=0, keepdims=True),
        jnp.sum(upstream, axis=0, keepdims=True),
    )


def vmem_specs(count):
    return [pl.BlockSpec(memory_space=pltpu.VMEM) for unused in range(count)]


SMEM_SPEC = pl.BlockSpec(memory_space=pltpu.SMEM)
PARAMS = pltpu.CompilerParams(vmem_limit_bytes=56 << 20)


def whole_weight(at_ref, mine_ref, other_ref, weight_ref):
    half = mine_ref.shape[0]

    @pl.when(pl.program_id(0) == 0)
    def _():
        weight_ref[pl.ds(pl.multiple_of(at_ref[0] * half, half), half), :] = mine_ref[...]
        weight_ref[pl.ds(pl.multiple_of((1 - at_ref[0]) * half, half), half), :] = other_ref[...]


def project_kernel(at_ref, low_ref, mine_ref, other_ref, add_ref, out_ref, weight_ref):
    whole_weight(at_ref, mine_ref, other_ref, weight_ref)
    step, rows, model = low_ref.shape
    low = low_ref[...].reshape(step * rows, model)
    total = dot_plain(low, weight_ref[...]) + add_ref[...]
    out_ref[...] = total.astype(BF16).reshape(step, rows, total.shape[1])


def project(at, low, mine, other, add):
    sources, rows, model = low.shape
    half, width = mine.shape
    whole = lambda i, *unused: (0, 0)
    each = lambda i, *unused: (i, 0, 0)
    return pl.pallas_call(
        project_kernel,
        grid_spec=pltpu.PrefetchScalarGridSpec(
            num_scalar_prefetch=1,
            grid=(sources // 2,),
            in_specs=[
                pl.BlockSpec((2, rows, model), each),
                pl.BlockSpec((half, width), whole),
                pl.BlockSpec((half, width), whole),
                pl.BlockSpec((1, width), whole),
            ],
            out_specs=pl.BlockSpec((2, rows, width), each),
            scratch_shapes=[pltpu.VMEM((2 * half, width), BF16)],
        ),
        out_shape=jax.ShapeDtypeStruct((sources, rows, width), BF16),
        compiler_params=PARAMS,
        name="project",
    )(at, low, mine, other, add)


def unproject_kernel(
    at_ref,
    halo_ref,
    low_ref,
    packed_ref,
    extra_ref,
    extra_halo_ref,
    mine_ref,
    other_ref,
    back_ref,
    keep_ref,
    send_ref,
    cols_ref,
    gain_ref,
    shift_ref,
    weight_ref,
    acc_ref,
):
    whole_weight(at_ref, mine_ref, other_ref, weight_ref)
    step = pl.program_id(0)
    sources, halves, stripe, width = packed_ref.shape
    part = extra_ref.shape[2]
    half, unused = mine_ref.shape
    pieces = []
    for source in range(sources):
        first = packed_ref[source, 0].astype(F32)
        second = packed_ref[source, 1].astype(F32)
        added = extra_halo_ref[source].astype(F32)
        added = jnp.where(step * sources + source < halo_ref[0], added, 0.0)
        first = jnp.concatenate([first[:, :part] + extra_ref[source].astype(F32), first[:, part:]], 1)
        second = jnp.concatenate([second[:, :part] + added, second[:, part:]], 1)
        pieces = pieces + [first, second]
    grads = jnp.concatenate(pieces, axis=0).astype(BF16)
    low = low_ref[...].reshape(grads.shape[0], low_ref.shape[2])
    back = dot_transposed(grads, weight_ref[...]).astype(BF16)
    back_ref[...] = back.reshape(back_ref.shape)
    share = dot_inner(low, grads)
    columns = jnp.sum(grads.astype(F32), axis=0, keepdims=True)

    @pl.when(step == 0)
    def _():
        acc_ref[...] = share
        cols_ref[...] = columns

    @pl.when(step > 0)
    def _():
        acc_ref[...] += share
        cols_ref[...] += columns

    @pl.when(step == pl.num_programs(0) - 1)
    def _():
        own = pl.ds(pl.multiple_of(at_ref[0] * half, half), half)
        rest = pl.ds(pl.multiple_of((1 - at_ref[0]) * half, half), half)
        weight = weight_ref[...].astype(F32)
        gain_ref[...] = jnp.sum(acc_ref[...] * weight, axis=1, keepdims=True)
        shift_ref[...] = jnp.sum(cols_ref[...] * weight, axis=1, keepdims=True)
        for ref, at in ((keep_ref, own), (send_ref, rest)):
            ref[:, :width] = acc_ref[at, :].astype(BF16)
            ref[:, width:] = jnp.zeros((half, ref.shape[1] - width), BF16)


def unproject(at, halo_count, low, packed, extra, extra_halo, mine, other):
    sources, rows, model = low.shape
    stripe = packed.shape[2]
    half, width = mine.shape
    part = extra.shape[2]
    halo_steps = extra_halo.shape[0] // 2
    whole = lambda i, *unused: (0, 0)
    each = lambda i, *unused: (i, 0, 0)
    return pl.pallas_call(
        unproject_kernel,
        grid_spec=pltpu.PrefetchScalarGridSpec(
            num_scalar_prefetch=2,
            grid=(sources // 2,),
            in_specs=[
                pl.BlockSpec((2, rows, model), each),
                pl.BlockSpec((2, 2, stripe, width), lambda i, *unused: (i, 0, 0, 0)),
                pl.BlockSpec((2, stripe, part), each),
                pl.BlockSpec(
                    (2, stripe, part),
                    lambda i, *unused: (jnp.minimum(i, halo_steps - 1), 0, 0),
                ),
                pl.BlockSpec((half, width), whole),
                pl.BlockSpec((half, width), whole),
            ],
            out_specs=[
                pl.BlockSpec((2, rows, model), each),
                pl.BlockSpec((half, model), whole),
                pl.BlockSpec((half, model), whole),
                pl.BlockSpec((1, width), whole),
                pl.BlockSpec((model, 1), whole),
                pl.BlockSpec((model, 1), whole),
            ],
            scratch_shapes=[
                pltpu.VMEM((2 * half, width), BF16),
                pltpu.VMEM((2 * half, width), F32),
            ],
        ),
        out_shape=[
            jax.ShapeDtypeStruct((sources, rows, model), BF16),
            jax.ShapeDtypeStruct((half, model), BF16),
            jax.ShapeDtypeStruct((half, model), BF16),
            jax.ShapeDtypeStruct((1, width), F32),
            jax.ShapeDtypeStruct((model, 1), F32),
            jax.ShapeDtypeStruct((model, 1), F32),
        ],
        compiler_params=PARAMS,
        name="unproject",
    )(at, halo_count, low, packed, extra, extra_halo, mine, other)


def feed_kernel(
    at_ref,
    x_ref,
    ups_ref,
    mixed_ref,
    out_w_ref,
    out_b_ref,
    gain_ref,
    bias_ref,
    back_b_ref,
    in_w_ref,
    in_b_ref,
    back_w_ref,
    out_ref,
    dmid_ref,
    dmixed_ref,
    din_keep_ref,
    din_send_ref,
    dback_keep_ref,
    dback_send_ref,
    din_b_ref,
    vectors_ref,
    attended_ref,
    middle_ref,
    low_ref,
    acc_ref,
    grad_acc_ref,
    square_ref,
):
    step = pl.program_id(0)
    sources, rows, width = mixed_ref.shape
    count, model = x_ref.shape
    half = model // 2
    groups = count // rows
    triples = sources // groups
    own = pl.ds(pl.multiple_of(at_ref[0] * half, half), half)
    rest = pl.ds(pl.multiple_of((1 - at_ref[0]) * half, half), half)

    @pl.when(step == 0)
    def _():
        for group in range(groups):
            attended_ref[group * rows : (group + 1) * rows, :] = jnp.concatenate(
                [mixed_ref[triple * groups + group] for triple in range(triples)], axis=1
            )
        middle = x_ref[...].astype(F32) + dot_plain(attended_ref[...], out_w_ref[...])
        middle = middle + out_b_ref[...]
        middle_ref[...] = middle
        low_ref[...] = norm_forward(middle, gain_ref[...], bias_ref[...])[0].astype(BF16)
        acc_ref[...] = jnp.zeros_like(acc_ref)
        grad_acc_ref[...] = jnp.zeros_like(grad_acc_ref)

    @pl.when(step < pl.num_programs(0) - 1)
    def _():
        hidden_pre = dot_plain(low_ref[...], in_w_ref[...]) + in_b_ref[...]
        grad_hidden = dot_transposed(ups_ref[...], back_w_ref[...])
        below = 0.5 * (1.0 + lax.erf(hidden_pre * 0.5**0.5))
        hidden = (hidden_pre * below).astype(BF16)
        density = jnp.exp(-0.5 * hidden_pre * hidden_pre) * 0.3989422804014327
        grad_pre_wide = grad_hidden * (below + hidden_pre * density)
        grad_pre = grad_pre_wide.astype(BF16)
        din_b_ref[0] = jnp.sum(grad_pre.astype(F32), axis=0, keepdims=True)
        share = dot_plain(hidden, back_w_ref[...])
        grad_share = dot_transposed(grad_pre, in_w_ref[...])
        dback = dot_inner(hidden, ups_ref[...]).astype(BF16)

        @pl.when(step < (pl.num_programs(0) - 1) // 2)
        def _():
            dback_keep_ref[0] = dback

        @pl.when(step >= (pl.num_programs(0) - 1) // 2)
        def _():
            dback_send_ref[0] = dback

        square_ref[...] = dot_inner(low_ref[...], grad_pre).astype(BF16)
        din_keep_ref[0] = square_ref[own, :]
        din_send_ref[0] = square_ref[rest, :]

        acc_ref[...] += share
        grad_acc_ref[...] += grad_share

    @pl.when(step == pl.num_programs(0) - 1)
    def _():
        middle = middle_ref[...]
        out_ref[...] = (middle + acc_ref[...] + back_b_ref[...]).astype(BF16)
        upstream = ups_ref[...].astype(F32)
        unused, normed, scaled = norm_forward(middle, 1.0, 0.0)
        change, dgain, dbias = norm_backward(grad_acc_ref[...], normed, scaled, gain_ref[...])
        dmid = upstream + change
        dmid_ref[...] = dmid
        branch = dmid.astype(BF16)
        square_ref[...] = dot_inner(attended_ref[...], branch).astype(BF16)
        din_keep_ref[0] = square_ref[own, :]
        din_send_ref[0] = square_ref[rest, :]
        vectors_ref[0:1, :] = jnp.sum(branch.astype(F32), axis=0, keepdims=True)
        vectors_ref[1:2, :] = dgain
        vectors_ref[2:3, :] = dbias
        vectors_ref[3:4, :] = jnp.sum(upstream, axis=0, keepdims=True)
        dattended = dot_transposed(branch, out_w_ref[...]).astype(BF16)
        for group in range(groups):
            for triple in range(triples):
                dmixed_ref[triple * groups + group] = dattended[
                    group * rows : (group + 1) * rows, triple * width : (triple + 1) * width
                ]


def feed(at, rows_in, ups, mixed, out_w, out_b, gain, bias, back_b, in_w, in_b, back_w):
    count, model = rows_in.shape
    hidden = in_w.shape[1]
    blocks = hidden // model
    half = model // 2
    whole = lambda i, *unused: (0, 0)
    whole_three = lambda i, *unused: (0, 0, 0)

    def step_at(i):
        return jnp.minimum(i, blocks - 1)

    def block_at(i, at_ref):
        return (step_at(i) + at_ref[0] * (blocks // 2)) % blocks

    def grad_at(i, at_ref):
        return jnp.where(i < blocks, block_at(i, at_ref), blocks)

    full = pl.BlockSpec((count, model), whole)
    vector = pl.BlockSpec((1, model), whole)
    return pl.pallas_call(
        feed_kernel,
        grid_spec=pltpu.PrefetchScalarGridSpec(
            num_scalar_prefetch=1,
            grid=(blocks + 1,),
            in_specs=[
                full,
                full,
                pl.BlockSpec(mixed.shape, whole_three),
                pl.BlockSpec((model, model), whole),
                vector,
                vector,
                vector,
                vector,
                pl.BlockSpec((model, model), lambda i, at_ref: (0, block_at(i, at_ref))),
                pl.BlockSpec((1, model), lambda i, at_ref: (0, block_at(i, at_ref))),
                pl.BlockSpec((model, model), lambda i, at_ref: (block_at(i, at_ref), 0)),
            ],
            out_specs=[
                full,
                full,
                pl.BlockSpec(mixed.shape, whole_three),
                pl.BlockSpec((1, half, model), lambda i, at_ref: (grad_at(i, at_ref), 0, 0)),
                pl.BlockSpec((1, half, model), lambda i, at_ref: (grad_at(i, at_ref), 0, 0)),
                pl.BlockSpec(
                    (1, model, model),
                    lambda i, *unused: (jnp.minimum(i, blocks // 2 - 1), 0, 0),
                ),
                pl.BlockSpec(
                    (1, model, model),
                    lambda i, *unused: (jnp.maximum(step_at(i) - blocks // 2, 0), 0, 0),
                ),
                pl.BlockSpec((1, 1, model), lambda i, at_ref: (block_at(i, at_ref), 0, 0)),
                pl.BlockSpec((4, model), whole),
            ],
            scratch_shapes=[
                pltpu.VMEM((count, model), BF16),
                pltpu.VMEM((count, model), F32),
                pltpu.VMEM((count, model), BF16),
                pltpu.VMEM((count, model), F32),
                pltpu.VMEM((count, model), F32),
                pltpu.VMEM((model, model), BF16),
            ],
        ),
        out_shape=[
            jax.ShapeDtypeStruct((count, model), BF16),
            jax.ShapeDtypeStruct((count, model), F32),
            jax.ShapeDtypeStruct(mixed.shape, BF16),
            jax.ShapeDtypeStruct((blocks + 1, half, model), BF16),
            jax.ShapeDtypeStruct((blocks + 1, half, model), BF16),
            jax.ShapeDtypeStruct((blocks // 2, model, model), BF16),
            jax.ShapeDtypeStruct((blocks // 2, model, model), BF16),
            jax.ShapeDtypeStruct((blocks, 1, model), F32),
            jax.ShapeDtypeStruct((4, model), F32),
        ],
        compiler_params=PARAMS,
        name="feed",
    )(at, rows_in, ups, mixed, out_w, out_b, gain, bias, back_b, in_w, in_b, back_w)


def head_columns(block, kind, head, heads):
    at = (kind * heads + head) * HEAD
    return block[:, at : at + HEAD]


def sorted_rows(stripe, source, half, span):
    return source * stripe if half == 0 else span + (HP - 1 - source) * stripe


def load_queries(packed_ref, target_ref, heads, kind, scaled):
    stripe = packed_ref.shape[2]
    span = HP * stripe
    for source in range(HP):
        for half in range(2):
            at = sorted_rows(stripe, source, half, span)
            block = packed_ref[source, half]
            for head in range(heads):
                part = head_columns(block, kind, head, heads)
                if scaled:
                    part = part * jnp.asarray(HEAD**-0.5, BF16)
                target_ref[head, at : at + stripe, :] = part


def load_keys(rows_of, total, stripe, heads, keys_ref, values_ref, turned_ref, turned_kind):
    for block_at in range(total // stripe):
        block = rows_of(block_at)
        at = block_at * stripe
        for head in range(heads):
            keys_ref[head, at : at + stripe, :] = head_columns(block, 0, head, heads)
            values_ref[head, at : at + stripe, :] = head_columns(block, 1, head, heads)
    source_ref = keys_ref if turned_kind == 0 else values_ref
    for chunk in range(total // TILE):
        for head in range(heads):
            turned_ref[head, chunk] = source_ref[
                head, chunk * TILE : (chunk + 1) * TILE, :
            ].T


def local_rows(packed_ref):
    stripe = packed_ref.shape[2]

    def rows_of(block_at):
        if block_at < HP:
            return packed_ref[block_at, 0]
        return packed_ref[2 * HP - 1 - block_at, 1]

    return rows_of


def remote_rows(prompts_ref, halo_ref):
    parts = prompts_ref.shape[0]
    halo_blocks = halo_ref.shape[0]

    def rows_of(block_at):
        if block_at < parts * HP:
            return prompts_ref[block_at // HP, block_at % HP]
        return halo_ref[halo_blocks - 1 - (block_at - parts * HP)]

    return rows_of


def row_slice(index, size=TILE):
    if isinstance(index, int):
        return pl.ds(index * size, size)
    return pl.ds(pl.multiple_of(index * size, size), size)


def tile_iotas():
    return (
        lax.broadcasted_iota(jnp.int32, (TILE, TILE), 0),
        lax.broadcasted_iota(jnp.int32, (TILE, TILE), 1),
    )


def forward_step(query_tile, chunk, subs, mask, refs, heads):
    queries_ref, keys_ref, turned_ref, top_ref, sum_ref, acc_ref = refs
    for head in range(heads):
        query = queries_ref[head, row_slice(query_tile), :]
        scores = []
        for sub in range(subs):
            part = dot_transposed(keys_ref[head, row_slice(chunk + sub), :], query)
            if mask is not None and sub == subs - 1:
                part = jnp.where(mask, part, NEGATIVE)
            scores.append(part)
        old = top_ref[query_tile, head]
        new = old
        for part in scores:
            new = jnp.maximum(new, jnp.max(part, axis=0, keepdims=True))
        alpha = jnp.exp(old - new)
        total = sum_ref[query_tile, head] * alpha
        acc = acc_ref[query_tile, head] * alpha
        for sub, part in enumerate(scores):
            soft = jnp.exp(part - new)
            total = total + jnp.sum(soft, axis=0, keepdims=True)
            acc = acc + dot_plain(turned_ref[head, chunk + sub], soft.astype(BF16))
        top_ref[query_tile, head] = new
        sum_ref[query_tile, head] = total
        acc_ref[query_tile, head] = acc


def loop(first, last, step):
    def run(index, unused):
        step(index)
        return unused

    lax.fori_loop(first, last, run, 0)


def walk_local(tiles, scalars_ref, starts_ref, step):
    wide = 4 if tiles % 4 == 0 else 1

    def prompt_tile(tile):
        down, across = tile_iotas()
        step(tile, 0, tile + 1, down <= across)

    def cont_tile(tile):
        query_tile = tiles + tile
        loop(0, tiles // wide, lambda chunk: step(query_tile, chunk * wide, wide, None))

        def band(chunk):
            down, across = tile_iotas()
            shifted = down + (chunk - tile) * TILE
            begin = starts_ref[tile] - tile * TILE
            mask = (shifted <= across) & (shifted >= begin)
            step(query_tile, tiles + chunk, 1, mask)

        loop(scalars_ref[tile], tile + 1, band)

    for tile in range(tiles):
        prompt_tile(tile)
    loop(0, tiles, cont_tile)


def walk_remote(tiles, parts, halo_tiles, scalars_ref, starts_ref, step, done):
    wide = 4 if tiles % 4 == 0 else 1

    def whole(query_tile, part):
        loop(
            0,
            tiles // wide,
            lambda chunk: step(query_tile, part * tiles + chunk * wide, wide, None),
        )

    def prompt_tile(tile):
        for part in range(parts):

            @pl.when(scalars_ref[2 * tiles + part] > 0)
            def _():
                whole(tile, part)

        done(tile, False)

    def cont_tile(tile):
        query_tile = tiles + tile
        for part in range(parts):
            whole(query_tile, part)

        def band(chunk):
            down, unused = tile_iotas()
            shifted = down + (chunk - halo_tiles) * TILE
            step(query_tile, parts * tiles + chunk, 1, shifted >= starts_ref[tile])

        loop(scalars_ref[tiles + tile], halo_tiles, band)
        done(query_tile, True)

    loop(0, tiles, prompt_tile)
    loop(0, tiles, cont_tile)


def forward_local_kernel(
    scalars_ref,
    starts_ref,
    packed_ref,
    top_ref,
    sum_ref,
    acc_ref,
    queries_ref,
    keys_ref,
    values_ref,
    turned_ref,
):
    heads = queries_ref.shape[0]
    stripe = packed_ref.shape[2]
    span = HP * stripe
    load_queries(packed_ref, queries_ref, heads, 2, True)
    load_keys(
        local_rows(packed_ref), 2 * span, stripe, heads, keys_ref, values_ref, turned_ref, 1
    )
    top_ref[...] = jnp.full(top_ref.shape, NEGATIVE, F32)
    sum_ref[...] = jnp.zeros(sum_ref.shape, F32)
    acc_ref[...] = jnp.zeros(acc_ref.shape, F32)
    refs = (queries_ref, keys_ref, turned_ref, top_ref, sum_ref, acc_ref)
    walk_local(
        span // TILE,
        scalars_ref,
        starts_ref,
        lambda tile, chunk, subs, mask: forward_step(tile, chunk, subs, mask, refs, heads),
    )


def store_rows(out_ref, block, query_tile, continued, columns):
    stripe = out_ref.shape[2]
    per = TILE // stripe
    tiles = HP // per
    for piece in range(per):
        rows = block[piece * stripe : (piece + 1) * stripe, :]
        if continued:
            source = HP - 1 - ((query_tile - tiles) * per + piece)
            out_ref[source, 1, :, columns] = rows
        else:
            out_ref[query_tile * per + piece, 0, :, columns] = rows


def forward_remote_kernel(
    scalars_ref,
    starts_ref,
    packed_ref,
    prompts_ref,
    halo_ref,
    top_in_ref,
    sum_in_ref,
    acc_in_ref,
    out_ref,
    log_ref,
    mixed_ref,
    queries_ref,
    keys_ref,
    values_ref,
    turned_ref,
    top_ref,
    sum_ref,
    acc_ref,
):
    heads = queries_ref.shape[0]
    stripe = packed_ref.shape[2]
    span = HP * stripe
    parts = prompts_ref.shape[0]
    halo = halo_ref.shape[0] * stripe
    load_queries(packed_ref, queries_ref, heads, 2, True)
    load_keys(
        remote_rows(prompts_ref, halo_ref),
        parts * span + halo,
        stripe,
        heads,
        keys_ref,
        values_ref,
        turned_ref,
        1,
    )
    top_ref[...] = top_in_ref[...]
    sum_ref[...] = sum_in_ref[...]
    acc_ref[...] = acc_in_ref[...]
    refs = (queries_ref, keys_ref, turned_ref, top_ref, sum_ref, acc_ref)

    def done(query_tile, continued):
        mixed = []
        for head in range(heads):
            total = sum_ref[query_tile, head]
            part = acc_ref[query_tile, head] / total
            log_ref[query_tile, head] = top_ref[query_tile, head] + jnp.log(total)
            mixed_ref[query_tile, head] = part
            mixed.append(part)
        block = jnp.concatenate(mixed, axis=0).T.astype(BF16)
        store_rows(out_ref, block, query_tile, continued, slice(None))

    walk_remote(
        span // TILE,
        parts,
        halo // TILE,
        scalars_ref,
        starts_ref,
        lambda tile, chunk, subs, mask: forward_step(tile, chunk, subs, mask, refs, heads),
        done,
    )


def forward_local(scalars, starts, packed, heads):
    stripe = packed.shape[2]
    span = HP * stripe
    tiles = 2 * span // TILE
    return pl.pallas_call(
        forward_local_kernel,
        in_specs=[SMEM_SPEC] + vmem_specs(2),
        out_specs=vmem_specs(3),
        out_shape=[
            jax.ShapeDtypeStruct((tiles, heads, 1, TILE), F32),
            jax.ShapeDtypeStruct((tiles, heads, 1, TILE), F32),
            jax.ShapeDtypeStruct((tiles, heads, HEAD, TILE), F32),
        ],
        scratch_shapes=[
            pltpu.VMEM((heads, 2 * span, HEAD), BF16),
            pltpu.VMEM((heads, 2 * span, HEAD), BF16),
            pltpu.VMEM((heads, 2 * span, HEAD), BF16),
            pltpu.VMEM((heads, tiles, HEAD, TILE), BF16),
        ],
        compiler_params=PARAMS,
        name="forward_local",
    )(scalars, starts, packed)


def forward_remote(scalars, starts, packed, prompts, halo, state, heads):
    stripe = packed.shape[2]
    span = HP * stripe
    tiles = 2 * span // TILE
    rows = prompts.shape[0] * span + halo.shape[0] * stripe
    return pl.pallas_call(
        forward_remote_kernel,
        in_specs=[SMEM_SPEC] + vmem_specs(7),
        out_specs=vmem_specs(3),
        out_shape=[
            jax.ShapeDtypeStruct((HP, 2, stripe, heads * HEAD), BF16),
            jax.ShapeDtypeStruct((tiles, heads, 1, TILE), F32),
            jax.ShapeDtypeStruct((tiles, heads, HEAD, TILE), F32),
        ],
        scratch_shapes=[
            pltpu.VMEM((heads, 2 * span, HEAD), BF16),
            pltpu.VMEM((heads, rows, HEAD), BF16),
            pltpu.VMEM((heads, rows, HEAD), BF16),
            pltpu.VMEM((heads, rows // TILE, HEAD, TILE), BF16),
            pltpu.VMEM((tiles, heads, 1, TILE), F32),
            pltpu.VMEM((tiles, heads, 1, TILE), F32),
            pltpu.VMEM((tiles, heads, HEAD, TILE), F32),
        ],
        compiler_params=PARAMS,
        name="forward_remote",
    )(scalars, starts, packed, prompts, halo, *state)


def backward_step(query_tile, chunk, subs, mask, refs, heads):
    (
        queries_ref,
        ups_ref,
        keys_ref,
        values_ref,
        turned_ref,
        log_ref,
        delta_ref,
        dquery_ref,
        dkeys_ref,
        dvalues_ref,
    ) = refs
    for head in range(heads):
        query = queries_ref[head, row_slice(query_tile), :]
        ups = ups_ref[head, row_slice(query_tile), :]
        logsum = log_ref[query_tile, head]
        delta = delta_ref[query_tile, head]
        dquery = dquery_ref[query_tile, head]
        for sub in range(subs):
            rows = row_slice(chunk + sub)
            scores = dot_transposed(keys_ref[head, rows, :], query)
            grad_soft = dot_transposed(values_ref[head, rows, :], ups)
            soft = jnp.exp(scores - logsum)
            if mask is not None and sub == subs - 1:
                soft = jnp.where(mask, soft, 0.0)
            grad_scores = (soft * (grad_soft - delta)).astype(BF16)
            dvalues_ref[head, rows, :] += dot_plain(soft.astype(BF16), ups)
            dkeys_ref[head, rows, :] += dot_plain(grad_scores, query)
            dquery = dquery + dot_plain(turned_ref[head, chunk + sub], grad_scores)
        dquery_ref[query_tile, head] = dquery


def key_grad_rows(dkeys_ref, dvalues_ref, at, stripe, heads):
    pieces = [dkeys_ref[head, at : at + stripe, :] for head in range(heads)]
    pieces = pieces + [dvalues_ref[head, at : at + stripe, :] for head in range(heads)]
    return jnp.concatenate(pieces, axis=1).astype(BF16)


def backward_remote_kernel(
    scalars_ref,
    starts_ref,
    packed_ref,
    ups_in_ref,
    prompts_ref,
    halo_ref,
    log_ref,
    mixed_ref,
    dprompts_ref,
    dhalo_ref,
    dquery_ref,
    delta_ref,
    queries_ref,
    ups_ref,
    keys_ref,
    values_ref,
    turned_ref,
    dkeys_ref,
    dvalues_ref,
):
    heads = queries_ref.shape[0]
    stripe = packed_ref.shape[2]
    span = HP * stripe
    parts = prompts_ref.shape[0]
    halo_blocks = halo_ref.shape[0]
    halo = halo_blocks * stripe
    load_queries(packed_ref, queries_ref, heads, 2, True)
    load_queries(ups_in_ref, ups_ref, heads, 0, False)
    load_keys(
        remote_rows(prompts_ref, halo_ref),
        parts * span + halo,
        stripe,
        heads,
        keys_ref,
        values_ref,
        turned_ref,
        0,
    )
    for query_tile in range(2 * span // TILE):
        for head in range(heads):
            ups = ups_ref[head, query_tile * TILE : (query_tile + 1) * TILE, :]
            delta_ref[query_tile, head] = jnp.sum(
                ups.T.astype(F32) * mixed_ref[query_tile, head], axis=0, keepdims=True
            )
    dquery_ref[...] = jnp.zeros(dquery_ref.shape, F32)
    dkeys_ref[...] = jnp.zeros(dkeys_ref.shape, F32)
    dvalues_ref[...] = jnp.zeros(dvalues_ref.shape, F32)
    refs = (
        queries_ref,
        ups_ref,
        keys_ref,
        values_ref,
        turned_ref,
        log_ref,
        delta_ref,
        dquery_ref,
        dkeys_ref,
        dvalues_ref,
    )
    walk_remote(
        span // TILE,
        parts,
        halo // TILE,
        scalars_ref,
        starts_ref,
        lambda tile, chunk, subs, mask: backward_step(tile, chunk, subs, mask, refs, heads),
        lambda tile, continued: None,
    )
    for block_at in range(parts * HP):
        dprompts_ref[block_at // HP, block_at % HP] = key_grad_rows(
            dkeys_ref, dvalues_ref, block_at * stripe, stripe, heads
        )
    for block_at in range(halo_blocks):
        dhalo_ref[halo_blocks - 1 - block_at] = key_grad_rows(
            dkeys_ref, dvalues_ref, parts * span + block_at * stripe, stripe, heads
        )


def backward_local_kernel(
    scalars_ref,
    starts_ref,
    packed_ref,
    ups_in_ref,
    log_ref,
    delta_ref,
    dquery_in_ref,
    out_ref,
    queries_ref,
    ups_ref,
    keys_ref,
    values_ref,
    turned_ref,
    dquery_ref,
    dkeys_ref,
    dvalues_ref,
):
    heads = queries_ref.shape[0]
    stripe = packed_ref.shape[2]
    span = HP * stripe
    width = heads * HEAD
    load_queries(packed_ref, queries_ref, heads, 2, True)
    load_queries(ups_in_ref, ups_ref, heads, 0, False)
    load_keys(
        local_rows(packed_ref), 2 * span, stripe, heads, keys_ref, values_ref, turned_ref, 0
    )
    dquery_ref[...] = dquery_in_ref[...]
    dkeys_ref[...] = jnp.zeros(dkeys_ref.shape, F32)
    dvalues_ref[...] = jnp.zeros(dvalues_ref.shape, F32)
    refs = (
        queries_ref,
        ups_ref,
        keys_ref,
        values_ref,
        turned_ref,
        log_ref,
        delta_ref,
        dquery_ref,
        dkeys_ref,
        dvalues_ref,
    )
    walk_local(
        span // TILE,
        scalars_ref,
        starts_ref,
        lambda tile, chunk, subs, mask: backward_step(tile, chunk, subs, mask, refs, heads),
    )
    for source in range(HP):
        for half in range(2):
            at = sorted_rows(stripe, source, half, span)
            out_ref[source, half, :, : 2 * width] = key_grad_rows(
                dkeys_ref, dvalues_ref, at, stripe, heads
            )
    pad = out_ref.shape[3] - 3 * width
    for query_tile in range(2 * span // TILE):
        turned = jnp.concatenate([dquery_ref[query_tile, head] for head in range(heads)], axis=0)
        block = (turned * HEAD**-0.5).T
        if pad:
            block = jnp.concatenate([block, jnp.zeros((TILE, pad), F32)], axis=1)
        store_rows(
            out_ref,
            block.astype(BF16),
            query_tile,
            query_tile >= span // TILE,
            slice(2 * width, None),
        )


def backward_remote(scalars, starts, packed, ups, prompts, halo, logsum, mixed, heads):
    stripe = packed.shape[2]
    span = HP * stripe
    tiles = 2 * span // TILE
    rows = prompts.shape[0] * span + halo.shape[0] * stripe
    return pl.pallas_call(
        backward_remote_kernel,
        in_specs=[SMEM_SPEC] + vmem_specs(7),
        out_specs=vmem_specs(4),
        out_shape=[
            jax.ShapeDtypeStruct(prompts.shape, BF16),
            jax.ShapeDtypeStruct(halo.shape, BF16),
            jax.ShapeDtypeStruct((tiles, heads, HEAD, TILE), F32),
            jax.ShapeDtypeStruct((tiles, heads, 1, TILE), F32),
        ],
        scratch_shapes=[
            pltpu.VMEM((heads, 2 * span, HEAD), BF16),
            pltpu.VMEM((heads, 2 * span, HEAD), BF16),
            pltpu.VMEM((heads, rows, HEAD), BF16),
            pltpu.VMEM((heads, rows, HEAD), BF16),
            pltpu.VMEM((heads, rows // TILE, HEAD, TILE), BF16),
            pltpu.VMEM((heads, rows, HEAD), F32),
            pltpu.VMEM((heads, rows, HEAD), F32),
        ],
        compiler_params=PARAMS,
        name="backward_remote",
    )(scalars, starts, packed, ups, prompts, halo, logsum, mixed)


def backward_local(scalars, starts, packed, ups, logsum, delta, dquery, heads):
    stripe = packed.shape[2]
    span = HP * stripe
    tiles = 2 * span // TILE
    rows = 2 * span
    return pl.pallas_call(
        backward_local_kernel,
        in_specs=[SMEM_SPEC] + vmem_specs(6),
        out_specs=vmem_specs(1)[0],
        out_shape=jax.ShapeDtypeStruct(packed.shape, BF16),
        scratch_shapes=[
            pltpu.VMEM((heads, rows, HEAD), BF16),
            pltpu.VMEM((heads, rows, HEAD), BF16),
            pltpu.VMEM((heads, rows, HEAD), BF16),
            pltpu.VMEM((heads, rows, HEAD), BF16),
            pltpu.VMEM((heads, tiles, HEAD, TILE), BF16),
            pltpu.VMEM((tiles, heads, HEAD, TILE), F32),
            pltpu.VMEM((heads, rows, HEAD), F32),
            pltpu.VMEM((heads, rows, HEAD), F32),
        ],
        compiler_params=PARAMS,
        name="backward_local",
    )(scalars, starts, packed, ups, logsum, delta, dquery)


def gather_pair(shard):
    if lax.axis_size("wsh") == 2:
        other = lax.ppermute(shard, "wsh", [(0, 1), (1, 0)])
        return (shard, other)
    whole = lax.all_gather(shard, "wsh", axis=0, tiled=True)
    return tuple(jnp.split(whole, 2, axis=0))


def scatter_rows(keep, send, axis):
    if lax.axis_size("wsh") == 2:
        got = lax.ppermute(send, "wsh", [(0, 1), (1, 0)])
        return (keep.astype(F32) + got.astype(F32)).astype(BF16)
    whole = jnp.concatenate([keep, send], axis=axis)
    return lax.psum_scatter(whole, "wsh", scatter_dimension=axis, tiled=True)


def traded(value, bit):
    ways = lax.axis_size("ctx")
    return lax.ppermute(value, "ctx", [(i, i ^ (1 << bit)) for i in range(ways)])


def scatter_step(parts, orders, step):
    index = lax.axis_index("ctx")
    done = []
    for part, order in zip(parts, orders):
        flag = (index >> order[step]) & 1
        count = part.shape[0] // 2
        keep = lax.dynamic_slice_in_dim(part, flag * count, count, 0)
        send = lax.dynamic_slice_in_dim(part, (1 - flag) * count, count, 0)
        got = traded(send, order[step])
        done.append((keep.astype(F32) + got.astype(F32)).astype(BF16))
    return done


def gather_step(parts, orders, step):
    index = lax.axis_index("ctx")
    done = []
    for part, order in zip(parts, orders):
        flag = (index >> order[step]) & 1
        got = traded(part, order[step])
        first = jnp.where(flag == 0, part, got)
        second = jnp.where(flag == 0, got, part)
        done.append(jnp.concatenate([first, second], axis=0))
    return done


def body(
    tokens,
    cont_lengths,
    grad_out,
    ln_gain_one,
    ln_bias_one,
    w_query,
    b_query,
    w_key,
    w_value,
    b_value,
    w_out,
    b_out,
    ln_gain_two,
    ln_bias_two,
    w_in,
    b_in,
    w_back,
    b_back,
):
    groups, rows, model = tokens.shape
    ways = lax.axis_size("ctx")
    shards = lax.axis_size("wsh")
    wsh_at = lax.axis_index("wsh")
    parts = ways // HP
    stripe = rows // 2
    span = HP * stripe
    tiles = span // TILE
    heads = HEADS * groups // HP
    triples = HEADS // heads
    width = heads * HEAD
    packed_width = -(-3 * width // 128) * 128
    pad = packed_width - 3 * width
    count = groups * rows
    hidden_size = w_in.shape[1]
    blocks = hidden_size // model
    shard_rows = model // shards
    my_ctx = lax.axis_index("ctx")
    part_at = my_ctx // HP
    group_at = (my_ctx % HP) % groups
    triple_at = (my_ctx % HP) // groups
    half_at = wsh_at if shards == 2 else jnp.zeros((), jnp.int32)
    at_vector = half_at.astype(jnp.int32).reshape(1)

    small_rows = [ln_gain_one, ln_bias_one, b_query, b_value, b_out, ln_gain_two, ln_bias_two]
    small_rows = small_rows + [b_back, b_in]
    small = jnp.concatenate([row.reshape(-1, shard_rows) for row in small_rows], axis=0)
    if shards == 2:
        got = lax.ppermute(small, "wsh", [(0, 1), (1, 0)])
        small = jnp.where(wsh_at == 0, jnp.stack([small, got]), jnp.stack([got, small]))
    else:
        small = lax.all_gather(small, "wsh", axis=0, tiled=False)
    vectors = [small[:, at].reshape(1, model).astype(F32) for at in range(8)]
    gain_one, bias_one, query_b, value_b, out_b, gain_two, bias_two, back_b = vectors
    in_b = small[:, 8:].reshape(1, hidden_size).astype(F32)
    out_w = lax.all_gather(w_out, "wsh", axis=0, tiled=True)
    in_w = lax.all_gather(w_in, "wsh", axis=0, tiled=True)
    back_w = lax.all_gather(w_back, "wsh", axis=0, tiled=True)

    token_rows = tokens.reshape(count, model)
    inputs = token_rows.astype(F32)
    cube = [[part * HP + at for at in range(HP)] for part in range(parts)]

    def exchange(value):
        return lax.all_to_all(value, "ctx", 0, 0, axis_index_groups=cube)

    low_one = norm_forward(inputs, gain_one, bias_one)[0].astype(BF16)
    low_one = low_one.reshape(1, groups, rows, model)
    low_one = jnp.broadcast_to(low_one, (HP // groups, groups, rows, model))
    low_all = exchange(low_one.reshape(HP, rows, model))

    def own_columns(value):
        return lax.dynamic_slice_in_dim(value, triple_at * width, width, 1)

    stacked = [own_columns(w_key), own_columns(w_value), own_columns(w_query)]
    stacked_b = [jnp.zeros((1, width), F32), own_columns(value_b), own_columns(query_b)]
    if pad:
        stacked.append(jnp.zeros((shard_rows, pad), BF16))
        stacked_b.append(jnp.zeros((1, pad), F32))
    first_w, second_w = gather_pair(jnp.concatenate(stacked, axis=1))
    packed = project(at_vector, low_all, first_w, second_w, jnp.concatenate(stacked_b, axis=1))
    packed = packed.reshape(HP, 2, stripe, packed_width)

    lengths = lax.dynamic_index_in_dim(cont_lengths, group_at, 0, keepdims=False)
    seg_ends = jnp.cumsum(lengths, dtype=jnp.int32)
    chunk_start = (parts - 1 - part_at) * span
    places = chunk_start + jnp.arange(span, dtype=jnp.int32)
    begins = jnp.max(
        jnp.where(seg_ends[None, :] <= places[:, None], seg_ends[None, :], 0), axis=1
    )
    starts = (begins - chunk_start).reshape(tiles, 1, TILE)
    halo_rows = min(MOSTLEN, span)
    halo_tiles = halo_rows // TILE
    halo_blocks = halo_rows // stripe
    first_start = starts[:, 0, 0]
    local_first = jnp.maximum(first_start, 0) // TILE
    has_halo = part_at < parts - 1
    halo_first = jnp.where(
        has_halo, jnp.clip(first_start + halo_rows, 0, halo_rows) // TILE, halo_tiles
    )
    seen = [(part_at >= shift).astype(jnp.int32).reshape(1) for shift in range(1, parts)]
    scalars = jnp.concatenate([local_first, halo_first] + seen).astype(jnp.int32)

    def shifted(value, shift):
        pairs = [
            (part * HP + at, ((part + shift) % parts) * HP + at)
            for part in range(parts)
            for at in range(HP)
        ]
        return lax.ppermute(value, "ctx", pairs)

    def to_former(value):
        pairs = [(i, i - HP) for i in range(HP, ways)]
        return lax.ppermute(value, "ctx", pairs)

    def to_latter(value):
        pairs = [(i, i + HP) for i in range(ways - HP)]
        return lax.ppermute(value, "ctx", pairs)

    own_prompts = packed[:, 0, :, : 2 * width]
    prompts = jnp.stack([shifted(own_prompts, shift) for shift in range(1, parts)])
    halo = to_former(packed[:halo_blocks, 1, :, : 2 * width])
    state = forward_local(scalars, starts, packed, heads)
    mixed_rows, logsum, mixed = forward_remote(
        scalars, starts, packed, prompts, halo, state, heads
    )
    attended = exchange(mixed_rows.reshape(HP, rows, width))

    (
        out_rows,
        grad_middle,
        dattended,
        din_keep,
        din_send,
        dback_keep,
        dback_send,
        din_b,
        mid_vectors,
    ) = feed(
        at_vector,
        token_rows,
        grad_out.reshape(count, model),
        attended,
        out_w,
        out_b,
        gain_two,
        bias_two,
        back_b,
        in_w,
        in_b,
        back_w,
    )
    ups = exchange(dattended).reshape(HP, 2, stripe, width)
    back_keep = dback_keep.reshape(-1, model)
    back_send = dback_send.reshape(-1, model)
    sums = [
        scatter_rows(din_keep, din_send, 1).reshape(-1, model),
        scatter_rows(back_keep, back_send, 0),
    ]
    bits = ways.bit_length() - 1
    rest = tuple(range(2, bits))
    orders = [(0, 1) + rest, (1, 0) + rest]
    own_order = (2, 0, 1) + tuple(range(3, bits))
    *sums, ups = lax.optimization_barrier((*sums, ups))
    sums = scatter_step(sums, orders, 0)

    dprompts, dhalo, dquery, delta = backward_remote(
        scalars, starts, packed, ups, prompts, halo, logsum, mixed, heads
    )
    *sums, dprompts, dhalo, dquery = lax.optimization_barrier((*sums, dprompts, dhalo, dquery))
    sums = scatter_step(sums, orders, 1)
    returned = [shifted(dprompts[shift - 1], parts - shift) for shift in range(1, parts)]
    if parts > 2:
        returned = [sum(piece.astype(F32) for piece in returned).astype(BF16)]
    returned_halo = to_latter(dhalo)
    dpacked = backward_local(scalars, starts, packed, ups, logsum, delta, dquery, heads)
    *sums, dpacked = lax.optimization_barrier((*sums, dpacked))
    sums = scatter_step(sums, orders, 2)
    halo_count = jnp.full((1,), halo_blocks, jnp.int32)
    dlow, keep, send, columns, gain_rows, shift_rows = unproject(
        at_vector, halo_count, low_all, dpacked, returned[0], returned_halo, first_w, second_w
    )

    upstream = exchange(dlow).reshape(triples, count, model)
    for step in range(3, bits):
        sums = scatter_step(sums, orders, step)
    group_bits = groups.bit_length() - 1
    sum_bits = list(range(3, bits)) + list(range(group_bits))
    own_sum = scatter_rows(keep, send, 0)
    for bit in sum_bits:
        (own_sum,) = scatter_step([own_sum], [(bit,)], 0)
    upstream = jnp.sum(upstream.astype(F32), axis=0)
    unused, hat_one, scale_one = norm_forward(inputs, gain_one, bias_one)
    change = norm_backward(upstream, hat_one, scale_one, gain_one)[0]
    grad_rows = grad_middle + change

    grad_bias_one = shift_rows.reshape(1, model)
    grad_gain_one = (gain_rows.reshape(1, model) - bias_one * grad_bias_one) / gain_one
    place = (jnp.arange(triples) == triple_at)[:, None]
    spread = jnp.where(place, columns, 0.0)
    pieces = [mid_vectors, din_b, grad_gain_one, grad_bias_one, spread]
    flat = jnp.concatenate([piece.reshape(-1) for piece in pieces])
    length = flat.shape[0]
    flat = flat.reshape(-1, 128)
    if shards == 2:
        flat = flat + lax.ppermute(flat, "wsh", [(0, 1), (1, 0)])
    else:
        flat = lax.psum(flat, "wsh")
    for bit in range(bits):
        flat = flat + traded(flat, bit)
    own_piece = own_sum[None]
    for step in reversed(range(bits)):
        (own_piece,) = gather_step([own_piece], [own_order], step)
        sums = gather_step(sums, orders, step)
    flat = flat.reshape(-1)
    in_rows = blocks * shard_rows
    first_sum = sums[0].reshape(-1, model)
    in_done, out_done = first_sum[:in_rows], first_sum[in_rows:]
    back_done = sums[1]
    piece_rows = own_piece.shape[1]
    own_piece = own_piece.reshape((2,) * bits + (piece_rows, model))
    wanted = list(range(2, group_bits - 1, -1)) + sum_bits
    own_piece = own_piece.transpose([own_order.index(bit) for bit in wanted] + [bits, bits + 1])
    last = own_piece.reshape(triples, shard_rows, model)

    def own(vector):
        size = vector.shape[0] // shards
        return lax.dynamic_slice_in_dim(vector, wsh_at * size, size, 0)

    new_out_b, new_gain_two, new_bias_two, new_back_b = [
        own(flat[at * model : (at + 1) * model]) for at in range(4)
    ]
    at = 4 * model + hidden_size
    new_in_b = own(flat[4 * model : at])
    new_gain_one = own(flat[at : at + model])
    new_bias_one = own(flat[at + model : at + 2 * model])
    columns = flat[at + 2 * model : length].reshape(triples, packed_width)

    def unvector(kind):
        return own(columns[:, kind * width : (kind + 1) * width].reshape(model))

    def untriple(kind):
        piece = last[:, :, kind * width : (kind + 1) * width]
        return piece.transpose(1, 0, 2).reshape(shard_rows, model).astype(F32)

    new_key_w, new_value_w, new_query_w = [untriple(kind) for kind in range(3)]
    return (
        out_rows.reshape(groups, rows, model),
        grad_rows.reshape(groups, rows, model),
        new_gain_one,
        new_bias_one,
        new_query_w,
        unvector(2),
        new_key_w,
        new_value_w,
        unvector(1),
        out_done.astype(F32),
        new_out_b,
        new_gain_two,
        new_bias_two,
        in_done.reshape(blocks, shard_rows, model).transpose(1, 0, 2).reshape(shard_rows, hidden_size).astype(F32),
        new_in_b,
        back_done.astype(F32),
        new_back_b,
    )


def solution(mesh):
    placed = (
        P("wsh", "ctx", None),
        P("wsh", None),
        P("wsh", "ctx", None),
        P("wsh"),
        P("wsh"),
        P("wsh", None),
        P("wsh"),
        P("wsh", None),
        P("wsh", None),
        P("wsh"),
        P("wsh", None),
        P("wsh"),
        P("wsh"),
        P("wsh"),
        P("wsh", None),
        P("wsh"),
        P("wsh", None),
        P("wsh"),
    )
    return jax.shard_map(
        body,
        mesh=mesh,
        in_specs=placed,
        out_specs=(
            P("wsh", "ctx", None),
            P("wsh", "ctx", None),
            P("wsh"),
            P("wsh"),
            P("wsh", None),
            P("wsh"),
            P("wsh", None),
            P("wsh", None),
            P("wsh"),
            P("wsh", None),
            P("wsh"),
            P("wsh"),
            P("wsh"),
            P("wsh", None),
            P("wsh"),
            P("wsh", None),
            P("wsh"),
        ),
        check_vma=False,
    )
```
